128 devices in a mesh: row: 16 (over y, z_hi, core), col: 8 (over x, z_lo).
Axes of the slice: x: 4, y: 4, z: 4 (z_hi: 2, z_lo: 2; z = z_hi * 2 + z_lo), core: 2. Of those that a mesh axis runs over, the one named last changes fastest.
Arguments:
- prior_voltage: float32 [4, 2048, 4096], P(None, 'row', 'col'), may hold values from 0.5 to 1.5
- baseline_admittance: float32 [4, 2048, 4096], P(None, 'row', 'col'), may hold values from 0.5 to 2
- block_warmth: float32 [4, 512, 1024], P(None, 'row', 'col'), may hold values from 0 to 2
- interlayer_indicator: int32 [3, 2048, 4096], P(None, 'row', 'col'), may hold values 0 or 1
- feeder_indicator: int32 [4, 2048, 4096], P(None, 'row', 'col'), may hold values 0 or 1
- injected_amperes: float32 [4, 2048, 4096], P(None, 'row', 'col'), may hold values from 0.5 to 4
Outputs:
- revised_voltage: float32 [4, 2048, 4096], P(None, 'row', 'col')
- revised_warmth: float32 [4, 512, 1024], P(None, 'row', 'col')
The draws below stay inside these ranges and needn't reach their ends.
All inputs are finite; a program needn't handle non-finite values. No bound on the sum of `interlayer_indicator` or of `feeder_indicator` on one device may be relied on, other than what follows from the above.
Results may differ from the reference program's by a relative error of at most 0.00002.
Values sent between devices are 32-bit elements; how exact they have to be, the bound alone decides.
A program may use at most 128 MiB of HBM per device.

```python
import math
import jax
import jax.numpy as jnp
from jax import lax

LAYER_COUNT = 4
BLOCK_REFINE = 4
SWEEPS = 3
HEAT_SWEEPS = 4
NR = 2048
NC = 4096
BLOCK_HEIGHTWISE = 512
BLOCK_WIDTHWISE = 1024


def touch_ends(result, rng, smallest, high):
    extent = result.shape
    index_at = [jax.random.randint(jax.random.fold_in(rng, axis), (), 0, extent[axis]) for axis in range(len(extent))]
    result = result.at[tuple(index_at)].set(smallest)
    longest = extent.index(max(extent))
    index_at[longest] = (index_at[longest] + 1) % extent[longest]
    return result.at[tuple(index_at)].set(high)


def levels(rng, extent, cuts, low, top_value):
    def one(position, parts):
        draws = jax.random.uniform(jax.random.fold_in(jax.random.fold_in(rng, 6), position), (parts,), jnp.float32, low / len(cuts), top_value / len(cuts))
        return jnp.repeat(jnp.exp(draws), extent[position] // parts).reshape((-1,) + (1,) * (len(extent) - position - 1))

    factor_of = one(*cuts[0])
    for cut in cuts[1:]:
        factor_of = factor_of * one(*cut)
    return factor_of


def setup_inputs(seed: int = 0) -> dict:
    key_list = jax.random.split(jax.random.key(seed), 7)
    prior_voltage = jnp.clip(0.5 + 1.0 * jax.random.uniform(key_list[0], (LAYER_COUNT, NR, NC), jnp.float32) ** levels(key_list[0], (LAYER_COUNT, NR, NC), ((1, 16), (2, 8)), -0.2, 0.2), 0.5, 1.5)
    baseline_admittance = jnp.clip(jnp.exp(math.log(2.0) - 1.3862944 * jax.random.uniform(key_list[1], (LAYER_COUNT, NR, NC), jnp.float32) ** levels(key_list[1], (LAYER_COUNT, NR, NC), ((1, 16), (2, 8)), -0.2, 0.2)), 0.5, 2.0)
    block_warmth = jnp.clip(2.0 * jax.random.uniform(key_list[2], (LAYER_COUNT, BLOCK_HEIGHTWISE, BLOCK_WIDTHWISE), jnp.float32) ** levels(key_list[2], (LAYER_COUNT, BLOCK_HEIGHTWISE, BLOCK_WIDTHWISE), ((1, 16), (2, 8)), -0.2, 0.2), 0.0, 2.0)
    interlayer_indicator = touch_ends((jax.random.randint(key_list[3], (LAYER_COUNT - 1, NR, NC), 0, 2) < 1).astype(jnp.int32), jax.random.fold_in(key_list[3], 1), 0, 1)
    feeder_indicator = touch_ends((jax.random.randint(key_list[4], (LAYER_COUNT, NR, NC), 0, 4) < 1).astype(jnp.int32), jax.random.fold_in(key_list[4], 1), 0, 1)
    injected_amperes = jnp.clip(jnp.exp(math.log(4.0) - 2.0794415 * jax.random.uniform(key_list[5], (LAYER_COUNT, NR, NC), jnp.float32) ** levels(key_list[5], (LAYER_COUNT, NR, NC), ((1, 16), (2, 8)), -0.2, 0.2)), 0.5, 4.0)
    return dict(prior_voltage=prior_voltage, baseline_admittance=baseline_admittance, block_warmth=block_warmth, interlayer_indicator=interlayer_indicator, feeder_indicator=feeder_indicator, injected_amperes=injected_amperes)


warmth_sensitivity = 0.5
via_cond = 1.0
leak_cond = 0.2
spectrum_low = 0.05
spectrum_high = 1.95
warming_weight = 0.3
layer_admittance = 1.0
drain_admittance = 1.0
heat_gain = 0.0625
interval_length = 0.12

def bordered_array(voltage_grid):
    return jnp.pad(voltage_grid, ((0, 0), (1, 1), (1, 1)))

def neighbours(voltage_grid):
    return (voltage_grid[:, :-2, 1:-1], voltage_grid[:, 2:, 1:-1], voltage_grid[:, 1:-1, :-2], voltage_grid[:, 1:-1, 2:])

def planar_edges(cond_pad):
    center = cond_pad[:, 1:-1, 1:-1]
    return tuple((jnp.sqrt(center * other) for other in neighbours(cond_pad)))

def vertical(voltage_grid, vias):
    nought_value = jnp.zeros_like(voltage_grid[:1])
    return jnp.concatenate([vias * voltage_grid[1:], nought_value], 0) + jnp.concatenate([nought_value, vias * voltage_grid[:-1]], 0)

def via_total(vias):
    nought_value = jnp.zeros_like(vias[:1])
    return jnp.concatenate([vias, nought_value], 0) + jnp.concatenate([nought_value, vias], 0)

def operate(field_pad, edges, vias, diag):
    center = field_pad[:, 1:-1, 1:-1]
    near = jnp.zeros_like(center)
    for edge, other in zip(edges, neighbours(field_pad)):
        near = near + edge * other
    return diag * center - near - vertical(center, vias)

def joule_power(field_pad, edges, vias):
    center = field_pad[:, 1:-1, 1:-1]
    total = leak_cond * center * center
    for edge, other in zip(edges, neighbours(field_pad)):
        total = total + 0.5 * edge * (center - other) ** 2
    drop = vias * (center[:-1] - center[1:]) ** 2
    nought_value = jnp.zeros_like(center[:1])
    return total + 0.5 * (jnp.concatenate([drop, nought_value], 0) + jnp.concatenate([nought_value, drop], 0))

def warming_increment(warmth_excess, diffusivity, warmth_border, diffusivity_border, warming_load):
    energy_flow = jnp.zeros_like(warmth_excess)
    for partner_warmth, partner_diffusivity in zip(neighbours(warmth_border), neighbours(diffusivity_border)):
        energy_flow = energy_flow + jnp.sqrt(diffusivity * partner_diffusivity) * (partner_warmth - warmth_excess)
    nought_value = jnp.zeros_like(warmth_excess[:1])
    upright_flow = layer_admittance * (jnp.concatenate([warmth_excess[1:] - warmth_excess[:-1], nought_value], 0) + jnp.concatenate([nought_value, warmth_excess[:-1] - warmth_excess[1:]], 0))
    layer_total = warmth_excess.shape[0]
    upper_layer = (lax.broadcasted_iota(jnp.int32, (layer_total, 1, 1), 0) == layer_total - 1).astype(jnp.float32)
    return warmth_excess + interval_length * (energy_flow + upright_flow + warming_load - drain_admittance * upper_layer * warmth_excess)

def reference(prior_voltage, baseline_admittance, block_warmth, interlayer_indicator, feeder_indicator, injected_amperes):
    warmth_on_points = jnp.repeat(jnp.repeat(block_warmth, BLOCK_REFINE, axis=1), BLOCK_REFINE, axis=2)
    admittance = baseline_admittance * jnp.exp(-warmth_sensitivity * warmth_on_points)
    vias = via_cond * interlayer_indicator.astype(jnp.float32)
    inject = feeder_indicator.astype(jnp.float32) * injected_amperes
    edges = planar_edges(bordered_array(admittance))
    diag = leak_cond + edges[0] + edges[1] + edges[2] + edges[3] + via_total(vias)
    center_c = 0.5 * (spectrum_high + spectrum_low)
    half = 0.5 * (spectrum_high - spectrum_low)
    sigma = center_c / half
    rho = 1.0 / sigma
    voltage_grid = prior_voltage
    resid = inject - operate(bordered_array(voltage_grid), edges, vias, diag)
    step = resid / (diag * center_c)
    for sweep in range(SWEEPS):
        voltage_grid = voltage_grid + step
        if sweep < SWEEPS - 1:
            resid = inject - operate(bordered_array(voltage_grid), edges, vias, diag)
            rho_new = 1.0 / (2.0 * sigma - rho)
            step = rho_new * rho * step + 2.0 * rho_new / half * (resid / diag)
            rho = rho_new
    power = joule_power(bordered_array(voltage_grid), edges, vias)
    layer_total, rows, cols = power.shape
    warming_load = power.reshape(layer_total, rows // BLOCK_REFINE, BLOCK_REFINE, cols // BLOCK_REFINE, BLOCK_REFINE).sum(axis=(2, 4)) * heat_gain
    warmth_excess = block_warmth
    for sweep in range(HEAT_SWEEPS):
        diffusivity = jnp.exp(-warming_weight * warmth_excess)
        warmth_excess = warming_increment(warmth_excess, diffusivity, bordered_array(warmth_excess), bordered_array(diffusivity), warming_load)
    return (voltage_grid, warmth_excess)
```

```python
import functools

import jax
import jax.numpy as jnp
from jax import lax
from jax.experimental import pallas as pl
from jax.experimental.pallas import tpu as pltpu
from jax.sharding import PartitionSpec as P

F32 = jnp.float32
BF16 = jnp.bfloat16
MESH = pl.DeviceIdType.MESH

LEAK = 0.2
HALF = 0.95
SIGMA = 1.0 / HALF
RHO0 = 1.0 / SIGMA
RHO1 = 1.0 / (2.0 * SIGMA - RHO0)
RHO2 = 1.0 / (2.0 * SIGMA - RHO1)
STEP_1 = (RHO1 * RHO0, 2.0 * RHO1 / HALF)
STEP_2 = (RHO2 * RHO1, 2.0 * RHO2 / HALF)
HEAT_SWEEPS = 4
DT = 0.12
GAIN = 0.0625

ROWS = 128
M0 = 8
S0 = 144
R_ALL = 184
Q0 = 16
Q_ALL = 160
H0 = 12
H_ALL = 56

DIRS = ((-1, 0), (1, 0), (0, -1), (0, 1), (-1, -1), (-1, 1), (1, -1), (1, 1))


def iota(shape, dim):
    return lax.broadcasted_iota(jnp.int32, shape, dim)


def split3(x):
    high = x.astype(BF16)
    rest = x - high.astype(F32)
    mid = rest.astype(BF16)
    low = (rest - mid.astype(F32)).astype(BF16)
    return jnp.concatenate([high, mid, low], axis=0)


def dot3(x, ones):
    rows = x.shape[0]
    y = jnp.dot(split3(x), ones, preferred_element_type=F32)
    return y[:rows] + y[rows : 2 * rows] + y[2 * rows :]


def one_zero(mask):
    return jnp.where(mask, 1.0, 0.0).astype(BF16)


class Tile:
    @staticmethod
    def left(x):
        lane = iota(x.shape, 3)
        y = pltpu.roll(x, 1, 3)
        return jnp.where(lane == 0, jnp.concatenate([y[:, 3:], y[:, :3]], axis=1), y)

    @staticmethod
    def right(x):
        lane = iota(x.shape, 3)
        y = pltpu.roll(x, 127, 3)
        return jnp.where(lane == 127, jnp.concatenate([y[:, 1:], y[:, :1]], axis=1), y)

    @staticmethod
    def tiers(vias, x):
        up = vias * x[1:]
        down = vias * x[:3]
        return jnp.concatenate([up[:1], up[1:] + down[:2], down[2:]], axis=0)

    @staticmethod
    def via_sum(vias):
        return jnp.concatenate([vias[:1], vias[1:] + vias[:2], vias[2:]], axis=0)

    @staticmethod
    def drops(vias, x):
        e = x[:3] - x[1:]
        e = vias * (e * e)
        return jnp.concatenate([e[:1], e[1:] + e[:2], e[2:]], axis=0)


class Strip:
    @staticmethod
    def left(x):
        return pltpu.roll(x, 1, 1)

    @staticmethod
    def right(x):
        return pltpu.roll(x, 127, 1)

    @staticmethod
    def tiers(vias, x):
        return vias * pltpu.roll(x, 96, 1) + pltpu.roll(vias * x, 32, 1)

    @staticmethod
    def via_sum(vias):
        return vias + pltpu.roll(vias, 32, 1)

    @staticmethod
    def drops(vias, x):
        e = x - pltpu.roll(x, 96, 1)
        e = vias * (e * e)
        return e + pltpu.roll(e, 32, 1)


def around(kind, read, mid):
    return read(-1) + read(1) + kind.left(mid) + kind.right(mid)


def sweep_first(kind, at, g, x, j, v, inv, d, w_in, w_out):
    gm, wm, xm, vm = at(g)(0), at(w_in)(0), at(x)(0), at(v)(0)
    diag = LEAK + gm * around(kind, at(g), gm) + kind.via_sum(vm)
    i = 1.0 / diag
    new = i * (at(j)(0) + gm * around(kind, at(w_in), wm) + kind.tiers(vm, xm))
    at(inv).put(i)
    at(d).put(new - xm)
    at(w_out).put(gm * new)
    return new


def sweep_next(kind, at, g, x, j, v, inv, d, w_in, w_out, weights, last):
    gm, wm, xm, vm = at(g)(0), at(w_in)(0), at(x)(0), at(v)(0)
    z = at(inv)(0) * (at(j)(0) + gm * around(kind, at(w_in), wm) + kind.tiers(vm, xm)) - xm
    step = weights[0] * at(d)(0) + weights[1] * z
    new = xm + step
    if not last:
        at(d).put(step)
        at(w_out).put(gm * new)
    return new


def node_power(kind, at, g, x, v):
    gm, xm = at(g)(0), at(x)(0)
    up = xm - at(x)(-1)
    down = xm - at(x)(1)
    right = xm - kind.right(xm)
    e = gm * kind.right(gm) * (right * right)
    rows = gm * (at(g)(-1) * (up * up) + at(g)(1) * (down * down))
    return LEAK * xm * xm + 0.5 * (rows + e + kind.left(e) + kind.drops(at(v)(0), xm))


class View:
    def __init__(self, ref, start, size):
        self.ref, self.start, self.size = ref, start, size

    def index(self, k):
        rows = pl.ds(self.start + k, self.size)
        return (slice(None),) * (len(self.ref.shape) - 2) + (rows, slice(None))

    def __call__(self, k):
        return self.ref[self.index(k)]

    def put(self, value):
        self.ref[self.index(0)] = value


def solve(kind, start, steps, size, g, x, j, v, inv, d, wa, wb, power, power_start):
    def over(body):
        if steps == 1:
            body(start, power_start)
            return

        def one(n, carry):
            off = pl.multiple_of(n * size, size)
            body(start + off, power_start + off)
            return carry

        lax.fori_loop(0, steps, one, 0)

    def first(row, _):
        at = lambda ref: View(ref, row, size)
        at(x).put(sweep_first(kind, at, g, x, j, v, inv, d, wa, wb))

    def second(row, _):
        at = lambda ref: View(ref, row, size)
        at(x).put(sweep_next(kind, at, g, x, j, v, inv, d, wb, wa, STEP_1, False))

    def third(row, _):
        at = lambda ref: View(ref, row, size)
        at(x).put(sweep_next(kind, at, g, x, j, v, inv, d, wa, wb, STEP_2, True))

    def fourth(row, out):
        at = lambda ref: View(ref, row, size)
        View(power, out, size).put(node_power(kind, at, g, x, v))

    over(first)
    over(second)
    over(third)
    over(fourth)


def pack_edges(tiers):
    rows = tiers[0][0].shape[0]
    lane = iota((rows, 128), 1)
    out = jnp.zeros((rows, 128), F32)
    for t, (first, last) in enumerate(tiers):
        base = t * 32
        low = pltpu.roll(first, (base + 4) % 128, 1)
        high = pltpu.roll(last, (base + 16 - 116) % 128, 1)
        out = jnp.where((lane >= base + 4) & (lane < base + 16), low, out)
        out = jnp.where((lane >= base + 16) & (lane < base + 28), high, out)
    return out


def with_sides(mid, from_left, from_right):
    l32 = iota(mid.shape, 1) % 32
    mid = jnp.where(l32 < 4, pltpu.roll(from_left, 104, 1), mid)
    return jnp.where(l32 >= 28, pltpu.roll(from_right, 24, 1), mid)


def kernel(
    n_row, n_col,
    v_h, a_h, t_h, vi_h, fe_h, in_h,
    xo_h, to_h,
    x, g, j, v, inv, d, wa, wb, power,
    expand, a_raw, vi_raw, fe_raw, in_raw, t_raw,
    qx, qg, qj, qv, qi, qd, qa, qb, qpower,
    ra_s, ra_r, rb_s, rb_r, cm_s, cm_r, cr_r,
    load, r2_s, r2_r, c2_s, c2_r, k2_r,
    ts, tu, hs, hu, tt, tl, ht, hl, t_out,
    in_sem, out_sem, send_sem, recv_sem, send2_sem, recv2_sem,
):
    row = lax.axis_index("row")
    col = lax.axis_index("col")

    def there(dr, dc):
        ok = None
        for cond in (
            (row > 0) if dr < 0 else (row < n_row - 1) if dr > 0 else None,
            (col > 0) if dc < 0 else (col < n_col - 1) if dc > 0 else None,
        ):
            if cond is not None:
                ok = cond if ok is None else jnp.logical_and(ok, cond)
        return ok

    def device(dr, dc):
        return {"row": row + dr, "col": col + dc}

    barrier = pltpu.get_barrier_semaphore()
    for dr, dc in DIRS:

        @pl.when(there(dr, dc))
        def _(dr=dr, dc=dc):
            pl.semaphore_signal(
                barrier, inc=1, device_id=device(dr, dc), device_id_type=MESH
            )

    copies = {}
    slot = 0

    def fetch(name, src, dst):
        nonlocal slot
        copy = pltpu.make_async_copy(src, dst, in_sem.at[slot])
        slot += 1
        copy.start()
        copies.setdefault(name, []).append(copy)

    fetch("t", t_h, t_raw)
    for name, src, dst, first in (
        ("a", a_h, a_raw, 0),
        ("x", v_h, x, M0),
        ("v", vi_h, vi_raw, 0),
        ("f", fe_h, fe_raw, 0),
        ("i", in_h, in_raw, 0),
    ):
        for b in range(4):
            fetch(
                name,
                src.at[:, :, pl.ds(128 * b, 128)],
                dst.at[:, b, pl.ds(first, ROWS), :],
            )

    def arrived(*names):
        for name in names:
            for copy in copies[name]:
                copy.wait()

    for ref in (x, g, wa, wb):
        for start in (0, M0 + ROWS, S0 + 32):
            ref[:, :, pl.ds(start, 8), :] = jnp.zeros((4, 4, 8, 128), F32)
    for ref in (qx, qg, qj, qv, qa, qb):
        for start in (0, Q0 + ROWS):
            ref[pl.ds(start, 16), :] = jnp.zeros((16, 128), F32)
    for ref in (ts, tu):
        for start in (0, 48):
            ref[:, pl.ds(start, 8), :] = jnp.zeros((4, 8, 128), F32)
    for ref in (hs, hu):
        for start in (0, 48):
            ref[pl.ds(start, 8), :] = jnp.zeros((8, 128), F32)
    for s in range(2):
        rb_s[s, pl.ds(16, 8), :] = jnp.zeros((8, 128), F32)
        r2_s[s, pl.ds(0, 8), :] = jnp.zeros((8, 128), F32)

        @pl.when(jnp.logical_not(there(*DIRS[s])))
        def _(s=s):
            ra_r[s] = jnp.zeros((15, 2, 8, 128), F32)
            rb_r[s] = jnp.zeros((40, 128), F32)
            r2_r[s] = jnp.zeros((24, 128), F32)

        @pl.when(jnp.logical_not(there(*DIRS[2 + s])))
        def _(s=s):
            cm_r[s] = jnp.zeros((96, 128), F32)
            c2_r[s] = jnp.zeros((32, 128), F32)

    for s in range(4):

        @pl.when(jnp.logical_not(there(*DIRS[4 + s])))
        def _(s=s):
            cr_r[s] = jnp.zeros((24, 128), F32)
            k2_r[s] = jnp.zeros((8, 128), F32)

    arrived("t")
    cells = jnp.exp(-0.25 * t_raw[...]).reshape(128, 128)
    wide = iota((128, 512), 1) // 4 == iota((128, 512), 0)
    fine = dot3(cells, one_zero(wide))
    for b in range(4):
        part = fine[:, 128 * b : 128 * (b + 1)].reshape(4, 32, 128)
        for k in range(4):
            expand[:, b, pl.ds(k, 32, 4), :] = part

    arrived("a", "x", "v", "f", "i")

    def prepare(n, carry):
        off = pl.multiple_of(n * 8, 8)
        at = lambda ref, first: View(ref, first + off, 8)
        adm = at(a_raw, 0)(0)
        gm = adm * lax.rsqrt(adm) * at(expand, 0)(0)
        at(g, M0).put(gm)
        at(wa, M0).put(gm * at(x, M0)(0))
        at(j, M0).put(at(fe_raw, 0)(0).astype(F32) * at(in_raw, 0)(0))
        at(v, M0).put(at(vi_raw, 0)(0).astype(F32))
        return carry

    lax.fori_loop(0, ROWS // 8, prepare, 0)

    for ref, packed, tiers in ((x, qx, 4), (g, qg, 4), (j, qj, 4), (v, qv, 3)):
        packed[pl.ds(Q0, ROWS), :] = pack_edges(
            [
                (ref[t, 0, pl.ds(M0, ROWS), :], ref[t, 3, pl.ds(M0, ROWS), :])
                for t in range(tiers)
            ]
        )
    t_edges = pack_edges([(t_raw[t], t_raw[t]) for t in range(4)])

    group = (iota((64, 128), 1) % 32) // 4
    for s, lane0 in ((0, 4), (1, 24)):
        mixed = jnp.zeros((64, 128), F32)
        for k, packed in enumerate((qx, qg, qj, qv)):
            for h in range(2):
                part = pltpu.roll(
                    packed[pl.ds(Q0 + 64 * h, 64), :], (h * 16 + k * 4 - lane0) % 128, 1
                )
                mixed = jnp.where(group == h * 4 + k, part, mixed)
        cm_s[s, pl.ds(0, 64), :] = mixed
        cm_s[s, pl.ds(64, 32), :] = t_edges
    for s, first in ((0, 0), (1, ROWS - 4)):
        for k, (ref, tiers) in enumerate(((x, 4), (g, 4), (j, 4), (v, 3))):
            for h in range(2):
                ra_s[s, pl.ds(4 * k, tiers), :, pl.ds(4 * h, 4), :] = ref[
                    :, pl.ds(2 * h, 2), pl.ds(M0 + first, 4), :
                ]
        for k, packed in enumerate((qx, qg, qj, qv)):
            rb_s[s, pl.ds(4 * k, 4), :] = packed[pl.ds(Q0 + first, 4), :]
        cell = 0 if s == 0 else 28
        rb_s[s, pl.ds(16, 4), :] = t_edges[cell : cell + 4]
        for t in range(4):
            rb_s[s, pl.ds(24 + 4 * t, 4), :] = t_raw[t, pl.ds(cell, 4), :]

    neighbours = 0
    for dr, dc in DIRS:
        neighbours = neighbours + there(dr, dc).astype(jnp.int32)
    pl.semaphore_wait(barrier, neighbours)

    def remote(src, dst, send, recv, dr, dc):
        return pltpu.make_async_remote_copy(
            src_ref=src,
            dst_ref=dst,
            send_sem=send,
            recv_sem=recv,
            device_id=device(dr, dc),
            device_id_type=MESH,
        )

    first_exchange = []
    for s in range(2):
        first_exchange.append((DIRS[s], ra_s.at[s], ra_r.at[1 - s], s, 1 - s))
        first_exchange.append((DIRS[s], rb_s.at[s], rb_r.at[1 - s], 2 + s, 3 - s))
        first_exchange.append((DIRS[2 + s], cm_s.at[s], cm_r.at[1 - s], 4 + s, 5 - s))
    for s in range(4):
        first_exchange.append(
            (DIRS[4 + s], rb_s.at[s // 2, pl.ds(0, 24)], cr_r.at[3 - s], 6 + s, 9 - s)
        )
    second_exchange = []
    for s in range(2):
        second_exchange.append((DIRS[s], r2_s.at[s], r2_r.at[1 - s], s, 1 - s))
        second_exchange.append((DIRS[2 + s], c2_s, c2_r.at[1 - s], 2 + s, 3 - s))
    for s in range(4):
        second_exchange.append(
            (DIRS[4 + s], r2_s.at[s // 2, pl.ds(0, 8)], k2_r.at[3 - s], 4 + s, 7 - s)
        )

    def start(exchange, sends, recvs):
        for (dr, dc), src, dst, a, b in exchange:

            @pl.when(there(dr, dc))
            def _(dr=dr, dc=dc, src=src, dst=dst, a=a, b=b):
                remote(src, dst, sends.at[a], recvs.at[b], dr, dc).start()

    def wait_recv(exchange, sends, recvs):
        for (dr, dc), src, dst, a, b in exchange:

            @pl.when(there(-dr, -dc))
            def _(dr=dr, dc=dc, src=src, dst=dst, a=a, b=b):
                remote(src, dst, sends.at[a], recvs.at[b], -dr, -dc).wait_recv()

    def wait_send(exchange, sends, recvs):
        for (dr, dc), src, dst, a, b in exchange:

            @pl.when(there(dr, dc))
            def _(dr=dr, dc=dc, src=src, dst=dst, a=a, b=b):
                remote(src, dst, sends.at[a], recvs.at[b], dr, dc).wait_send()

    start(first_exchange, send_sem, recv_sem)

    nodes = ((x, 4), (g, 4), (j, 4), (v, 3))
    for ref, _ in nodes:
        ref[:, :, pl.ds(S0 + 4, 12), :] = ref[:, :, pl.ds(M0, 12), :]
        ref[:, :, pl.ds(S0 + 16, 12), :] = ref[:, :, pl.ds(M0 + ROWS - 12, 12), :]

    solve(Tile, M0, ROWS // 8, 8, g, x, j, v, inv, d, wa, wb, power, 0)

    wait_recv(first_exchange, send_sem, recv_sem)

    for s, first in ((0, 0), (1, 28)):
        for k, (ref, tiers) in enumerate(nodes):
            for h in range(2):
                ref[:, pl.ds(2 * h, 2), pl.ds(S0 + first, 4), :] = ra_r[
                    s, pl.ds(4 * k, tiers), :, pl.ds(4 * h, 4), :
                ]
    strip = pl.ds(S0, 32)
    wa[:, :, strip, :] = g[:, :, strip, :] * x[:, :, strip, :]
    solve(Tile, S0, 4, 8, g, x, j, v, inv, d, wa, wb, power, ROWS)

    l32 = iota((64, 128), 1) % 32
    for k, packed in enumerate((qx, qg, qj, qv)):
        for s, first in ((0, Q0 - 4), (1, Q0 + ROWS)):
            part = pl.ds(4 * k, 4)
            packed[pl.ds(first, 4), :] = with_sides(
                rb_r[s, part, :], cr_r[2 * s, part, :], cr_r[2 * s + 1, part, :]
            )
        for h in range(2):
            rows = pl.ds(Q0 + 64 * h, 64)
            lane0 = h * 16 + k * 4
            mid = packed[rows, :]
            mid = jnp.where(
                l32 < 4, pltpu.roll(cm_r[0, pl.ds(0, 64), :], -lane0 % 128, 1), mid
            )
            packed[rows, :] = jnp.where(
                l32 >= 28, pltpu.roll(cm_r[1, pl.ds(0, 64), :], (28 - lane0) % 128, 1), mid
            )
    strip = pl.ds(8, 144)
    qa[strip, :] = qg[strip, :] * qx[strip, :]
    solve(Strip, 8, 1, 144, qg, qx, qj, qv, qi, qd, qa, qb, qpower, 8)

    x[:, :, pl.ds(M0, 4), :] = x[:, :, pl.ds(S0 + 4, 4), :]
    x[:, :, pl.ds(M0 + ROWS - 4, 4), :] = x[:, :, pl.ds(S0 + 24, 4), :]
    power[:, :, pl.ds(0, 4), :] = power[:, :, pl.ds(ROWS + 4, 4), :]
    power[:, :, pl.ds(ROWS - 4, 4), :] = power[:, :, pl.ds(ROWS + 24, 4), :]
    lane = iota((ROWS, 128), 1)
    sides = qx[pl.ds(Q0, ROWS), :]
    tile = pl.ds(M0, ROWS)
    for t in range(4):
        x[t, 0, tile, :] = jnp.where(
            lane < 4, pltpu.roll(sides, (-4 - 32 * t) % 128, 1), x[t, 0, tile, :]
        )
        x[t, 3, tile, :] = jnp.where(
            lane >= 124, pltpu.roll(sides, (100 - 32 * t) % 128, 1), x[t, 3, tile, :]
        )
    out_copies = []
    for b in range(4):
        copy = pltpu.make_async_copy(
            x.at[:, b, tile, :], xo_h.at[:, :, pl.ds(128 * b, 128)], out_sem.at[b]
        )
        copy.start()
        out_copies.append(copy)

    sums = power[:, :, pl.ds(0, 32, 4), :]
    edge_sums = qpower[pl.ds(Q0, 32, 4), :]
    for k in range(1, 4):
        sums = sums + power[:, :, pl.ds(k, 32, 4), :]
        edge_sums = edge_sums + qpower[pl.ds(Q0 + k, 32, 4), :]
    total = jnp.zeros((128, 128), F32)
    for h in range(2):
        node, cell = iota((256, 128), 0), iota((256, 128), 1)
        pick = (node // 4 + 64 * h == cell) & (cell > 0) & (cell < 127)
        both = jnp.concatenate(
            [sums[:, 2 * h].reshape(128, 128), sums[:, 2 * h + 1].reshape(128, 128)], axis=1
        )
        total = total + dot3(both, one_zero(pick))
    lane, cell = iota((128, 512), 0), iota((128, 512), 1)
    base = (cell // 128) * 32
    pick = ((cell % 128 == 0) & (lane >= base + 4) & (lane < base + 8)) | (
        (cell % 128 == 127) & (lane >= base + 24) & (lane < base + 28)
    )
    edge_cells = dot3(edge_sums, one_zero(pick))
    for t in range(4):
        load[t] = GAIN * (
            total[32 * t : 32 * (t + 1)] + edge_cells[:, 128 * t : 128 * (t + 1)]
        )

    l_edges = pack_edges([(load[t], load[t]) for t in range(4)])
    c2_s[...] = l_edges
    for s, cell in ((0, 0), (1, 28)):
        r2_s[s, pl.ds(0, 4), :] = l_edges[cell : cell + 4]
        for t in range(4):
            r2_s[s, pl.ds(8 + 4 * t, 4), :] = load[t, pl.ds(cell, 4), :]
    start(second_exchange, send2_sem, recv2_sem)

    for t in range(4):
        tt[t, pl.ds(0, 4), :] = rb_r[0, pl.ds(24 + 4 * t, 4), :]
        tt[t, pl.ds(4, 32), :] = t_raw[t]
        tt[t, pl.ds(36, 4), :] = rb_r[1, pl.ds(24 + 4 * t, 4), :]
    cells = pl.ds(64, 32)
    edge = pl.ds(16, 4)
    ht[pl.ds(0, 4), :] = with_sides(rb_r[0, edge, :], cr_r[0, edge, :], cr_r[1, edge, :])
    ht[pl.ds(4, 32), :] = with_sides(t_edges, cm_r[0, cells, :], cm_r[1, cells, :])
    ht[pl.ds(36, 4), :] = with_sides(rb_r[1, edge, :], cr_r[2, edge, :], cr_r[3, edge, :])

    r = iota((40, 128), 0)
    l32 = iota((40, 128), 1) % 32
    rows_in = ((r >= 4) | (row > 0)) & ((r < 36) | (row < n_row - 1))
    cols_in = ((l32 >= 4) | (col > 0)) & ((l32 < 28) | (col < n_col - 1))
    row_mask = jnp.where(rows_in, 1.0, 0.0).astype(F32)
    all_mask = jnp.where(rows_in & cols_in, 1.0, 0.0).astype(F32)
    tier = iota((40, 128), 1) // 32
    not_first = jnp.where(tier > 0, 1.0, 0.0).astype(F32)
    not_last = jnp.where(tier < 3, 1.0, 0.0).astype(F32)

    def increment_tile(theta):
        s = jnp.exp(-0.15 * theta) * row_mask
        u = s * theta
        ts[:, pl.ds(8, 40), :] = s
        tu[:, pl.ds(8, 40), :] = u
        near_s = ts[:, pl.ds(7, 40), :] + ts[:, pl.ds(9, 40), :]
        near_u = tu[:, pl.ds(7, 40), :] + tu[:, pl.ds(9, 40), :]
        near_s = near_s + pltpu.roll(s, 1, 2) + pltpu.roll(s, 127, 2)
        near_u = near_u + pltpu.roll(u, 1, 2) + pltpu.roll(u, 127, 2)
        flux = s * (near_u - theta * near_s)
        vert = jnp.concatenate(
            [
                theta[1:2] - theta[0:1],
                theta[0:2] + theta[2:4] - 2.0 * theta[1:3],
                theta[2:3] - 2.0 * theta[3:4],
            ],
            axis=0,
        )
        return flux + vert

    def increment_strip(theta):
        s = jnp.exp(-0.15 * theta) * all_mask
        u = s * theta
        hs[pl.ds(8, 40), :] = s
        hu[pl.ds(8, 40), :] = u
        near_s = hs[pl.ds(7, 40), :] + hs[pl.ds(9, 40), :]
        near_u = hu[pl.ds(7, 40), :] + hu[pl.ds(9, 40), :]
        near_s = near_s + pltpu.roll(s, 1, 1) + pltpu.roll(s, 127, 1)
        near_u = near_u + pltpu.roll(u, 1, 1) + pltpu.roll(u, 127, 1)
        flux = s * (near_u - theta * near_s)
        vert = (
            not_last * pltpu.roll(theta, 96, 1)
            + not_first * pltpu.roll(theta, 32, 1)
            - (1.0 + not_first) * theta
        )
        return flux + vert

    theta, side = tt[...], ht[...]
    gain, side_gain = increment_tile(theta), increment_strip(side)

    wait_recv(second_exchange, send2_sem, recv2_sem)
    for t in range(4):
        tl[t, pl.ds(0, 4), :] = r2_r[0, pl.ds(8 + 4 * t, 4), :]
        tl[t, pl.ds(4, 32), :] = load[t]
        tl[t, pl.ds(36, 4), :] = r2_r[1, pl.ds(8 + 4 * t, 4), :]
    edge = pl.ds(0, 4)
    hl[pl.ds(0, 4), :] = with_sides(r2_r[0, edge, :], k2_r[0, edge, :], k2_r[1, edge, :])
    hl[pl.ds(4, 32), :] = with_sides(l_edges, c2_r[0], c2_r[1])
    hl[pl.ds(36, 4), :] = with_sides(r2_r[1, edge, :], k2_r[2, edge, :], k2_r[3, edge, :])
    heat, side_heat = tl[...], hl[...]

    for sweep in range(HEAT_SWEEPS):
        if sweep > 0:
            gain, side_gain = increment_tile(theta), increment_strip(side)
        theta = theta + DT * (gain + heat)
        side = side + DT * (side_gain + side_heat)

    tt[...] = theta
    ht[...] = side
    lane = iota((32, 128), 1)
    sides = ht[pl.ds(4, 32), :]
    for t in range(4):
        mid = tt[t, pl.ds(4, 32), :]
        mid = jnp.where(lane < 4, pltpu.roll(sides, (-4 - 32 * t) % 128, 1), mid)
        mid = jnp.where(lane >= 124, pltpu.roll(sides, (100 - 32 * t) % 128, 1), mid)
        t_out[t] = mid
    copy = pltpu.make_async_copy(t_out, to_h, out_sem.at[4])
    copy.start()
    out_copies.append(copy)

    wait_send(first_exchange, send_sem, recv_sem)
    wait_send(second_exchange, send2_sem, recv2_sem)
    for copy in out_copies:
        copy.wait()


def vmem(*shape, dtype=F32):
    return pltpu.VMEM(shape, dtype)


def on_device(n_row, n_col, *args):
    node = (4, 4, R_ALL, 128)
    raw = (4, 4, ROWS, 128)
    strip = (Q_ALL, 128)
    scratch = [
        vmem(*node), vmem(*node), vmem(*node), vmem(3, *node[1:]),
        vmem(*node), vmem(*node), vmem(*node), vmem(*node),
        vmem(4, 4, ROWS + 32, 128),
        vmem(*raw), vmem(*raw), vmem(3, *raw[1:], dtype=jnp.int32),
        vmem(*raw, dtype=jnp.int32), vmem(*raw), vmem(4, 32, 128),
        *[vmem(*strip) for _ in range(9)],
        vmem(2, 15, 2, 8, 128), vmem(2, 15, 2, 8, 128),
        vmem(2, 40, 128), vmem(2, 40, 128),
        vmem(2, 96, 128), vmem(2, 96, 128),
        vmem(4, 24, 128),
        vmem(4, 32, 128),
        vmem(2, 24, 128), vmem(2, 24, 128),
        vmem(32, 128), vmem(2, 32, 128),
        vmem(4, 8, 128),
        vmem(4, H_ALL, 128), vmem(4, H_ALL, 128), vmem(H_ALL, 128), vmem(H_ALL, 128),
        vmem(4, 40, 128), vmem(4, 40, 128), vmem(40, 128), vmem(40, 128),
        vmem(4, 32, 128),
        pltpu.SemaphoreType.DMA((21,)),
        pltpu.SemaphoreType.DMA((5,)),
        pltpu.SemaphoreType.DMA((10,)),
        pltpu.SemaphoreType.DMA((10,)),
        pltpu.SemaphoreType.DMA((8,)),
        pltpu.SemaphoreType.DMA((8,)),
    ]
    hbm = pl.BlockSpec(memory_space=pl.ANY)
    return pl.pallas_call(
        functools.partial(kernel, n_row, n_col),
        out_shape=(
            jax.ShapeDtypeStruct((4, ROWS, 512), F32),
            jax.ShapeDtypeStruct((4, 32, 128), F32),
        ),
        in_specs=[hbm] * 6,
        out_specs=(hbm, hbm),
        scratch_shapes=scratch,
        compiler_params=pltpu.CompilerParams(
            collective_id=0,
            has_side_effects=True,
            vmem_limit_bytes=56 * 1024 * 1024,
        ),
    )(*args)


def solution(mesh):
    spec = P(None, "row", "col")
    return jax.shard_map(
        functools.partial(on_device, mesh.shape["row"], mesh.shape["col"]),
        mesh=mesh,
        in_specs=(spec,) * 6,
        out_specs=(spec, spec),
        check_vma=False,
    )
```

```python
import functools

import jax
import jax.numpy as jnp
from jax import lax
from jax.experimental import pallas as pl
from jax.experimental.pallas import tpu as pltpu
from jax.sharding import PartitionSpec as P

F32 = jnp.float32
BF16 = jnp.bfloat16
MESH = pl.DeviceIdType.MESH

LEAK = 0.2
HALF = 0.95
SIGMA = 1.0 / HALF
RHO0 = 1.0 / SIGMA
RHO1 = 1.0 / (2.0 * SIGMA - RHO0)
RHO2 = 1.0 / (2.0 * SIGMA - RHO1)
STEP_1 = (RHO1 * RHO0, 2.0 * RHO1 / HALF)
STEP_2 = (RHO2 * RHO1, 2.0 * RHO2 / HALF)
HEAT_SWEEPS = 4
DT = 0.12
GAIN = 0.0625
MAIN_UNROLL = 4
KERNEL_FLAGS = {}
STRIP_UNROLL = 1

ROWS = 128
M0 = 8
S0 = 144
R_ALL = 176
Q0 = 16
Q_ALL = 160

DIRS = ((-1, 0), (1, 0), (0, -1), (0, 1), (-1, -1), (-1, 1), (1, -1), (1, 1))


def iota(shape, dim):
    return lax.broadcasted_iota(jnp.int32, shape, dim)


def split3(x):
    high = x.astype(BF16)
    rest = x - high.astype(F32)
    mid = rest.astype(BF16)
    low = (rest - mid.astype(F32)).astype(BF16)
    return jnp.concatenate([high, mid, low], axis=0)


def dot3(x, ones):
    rows = x.shape[0]
    y = jnp.dot(split3(x), ones, preferred_element_type=F32)
    return y[:rows] + y[rows : 2 * rows] + y[2 * rows :]


def one_zero(mask):
    return jnp.where(mask, 1.0, 0.0).astype(BF16)


class Tile:
    tiers = range(4)

    @staticmethod
    def part(ref, t, row, size):
        return ref[t, :, pl.ds(row, size), :]

    @staticmethod
    def put(ref, t, row, size, value):
        ref[t, :, pl.ds(row, size), :] = value

    @staticmethod
    def left(x):
        lane = iota(x.shape, 2)
        y = pltpu.roll(x, 1, 2)
        return jnp.where(lane == 0, jnp.concatenate([y[3:], y[:3]], axis=0), y)

    @staticmethod
    def right(x):
        lane = iota(x.shape, 2)
        y = pltpu.roll(x, 127, 2)
        return jnp.where(lane == 127, jnp.concatenate([y[1:], y[:1]], axis=0), y)

    @staticmethod
    def vertical(read, v, x, t):
        if t == 0:
            return read(v, 0) * read(x, 1)
        if t == 3:
            return read(v, 2) * read(x, 2)
        return read(v, t) * read(x, t + 1) + read(v, t - 1) * read(x, t - 1)

    @staticmethod
    def via_sum(read, v, t):
        if t == 0:
            return read(v, 0)
        if t == 3:
            return read(v, 2)
        return read(v, t) + read(v, t - 1)

    @staticmethod
    def drops(read, v, x, t):
        total = None
        for low in (t - 1, t):
            if 0 <= low < 3:
                e = read(x, low) - read(x, low + 1)
                e = read(v, low) * (e * e)
                total = e if total is None else total + e
        return total


class Strip:
    tiers = (0,)

    @staticmethod
    def part(ref, t, row, size):
        return ref[pl.ds(row, size), :]

    @staticmethod
    def put(ref, t, row, size, value):
        ref[pl.ds(row, size), :] = value

    @staticmethod
    def left(x):
        return pltpu.roll(x, 1, 1)

    @staticmethod
    def right(x):
        return pltpu.roll(x, 127, 1)

    @staticmethod
    def vertical(read, v, x, t):
        vm, xm = read(v, t), read(x, t)
        return vm * pltpu.roll(xm, 96, 1) + pltpu.roll(vm * xm, 32, 1)

    @staticmethod
    def via_sum(read, v, t):
        vm = read(v, t)
        return vm + pltpu.roll(vm, 32, 1)

    @staticmethod
    def drops(read, v, x, t):
        xm = read(x, t)
        e = xm - pltpu.roll(xm, 96, 1)
        e = read(v, t) * (e * e)
        return e + pltpu.roll(e, 32, 1)


class Domain:
    def __init__(self, kind, g, j, v, inv, x, d, w, power):
        self.kind, self.g, self.j, self.v, self.inv = kind, g, j, v, inv
        self.x, self.d, self.w, self.power = x, d, w, power

    def sweep(self, p, row, out, size):
        kind, g, v = self.kind, self.g, self.v
        x, d, w = self.x[min(p, 3)], self.d, self.w
        for t in kind.tiers:
            read = lambda ref, t=t, k=0: kind.part(ref, t, row + k, size)
            put = lambda ref, value, t=t: kind.put(ref, t, row, size, value)

            def around(ref, mid):
                rows = read(ref, t, -1) + read(ref, t, 1)
                return rows + kind.left(mid) + kind.right(mid)

            gm, xm = read(g, t), read(x, t)
            if p == 3:
                up, down = xm - read(x, t, -1), xm - read(x, t, 1)
                right = xm - kind.right(xm)
                e = gm * kind.right(gm) * (right * right)
                rows = gm * (read(g, t, -1) * (up * up) + read(g, t, 1) * (down * down))
                total = rows + e + kind.left(e) + kind.drops(read, v, x, t)
                kind.put(self.power, t, out, size, LEAK * xm * xm + 0.5 * total)
                continue
            near = gm * around(w[p], read(w[p], t)) + kind.vertical(read, v, x, t)
            if p == 0:
                diag = LEAK + gm * around(g, gm) + kind.via_sum(read, v, t)
                inv = 1.0 / diag
                new = inv * (read(self.j, t) + near)
                put(self.inv, inv)
                put(d[0], new - xm)
            else:
                z = read(self.inv, t) * (read(self.j, t) + near) - xm
                weights = STEP_1 if p == 1 else STEP_2
                step = weights[0] * read(d[p - 1], t) + weights[1] * z
                new = xm + step
                if p == 1:
                    put(d[1], step)
            put(self.x[p + 1], new)
            if p < 2:
                put(w[p + 1], gm * new)


def solve(steps, unroll, *parts):
    for p in range(4):

        def one(n, carry):
            for domain, row, out, size in parts:
                off = pl.multiple_of(n * size, size)
                domain.sweep(p, row + off, out + off, size)
            return carry

        lax.fori_loop(0, steps, one, 0, unroll=unroll)


def lane32(shape):
    return (iota(shape, 1) + 20) % 32


def pack_edges(tiers):
    shape = tiers[0][0].shape
    group = ((iota(shape, 1) + 12) // 32) % 4
    out = jnp.zeros(shape, F32)
    for t, (first, last) in enumerate(tiers):
        ends = first if first is last else jnp.where(iota(shape, 1) < 64, first, last)
        if t:
            ends = pltpu.roll(ends, 32 * t, 1)
        out = jnp.where(group == t, ends, out)
    return jnp.where(lane32(shape) >= 16, out, pltpu.roll(out, 120, 1))


def unpack_edges(packed, tiers):
    ends = jnp.where(lane32(packed.shape) >= 20, packed, pltpu.roll(packed, 8, 1))
    return [pltpu.roll(ends, (-32 * t) % 128, 1) if t else ends for t in range(tiers)]


def with_sides(mid, from_left, from_right):
    l32 = lane32(mid.shape)
    mid = jnp.where((l32 >= 16) & (l32 < 20), pltpu.roll(from_left, 8, 1), mid)
    return jnp.where((l32 >= 12) & (l32 < 16), pltpu.roll(from_right, 120, 1), mid)


def kernel(
    n_row, n_col,
    v_h, a_h, t_h, vi_h, fe_h, in_h,
    x3, tt, ht, tl, hl,
    x, x1, x2, g, j, v, inv, d, d1, wa, wb, wc, power,
    expand, a_raw, vi_raw, fe_raw, in_raw, t_raw,
    qx, qx1, qx2, qx3, qg, qj, qv, qi, qd, qd1, qa, qb, qc, qpower,
    ra_s, ra_r, rb_s, rb_r, cm_s, cm_r, cr_r,
    load, r2_s, r2_r, c2_s, c2_r, k2_r, ts, tu, hs, hu,
    in_sem, send_sem, recv_sem, send2_sem, recv2_sem,
):
    row = lax.axis_index("row")
    col = lax.axis_index("col")

    def there(dr, dc):
        ok = None
        for cond in (
            (row > 0) if dr < 0 else (row < n_row - 1) if dr > 0 else None,
            (col > 0) if dc < 0 else (col < n_col - 1) if dc > 0 else None,
        ):
            if cond is not None:
                ok = cond if ok is None else jnp.logical_and(ok, cond)
        return ok

    def device(dr, dc):
        return {"row": row + dr, "col": col + dc}

    barrier = pltpu.get_barrier_semaphore()
    for dr, dc in DIRS:

        @pl.when(there(dr, dc))
        def _(dr=dr, dc=dc):
            pl.semaphore_signal(
                barrier, inc=1, device_id=device(dr, dc), device_id_type=MESH
            )

    copies = {}
    slot = 0

    def fetch(name, src, dst):
        nonlocal slot
        copy = pltpu.make_async_copy(src, dst, in_sem.at[slot])
        slot += 1
        copy.start()
        copies.setdefault(name, []).append(copy)

    fetch("t", t_h, t_raw)
    for name, src, dst, first in (
        ("a", a_h, a_raw, 0),
        ("x", v_h, x, M0),
        ("v", vi_h, vi_raw, 0),
        ("f", fe_h, fe_raw, 0),
        ("i", in_h, in_raw, 0),
    ):
        for b in range(4):
            fetch(
                name,
                src.at[:, :, pl.ds(128 * b, 128)],
                dst.at[:, b, pl.ds(first, ROWS), :],
            )

    def arrived(*names):
        for name in names:
            for copy in copies[name]:
                copy.wait()

    for ref in (x3, g, wa, wb, wc):
        for start in (0, M0 + ROWS, S0 + 24):
            ref[:, :, pl.ds(start, 8), :] = jnp.zeros((4, 4, 8, 128), F32)
    for ref in (qx, qx3, qg, qj, qv, qa, qb, qc):
        for start in (0, Q0 + ROWS):
            ref[pl.ds(start, 16), :] = jnp.zeros((16, 128), F32)
    for ref in (ts, tu):
        for start in (0, 48):
            ref[:, pl.ds(start, 8), :] = jnp.zeros((4, 8, 128), F32)
    for ref in (hs, hu):
        for start in (0, 48):
            ref[pl.ds(start, 8), :] = jnp.zeros((8, 128), F32)
    for s in range(2):
        rb_s[s, pl.ds(16, 8), :] = jnp.zeros((8, 128), F32)
        r2_s[s, pl.ds(0, 8), :] = jnp.zeros((8, 128), F32)

        @pl.when(jnp.logical_not(there(*DIRS[s])))
        def _(s=s):
            ra_r[s] = jnp.zeros((15, 2, 8, 128), F32)
            rb_r[s] = jnp.zeros((40, 128), F32)
            r2_r[s] = jnp.zeros((24, 128), F32)

        @pl.when(jnp.logical_not(there(*DIRS[2 + s])))
        def _(s=s):
            cm_r[s] = jnp.zeros((96, 128), F32)
            c2_r[s] = jnp.zeros((32, 128), F32)

    for s in range(4):

        @pl.when(jnp.logical_not(there(*DIRS[4 + s])))
        def _(s=s):
            cr_r[s] = jnp.zeros((24, 128), F32)
            k2_r[s] = jnp.zeros((8, 128), F32)

    arrived("t")
    cells = jnp.exp(-0.25 * t_raw[...]).reshape(128, 128)
    wide = iota((128, 512), 1) // 4 == iota((128, 512), 0)
    fine = dot3(cells, one_zero(wide))
    for b in range(4):
        part = fine[:, 128 * b : 128 * (b + 1)].reshape(4, 32, 128)
        for k in range(4):
            expand[:, b, pl.ds(k, 32, 4), :] = part

    arrived("a", "x", "v", "f", "i")

    def prepare(off):
        raw, rows = pl.ds(off, 8), pl.ds(M0 + off, 8)
        for t in range(4):
            adm = a_raw[t, :, raw, :]
            gm = adm * lax.rsqrt(adm) * expand[t, :, raw, :]
            g[t, :, rows, :] = gm
            wa[t, :, rows, :] = gm * x[t, :, rows, :]
            j[t, :, rows, :] = fe_raw[t, :, raw, :].astype(F32) * in_raw[t, :, raw, :]
            if t < 3:
                v[t, :, rows, :] = vi_raw[t, :, raw, :].astype(F32)

    def remote(src, dst, send, recv, dr, dc):
        return pltpu.make_async_remote_copy(
            src_ref=src,
            dst_ref=dst,
            send_sem=send,
            recv_sem=recv,
            device_id=device(dr, dc),
            device_id_type=MESH,
        )

    nodes = ((x, 4), (g, 4), (j, 4), (v, 3))
    strips = (qx, qg, qj, qv)

    prepare(0)
    prepare(ROWS - 8)
    for s, first in ((0, 0), (1, ROWS - 4)):
        for k, (ref, tiers) in enumerate(nodes):
            for h in range(2):
                ra_s[s, pl.ds(4 * k, tiers), :, pl.ds(4 * h, 4), :] = ref[
                    :, pl.ds(2 * h, 2), pl.ds(M0 + first, 4), :
                ]

    neighbours = 0
    for dr, dc in DIRS:
        neighbours = neighbours + there(dr, dc).astype(jnp.int32)
    pl.semaphore_wait(barrier, neighbours)

    row_exchange, first_exchange = [], []
    for s in range(2):
        row_exchange.append((DIRS[s], ra_s.at[s], ra_r.at[1 - s], s, 1 - s))
        first_exchange.append((DIRS[s], rb_s.at[s], rb_r.at[1 - s], 2 + s, 3 - s))
    for s in range(4):
        first_exchange.append(
            (DIRS[4 + s], rb_s.at[s // 2, pl.ds(0, 24)], cr_r.at[3 - s], 6 + s, 9 - s)
        )
    for s in range(2):
        first_exchange.append((DIRS[2 + s], cm_s.at[s], cm_r.at[1 - s], 4 + s, 5 - s))
    second_exchange = []
    for s in range(2):
        second_exchange.append((DIRS[s], r2_s.at[s], r2_r.at[1 - s], s, 1 - s))
        second_exchange.append((DIRS[2 + s], c2_s, c2_r.at[1 - s], 2 + s, 3 - s))
    for s in range(4):
        second_exchange.append(
            (DIRS[4 + s], r2_s.at[s // 2, pl.ds(0, 8)], k2_r.at[3 - s], 4 + s, 7 - s)
        )

    def start(exchange, sends, recvs):
        for (dr, dc), src, dst, a, b in exchange:

            @pl.when(there(dr, dc))
            def _(dr=dr, dc=dc, src=src, dst=dst, a=a, b=b):
                remote(src, dst, sends.at[a], recvs.at[b], dr, dc).start()

    def wait_recv(exchange, sends, recvs):
        for (dr, dc), src, dst, a, b in exchange:

            @pl.when(there(-dr, -dc))
            def _(dr=dr, dc=dc, src=src, dst=dst, a=a, b=b):
                remote(src, dst, sends.at[a], recvs.at[b], -dr, -dc).wait_recv()

    def wait_send(exchange, sends, recvs):
        for (dr, dc), src, dst, a, b in exchange:

            @pl.when(there(dr, dc))
            def _(dr=dr, dc=dc, src=src, dst=dst, a=a, b=b):
                remote(src, dst, sends.at[a], recvs.at[b], dr, dc).wait_send()

    start(row_exchange, send_sem, recv_sem)

    def prepare_more(n, carry):
        prepare(pl.multiple_of(n * 8, 8))
        return carry

    lax.fori_loop(1, ROWS // 8 - 1, prepare_more, 0, unroll=2)

    tile = pl.ds(M0, ROWS)
    for (ref, tiers), packed in zip(nodes, strips):
        packed[pl.ds(Q0, ROWS), :] = pack_edges(
            [(ref[t, 0, tile, :], ref[t, 3, tile, :]) for t in range(tiers)]
        )
    t_edges = pack_edges([(t_raw[t], t_raw[t]) for t in range(4)])
    for s, first in ((0, 0), (1, ROWS - 4)):
        for k, packed in enumerate(strips):
            rb_s[s, pl.ds(4 * k, 4), :] = packed[pl.ds(Q0 + first, 4), :]
        cell = 0 if s == 0 else 28
        rb_s[s, pl.ds(16, 4), :] = t_edges[cell : cell + 4]
        for t in range(4):
            rb_s[s, pl.ds(24 + 4 * t, 4), :] = t_raw[t, pl.ds(cell, 4), :]
    group = lane32((64, 128)) // 4
    for s, lane0 in ((0, 20), (1, 8)):
        mixed = jnp.zeros((64, 128), F32)
        for k, packed in enumerate(strips):
            for h in range(2):
                slot32 = h * 16 + k * 4
                part = packed[pl.ds(Q0 + 64 * h, 64), :]
                if slot32 != lane0:
                    part = pltpu.roll(part, (slot32 - lane0) % 128, 1)
                mixed = jnp.where(group == slot32 // 4, part, mixed)
        cm_s[s, pl.ds(0, 64), :] = mixed
        cm_s[s, pl.ds(64, 32), :] = t_edges
    start(first_exchange, send_sem, recv_sem)

    for ref, _ in nodes:
        ref[:, :, pl.ds(S0 + 4, 8), :] = ref[:, :, pl.ds(M0, 8), :]
        ref[:, :, pl.ds(S0 + 12, 8), :] = ref[:, :, pl.ds(M0 + ROWS - 8, 8), :]

    big = Domain(Tile, g, j, v, inv, (x, x1, x2, x3), (d, d1), (wa, wb, wc), power)
    side = Domain(
        Strip, qg, qj, qv, qi, (qx, qx1, qx2, qx3), (qd, qd1), (qa, qb, qc), qpower
    )
    solve(ROWS // 8, MAIN_UNROLL, (big, M0, 0, 8))

    wait_recv(row_exchange, send_sem, recv_sem)
    wait_recv(first_exchange, send_sem, recv_sem)

    for s, first in ((0, 0), (1, 20)):
        for k, (ref, tiers) in enumerate(nodes):
            for h in range(2):
                ref[:, pl.ds(2 * h, 2), pl.ds(S0 + first, 4), :] = ra_r[
                    s, pl.ds(4 * k, tiers), :, pl.ds(4 * h, 4), :
                ]
    strip = pl.ds(S0, 24)
    wa[:, :, strip, :] = g[:, :, strip, :] * x[:, :, strip, :]

    l32 = lane32((64, 128))
    for k, packed in enumerate(strips):
        for s, first in ((0, Q0 - 4), (1, Q0 + ROWS)):
            part = pl.ds(4 * k, 4)
            packed[pl.ds(first, 4), :] = with_sides(
                rb_r[s, part, :], cr_r[2 * s, part, :], cr_r[2 * s + 1, part, :]
            )
        for h in range(2):
            rows = pl.ds(Q0 + 64 * h, 64)
            slot32 = h * 16 + k * 4
            mid = packed[rows, :]
            for s, lane0 in ((0, 16), (1, 12)):
                part = cm_r[s, pl.ds(0, 64), :]
                if slot32 != lane0:
                    part = pltpu.roll(part, (lane0 - slot32) % 128, 1)
                mid = jnp.where((l32 >= lane0) & (l32 < lane0 + 4), part, mid)
            packed[rows, :] = mid
    strip = pl.ds(8, 144)
    qa[strip, :] = qg[strip, :] * qx[strip, :]
    solve(3, STRIP_UNROLL, (big, S0, ROWS, 8), (side, 8, 8, 48))

    power[:, :, pl.ds(0, 4), :] = power[:, :, pl.ds(ROWS + 4, 4), :]
    power[:, :, pl.ds(ROWS - 4, 4), :] = power[:, :, pl.ds(ROWS + 16, 4), :]

    sums = power[:, :, pl.ds(0, 32, 4), :]
    edge_sums = qpower[pl.ds(Q0, 32, 4), :]
    for k in range(1, 4):
        sums = sums + power[:, :, pl.ds(k, 32, 4), :]
        edge_sums = edge_sums + qpower[pl.ds(Q0 + k, 32, 4), :]
    total = jnp.zeros((128, 128), F32)
    for h in range(2):
        node, cell = iota((256, 128), 0), iota((256, 128), 1)
        pick = (node // 4 + 64 * h == cell) & (cell > 0) & (cell < 127)
        both = jnp.concatenate(
            [sums[:, 2 * h].reshape(128, 128), sums[:, 2 * h + 1].reshape(128, 128)], axis=1
        )
        total = total + dot3(both, one_zero(pick))
    lane, cell = iota((128, 512), 0), iota((128, 512), 1)
    base = (cell // 128) * 32
    pick = ((cell % 128 == 0) & (lane >= base) & (lane < base + 4)) | (
        (cell % 128 == 127) & ((lane - base + 12) % 128 < 4)
    )
    edge_cells = dot3(edge_sums, one_zero(pick))
    for t in range(4):
        load[t] = GAIN * (
            total[32 * t : 32 * (t + 1)] + edge_cells[:, 128 * t : 128 * (t + 1)]
        )

    l_edges = pack_edges([(load[t], load[t]) for t in range(4)])
    c2_s[...] = l_edges
    for s, cell in ((0, 0), (1, 28)):
        r2_s[s, pl.ds(0, 4), :] = l_edges[cell : cell + 4]
        for t in range(4):
            r2_s[s, pl.ds(8 + 4 * t, 4), :] = load[t, pl.ds(cell, 4), :]
    start(second_exchange, send2_sem, recv2_sem)

    x3[:, :, pl.ds(M0, 4), :] = x3[:, :, pl.ds(S0 + 4, 4), :]
    x3[:, :, pl.ds(M0 + ROWS - 4, 4), :] = x3[:, :, pl.ds(S0 + 16, 4), :]
    lane = iota((ROWS, 128), 1)
    for t, ends in enumerate(unpack_edges(qx3[pl.ds(Q0, ROWS), :], 4)):
        x3[t, 0, tile, :] = jnp.where(lane < 4, ends, x3[t, 0, tile, :])
        x3[t, 3, tile, :] = jnp.where(lane >= 124, ends, x3[t, 3, tile, :])

    for t in range(4):
        tt[t, pl.ds(0, 4), :] = rb_r[0, pl.ds(24 + 4 * t, 4), :]
        tt[t, pl.ds(4, 32), :] = t_raw[t]
        tt[t, pl.ds(36, 4), :] = rb_r[1, pl.ds(24 + 4 * t, 4), :]
    cells = pl.ds(64, 32)
    edge = pl.ds(16, 4)
    ht[pl.ds(0, 4), :] = with_sides(rb_r[0, edge, :], cr_r[0, edge, :], cr_r[1, edge, :])
    ht[pl.ds(4, 32), :] = with_sides(t_edges, cm_r[0, cells, :], cm_r[1, cells, :])
    ht[pl.ds(36, 4), :] = with_sides(rb_r[1, edge, :], cr_r[2, edge, :], cr_r[3, edge, :])
    heat_of = Heat(n_row, n_col, ts, tu, hs, hu)
    theta, side = tt[...], ht[...]
    tt[...] = theta + DT * heat_of.tile(theta)
    ht[...] = side + DT * heat_of.strip(side)

    wait_recv(second_exchange, send2_sem, recv2_sem)
    for t in range(4):
        tl[t, pl.ds(0, 4), :] = r2_r[0, pl.ds(8 + 4 * t, 4), :]
        tl[t, pl.ds(4, 32), :] = load[t]
        tl[t, pl.ds(36, 4), :] = r2_r[1, pl.ds(8 + 4 * t, 4), :]
    edge = pl.ds(0, 4)
    hl[pl.ds(0, 4), :] = with_sides(r2_r[0, edge, :], k2_r[0, edge, :], k2_r[1, edge, :])
    hl[pl.ds(4, 32), :] = with_sides(l_edges, c2_r[0], c2_r[1])
    hl[pl.ds(36, 4), :] = with_sides(r2_r[1, edge, :], k2_r[2, edge, :], k2_r[3, edge, :])

    wait_send(row_exchange, send_sem, recv_sem)
    wait_send(first_exchange, send_sem, recv_sem)
    wait_send(second_exchange, send2_sem, recv2_sem)


class Heat:
    def __init__(self, n_row, n_col, ts, tu, hs, hu):
        row, col = lax.axis_index("row"), lax.axis_index("col")
        self.refs = (ts, tu, hs, hu)
        r, l32 = iota((40, 128), 0), lane32((40, 128))
        rows_in = ((r >= 4) | (row > 0)) & ((r < 36) | (row < n_row - 1))
        cols_in = ((l32 < 16) | (l32 >= 20) | (col > 0)) & (
            (l32 < 12) | (l32 >= 16) | (col < n_col - 1)
        )
        tier = ((iota((40, 128), 1) + 20) // 32) % 4
        real = lambda mask: jnp.where(mask, 1.0, 0.0).astype(F32)
        self.row_mask, self.all_mask = real(rows_in), real(rows_in & cols_in)
        self.not_first, self.not_last = real(tier > 0), real(tier < 3)

    @staticmethod
    def flux(theta, s, u, s_ref, u_ref, rows, axis):
        def near(ref, mid):
            around = ref[rows(7)] + ref[rows(9)]
            return around + pltpu.roll(mid, 1, axis) + pltpu.roll(mid, 127, axis)

        s_ref[rows(8)] = s
        u_ref[rows(8)] = u
        return s * (near(u_ref, u) - theta * near(s_ref, s))

    def tile(self, theta):
        s = jnp.exp(-0.15 * theta) * self.row_mask
        rows = lambda k: (slice(None), pl.ds(k, 40), slice(None))
        flux = self.flux(theta, s, s * theta, *self.refs[:2], rows, 2)
        vert = jnp.concatenate(
            [
                theta[1:2] - theta[0:1],
                theta[0:2] + theta[2:4] - 2.0 * theta[1:3],
                theta[2:3] - 2.0 * theta[3:4],
            ],
            axis=0,
        )
        return flux + vert

    def strip(self, theta):
        s = jnp.exp(-0.15 * theta) * self.all_mask
        rows = lambda k: (pl.ds(k, 40), slice(None))
        flux = self.flux(theta, s, s * theta, *self.refs[2:], rows, 1)
        vert = (
            self.not_last * pltpu.roll(theta, 96, 1)
            + self.not_first * pltpu.roll(theta, 32, 1)
            - (1.0 + self.not_first) * theta
        )
        return flux + vert


def finish(
    n_row, n_col, x3, tt, ht, tl, hl, xo_h, to_h, ts, tu, hs, hu, t_out, out_sem
):
    copies = []
    for b in range(4):
        copy = pltpu.make_async_copy(
            x3.at[:, b, pl.ds(M0, ROWS), :], xo_h.at[:, :, pl.ds(128 * b, 128)], out_sem.at[b]
        )
        copy.start()
        copies.append(copy)
    for ref in (ts, tu):
        for start in (0, 48):
            ref[:, pl.ds(start, 8), :] = jnp.zeros((4, 8, 128), F32)
    for ref in (hs, hu):
        for start in (0, 48):
            ref[pl.ds(start, 8), :] = jnp.zeros((8, 128), F32)
    heat_of = Heat(n_row, n_col, ts, tu, hs, hu)
    heat, side_heat = tl[...], hl[...]
    theta, side = tt[...] + DT * heat, ht[...] + DT * side_heat
    for _ in range(HEAT_SWEEPS - 1):
        gain, side_gain = heat_of.tile(theta), heat_of.strip(side)
        theta = theta + DT * (gain + heat)
        side = side + DT * (side_gain + side_heat)
    lane = iota((32, 128), 1)
    for t, ends in enumerate(unpack_edges(side[4:36], 4)):
        t_out[t] = jnp.where((lane < 4) | (lane >= 124), ends, theta[t, 4:36])
    copy = pltpu.make_async_copy(t_out, to_h, out_sem.at[4])
    copy.start()
    copies.append(copy)
    for copy in copies:
        copy.wait()


def vmem(*shape, dtype=F32):
    return pltpu.VMEM(shape, dtype)


def on_device(n_row, n_col, *args):
    node = (4, 4, R_ALL, 128)
    raw = (4, 4, ROWS, 128)
    strip = (Q_ALL, 128)
    heat = [vmem(4, 56, 128), vmem(4, 56, 128), vmem(56, 128), vmem(56, 128)]
    scratch = [
        *[vmem(*node) for _ in range(5)], vmem(3, *node[1:]),
        *[vmem(*node) for _ in range(6)],
        vmem(4, 4, ROWS + 24, 128),
        vmem(*raw), vmem(*raw), vmem(3, *raw[1:], dtype=jnp.int32),
        vmem(*raw, dtype=jnp.int32), vmem(*raw), vmem(4, 32, 128),
        *[vmem(*strip) for _ in range(14)],
        vmem(2, 15, 2, 8, 128), vmem(2, 15, 2, 8, 128),
        vmem(2, 40, 128), vmem(2, 40, 128),
        vmem(2, 96, 128), vmem(2, 96, 128),
        vmem(4, 24, 128),
        vmem(4, 32, 128),
        vmem(2, 24, 128), vmem(2, 24, 128),
        vmem(32, 128), vmem(2, 32, 128),
        vmem(4, 8, 128),
        *heat,
        pltpu.SemaphoreType.DMA((21,)),
        pltpu.SemaphoreType.DMA((10,)),
        pltpu.SemaphoreType.DMA((10,)),
        pltpu.SemaphoreType.DMA((8,)),
        pltpu.SemaphoreType.DMA((8,)),
    ]
    hbm = pl.BlockSpec(memory_space=pltpu.HBM)
    local = pl.BlockSpec(memory_space=pltpu.VMEM)
    mids = pl.pallas_call(
        functools.partial(kernel, n_row, n_col),
        out_shape=tuple(
            pltpu.VMEM(shape, F32)
            for shape in (node, (4, 40, 128), (40, 128), (4, 40, 128), (40, 128))
        ),
        in_specs=[hbm] * 6,
        out_specs=(local,) * 5,
        scratch_shapes=scratch,
        compiler_params=pltpu.CompilerParams(
            collective_id=0,
            has_side_effects=True,
            vmem_limit_bytes=56 * 1024 * 1024,
            flags=KERNEL_FLAGS,
        ),
    )(*[pltpu.with_memory_space_constraint(arg, pltpu.HBM) for arg in args])
    return pl.pallas_call(
        functools.partial(finish, n_row, n_col),
        out_shape=(
            jax.ShapeDtypeStruct((4, ROWS, 512), F32),
            jax.ShapeDtypeStruct((4, 32, 128), F32),
        ),
        in_specs=[local] * 5,
        out_specs=(hbm, hbm),
        scratch_shapes=[*heat, vmem(4, 32, 128), pltpu.SemaphoreType.DMA((5,))],
        compiler_params=pltpu.CompilerParams(vmem_limit_bytes=4 * 1024 * 1024),
    )(*mids)


def solution(mesh):
    spec = P(None, "row", "col")
    return jax.shard_map(
        functools.partial(on_device, mesh.shape["row"], mesh.shape["col"]),
        mesh=mesh,
        in_specs=(spec,) * 6,
        out_specs=(spec, spec),
        check_vma=False,
    )
```

```python
import functools

import jax
import jax.numpy as jnp
from jax import lax
from jax.experimental import pallas as pl
from jax.experimental.pallas import tpu as pltpu
from jax.sharding import PartitionSpec as P

F32 = jnp.float32
BF16 = jnp.bfloat16
MESH = pl.DeviceIdType.MESH

LEAK = 0.2
HALF = 0.95
SIGMA = 1.0 / HALF
RHO0 = 1.0 / SIGMA
RHO1 = 1.0 / (2.0 * SIGMA - RHO0)
RHO2 = 1.0 / (2.0 * SIGMA - RHO1)
STEP_1 = (RHO1 * RHO0, 2.0 * RHO1 / HALF)
STEP_2 = (RHO2 * RHO1, 2.0 * RHO2 / HALF)
HEAT_SWEEPS = 4
DT = 0.12
GAIN = 0.0625
MAIN_UNROLL = 4
STRIP_UNROLL = 3

ROWS = 128
M0 = 8
S0 = 144
R_ALL = 176
Q0 = 16
Q_ALL = 160

DIRS = ((-1, 0), (1, 0), (0, -1), (0, 1), (-1, -1), (-1, 1), (1, -1), (1, 1))


def iota(shape, dim):
    return lax.broadcasted_iota(jnp.int32, shape, dim)


def split3(x):
    high = x.astype(BF16)
    rest = x - high.astype(F32)
    mid = rest.astype(BF16)
    low = (rest - mid.astype(F32)).astype(BF16)
    return jnp.concatenate([high, mid, low], axis=0)


def dot3(x, ones):
    rows = x.shape[0]
    y = jnp.dot(split3(x), ones, preferred_element_type=F32)
    return y[:rows] + y[rows : 2 * rows] + y[2 * rows :]


def one_zero(mask):
    return jnp.where(mask, 1.0, 0.0).astype(BF16)


class Tile:
    tiers = range(4)

    @staticmethod
    def part(ref, t, row, size):
        return ref[t, :, pl.ds(row, size), :]

    @staticmethod
    def put(ref, t, row, size, value):
        ref[t, :, pl.ds(row, size), :] = value

    @staticmethod
    def slot(ref, k, t):
        return ref[k, t]

    @staticmethod
    def put_slot(ref, k, t, value):
        ref[k, t] = value

    @staticmethod
    def left(x):
        lane = iota(x.shape, 2)
        y = pltpu.roll(x, 1, 2)
        return jnp.where(lane == 0, jnp.concatenate([y[3:], y[:3]], axis=0), y)

    @staticmethod
    def right(x):
        lane = iota(x.shape, 2)
        y = pltpu.roll(x, 127, 2)
        return jnp.where(lane == 127, jnp.concatenate([y[1:], y[:1]], axis=0), y)

    @staticmethod
    def vertical(read, v, x, t):
        if t == 0:
            return read(v, 0) * read(x, 1)
        if t == 3:
            return read(v, 2) * read(x, 2)
        return read(v, t) * read(x, t + 1) + read(v, t - 1) * read(x, t - 1)

    @staticmethod
    def via_sum(read, v, t):
        if t == 0:
            return read(v, 0)
        if t == 3:
            return read(v, 2)
        return read(v, t) + read(v, t - 1)

    @staticmethod
    def drops(read, v, x, t):
        total = None
        for low in (t - 1, t):
            if 0 <= low < 3:
                e = read(x, low) - read(x, low + 1)
                e = read(v, low) * (e * e)
                total = e if total is None else total + e
        return total


class Strip:
    tiers = (0,)

    @staticmethod
    def part(ref, t, row, size):
        return ref[pl.ds(row, size), :]

    @staticmethod
    def put(ref, t, row, size, value):
        ref[pl.ds(row, size), :] = value

    @staticmethod
    def slot(ref, k, t):
        return ref[k]

    @staticmethod
    def put_slot(ref, k, t, value):
        ref[k] = value

    @staticmethod
    def left(x):
        return pltpu.roll(x, 1, 1)

    @staticmethod
    def right(x):
        return pltpu.roll(x, 127, 1)

    @staticmethod
    def vertical(read, v, x, t):
        vm, xm = read(v, t), read(x, t)
        return vm * pltpu.roll(xm, 96, 1) + pltpu.roll(vm * xm, 32, 1)

    @staticmethod
    def via_sum(read, v, t):
        vm = read(v, t)
        return vm + pltpu.roll(vm, 32, 1)

    @staticmethod
    def drops(read, v, x, t):
        xm = read(x, t)
        e = xm - pltpu.roll(xm, 96, 1)
        e = read(v, t) * (e * e)
        return e + pltpu.roll(e, 32, 1)


class Domain:
    def __init__(self, kind, g, j, v, inv, gr, slots, x, w, power):
        self.kind, self.g, self.j, self.v, self.inv = kind, g, j, v, inv
        self.lr, self.lg, self.lw = slots
        self.gr, self.x, self.w, self.power = gr, x, w, power

    def lateral(self, p, row, size, slot):
        kind = self.kind
        for t in kind.tiers:
            if p == 3:
                x = kind.part(self.x[3], t, row, size)
                kind.put_slot(self.lw, slot, t, kind.right(x))
                continue
            w = kind.part(self.w[p], t, row, size)
            kind.put_slot(self.lw, slot, t, kind.left(w) + kind.right(w))
            if p == 0:
                g = kind.part(self.g, t, row, size)
                right = kind.right(g)
                kind.put_slot(self.lr, slot, t, right)
                kind.put_slot(self.lg, slot, t, kind.left(g) + right)

    def sweep(self, p, row, size, slot):
        kind, g, v = self.kind, self.g, self.v
        x, w = self.x[min(p, 3)], self.w
        for t in kind.tiers:
            read = lambda ref, t=t, k=0: kind.part(ref, t, row + k, size)
            put = lambda ref, value, t=t: kind.put(ref, t, row, size, value)
            gm, xm = read(g, t), read(x, t)
            if p == 3:
                right = xm - kind.slot(self.lw, slot, t)
                put(self.power[1], gm * (read(self.gr, t) * (right * right)))
                down = xm - read(x, t, 1)
                e = gm * (read(g, t, 1) * (down * down))
                put(self.power[2], e)
                node = (LEAK * xm) * xm + 0.5 * kind.drops(read, v, x, t)
                put(self.power[0], node + e)
                continue
            near = read(w[p], t, -1) + read(w[p], t, 1) + kind.slot(self.lw, slot, t)
            near = read(self.j, t) + gm * near + kind.vertical(read, v, x, t)
            if p == 0:
                near_g = read(g, t, -1) + read(g, t, 1) + kind.slot(self.lg, slot, t)
                inv = 1.0 / ((LEAK + gm * near_g) + kind.via_sum(read, v, t))
                new = inv * near
                put(self.inv, inv)
                put(self.gr, kind.slot(self.lr, slot, t))
            else:
                a, b = STEP_1 if p == 1 else STEP_2
                new = (1.0 + a - b) * xm - a * read(self.x[p - 1], t)
                new = new + b * (read(self.inv, t) * near)
            put(self.x[p + 1], new)
            if p < 2:
                put(w[p + 1], gm * new)


def solve(passes, steps, unroll, *parts):
    for p in passes:
        for domain, row, size in parts:
            domain.lateral(p, row, size, 0)

        def one(n, carry):
            for k in range(unroll):
                for domain, row, size in parts:
                    now = row + k * size
                    if steps > unroll:
                        now = now + pl.multiple_of(n * (unroll * size), unroll * size)
                    domain.sweep(p, now, size, k)
                    if steps > unroll or k + 1 < unroll:
                        domain.lateral(p, now + size, size, (k + 1) % unroll)
            return carry

        if steps > unroll:
            lax.fori_loop(0, steps // unroll, one, 0)
        else:
            one(0, 0)


def lane32(shape):
    return (iota(shape, 1) + 20) % 32


def pack_edges(tiers):
    shape = tiers[0][0].shape
    group = ((iota(shape, 1) + 12) // 32) % 4
    out = jnp.zeros(shape, F32)
    for t, (first, last) in enumerate(tiers):
        ends = first if first is last else jnp.where(iota(shape, 1) < 64, first, last)
        if t:
            ends = pltpu.roll(ends, 32 * t, 1)
        out = jnp.where(group == t, ends, out)
    return jnp.where(lane32(shape) >= 16, out, pltpu.roll(out, 120, 1))


def unpack_edges(packed, tiers):
    ends = jnp.where(lane32(packed.shape) >= 20, packed, pltpu.roll(packed, 8, 1))
    return [pltpu.roll(ends, (-32 * t) % 128, 1) if t else ends for t in range(tiers)]


def with_sides(mid, from_left, from_right):
    l32 = lane32(mid.shape)
    mid = jnp.where((l32 >= 16) & (l32 < 20), pltpu.roll(from_left, 8, 1), mid)
    return jnp.where((l32 >= 12) & (l32 < 16), pltpu.roll(from_right, 120, 1), mid)


def kernel(
    n_row, n_col,
    v_h, a_h, t_h, vi_h, fe_h, in_h,
    x3, tt, ht, tl, hl,
    x, x1, x2, g, j, v, inv, gr, lr, lg, lw, wa, wb, wc, p0, p1, p2,
    expand, x_raw, a_raw, vi_raw, fe_raw, in_raw, t_raw,
    qx, qx1, qx2, qx3, qg, qj, qv, qi, qgr, qlr, qlg, qlw, qa, qb, qc, q0, q1, q2,
    ra_s, ra_r, rb_s, rb_r, cm_s, cm_r, cr_r,
    load, r2_s, r2_r, c2_s, c2_r, k2_r, ts, tu, hs, hu, pick, pick_ends,
    in_sem, send_sem, recv_sem, send2_sem, recv2_sem,
):
    row = lax.axis_index("row")
    col = lax.axis_index("col")

    def there(dr, dc):
        ok = None
        for cond in (
            (row > 0) if dr < 0 else (row < n_row - 1) if dr > 0 else None,
            (col > 0) if dc < 0 else (col < n_col - 1) if dc > 0 else None,
        ):
            if cond is not None:
                ok = cond if ok is None else jnp.logical_and(ok, cond)
        return ok

    def device(dr, dc):
        return {"row": row + dr, "col": col + dc}

    barrier = pltpu.get_barrier_semaphore()
    for dr, dc in DIRS:

        @pl.when(there(dr, dc))
        def _(dr=dr, dc=dc):
            pl.semaphore_signal(
                barrier, inc=1, device_id=device(dr, dc), device_id_type=MESH
            )

    copies = {}
    slot = 0

    def fetch(name, src, dst):
        nonlocal slot
        copy = pltpu.make_async_copy(src, dst, in_sem.at[slot])
        slot += 1
        copy.start()
        copies.setdefault(name, []).append(copy)

    fetch("t", t_h, t_raw)
    inputs = ((a_h, a_raw), (v_h, x_raw), (fe_h, fe_raw), (in_h, in_raw), (vi_h, vi_raw))
    for name, first, size in (
        ("outer", 0, 8),
        ("outer", ROWS - 8, 8),
        ("inner", 8, ROWS - 16),
    ):
        for src, dst in inputs:
            rows = pl.ds(first, size)
            fetch(name, src.at[:, rows, :], dst.at[:, rows, :])

    def arrived(*names):
        for name in names:
            for copy in copies[name]:
                copy.wait()

    for ref in (x3, g, wa, wb, wc):
        for start in (0, M0 + ROWS, S0 + 24):
            ref[:, :, pl.ds(start, 8), :] = jnp.zeros((4, 4, 8, 128), F32)
    for ref in (qx, qx3, qg, qj, qv, qa, qb, qc):
        for start in (0, Q0 + ROWS):
            ref[pl.ds(start, 16), :] = jnp.zeros((16, 128), F32)
    for ref in (ts, tu):
        for start in (0, 48):
            ref[:, pl.ds(start, 8), :] = jnp.zeros((4, 8, 128), F32)
    for ref in (hs, hu):
        for start in (0, 48):
            ref[pl.ds(start, 8), :] = jnp.zeros((8, 128), F32)
    for s in range(2):
        rb_s[s, pl.ds(16, 8), :] = jnp.zeros((8, 128), F32)
        r2_s[s, pl.ds(0, 8), :] = jnp.zeros((8, 128), F32)

        @pl.when(jnp.logical_not(there(*DIRS[s])))
        def _(s=s):
            ra_r[s] = jnp.zeros((15, 2, 8, 128), F32)
            rb_r[s] = jnp.zeros((40, 128), F32)
            r2_r[s] = jnp.zeros((24, 128), F32)

        @pl.when(jnp.logical_not(there(*DIRS[2 + s])))
        def _(s=s):
            cm_r[s] = jnp.zeros((96, 128), F32)
            c2_r[s] = jnp.zeros((32, 128), F32)

    for s in range(4):

        @pl.when(jnp.logical_not(there(*DIRS[4 + s])))
        def _(s=s):
            cr_r[s] = jnp.zeros((24, 128), F32)
            k2_r[s] = jnp.zeros((8, 128), F32)

    node, cell = iota((256, 128), 0), iota((256, 128), 1)
    inner = (cell > 0) & (cell < 127)
    for h in range(2):
        own = inner & (node // 4 + 64 * h == cell)
        after = inner & (node // 4 + 64 * h + 1 == cell)
        last = node % 4 == 3
        pick[h, 0] = one_zero(own)
        pick[h, 1] = jnp.where(
            (own | after) & last, 0.5, jnp.where(own, 1.0, 0.0)
        ).astype(BF16)
    start_lane = jnp.where(cell % 32 == 0, cell, cell - 11)
    place = (node - start_lane + 1) % 128 - 1
    edge = (cell % 32 == 0) | (cell % 32 == 31)
    whole = edge & (place >= 0) & (place < 4)
    halved = edge & (node >= 128) & ((place == -1) | (place == 3))
    pick_ends[...] = jnp.where(halved, 0.5, jnp.where(whole, 1.0, 0.0)).astype(BF16)

    arrived("t")
    cells = jnp.exp(-0.25 * t_raw[...]).reshape(128, 128)
    wide = iota((128, 512), 1) // 4 == iota((128, 512), 0)
    fine = dot3(cells, one_zero(wide))
    for b in range(4):
        part = fine[:, 128 * b : 128 * (b + 1)].reshape(4, 32, 128)
        for k in range(4):
            expand[:, b, pl.ds(k, 32, 4), :] = part

    arrived("outer")

    def prepare(off):
        raw, rows = pl.ds(off, 8), pl.ds(M0 + off, 8)
        for t in range(4):
            for b in range(4):
                lanes = slice(128 * b, 128 * (b + 1))
                adm, old = a_raw[t, raw, lanes], x_raw[t, raw, lanes]
                gm = adm * lax.rsqrt(adm) * expand[t, b, raw, :]
                g[t, b, rows, :] = gm
                x[t, b, rows, :] = old
                wa[t, b, rows, :] = gm * old
                j[t, b, rows, :] = fe_raw[t, raw, lanes].astype(F32) * in_raw[t, raw, lanes]
                if t < 3:
                    v[t, b, rows, :] = vi_raw[t, raw, lanes].astype(F32)

    def remote(src, dst, send, recv, dr, dc):
        return pltpu.make_async_remote_copy(
            src_ref=src,
            dst_ref=dst,
            send_sem=send,
            recv_sem=recv,
            device_id=device(dr, dc),
            device_id_type=MESH,
        )

    nodes = ((x, 4), (g, 4), (j, 4), (v, 3))
    strips = (qx, qg, qj, qv)

    prepare(0)
    prepare(ROWS - 8)
    for s, first in ((0, 0), (1, ROWS - 4)):
        for k, (ref, tiers) in enumerate(nodes):
            for h in range(2):
                ra_s[s, pl.ds(4 * k, tiers), :, pl.ds(4 * h, 4), :] = ref[
                    :, pl.ds(2 * h, 2), pl.ds(M0 + first, 4), :
                ]

    neighbours = 0
    for dr, dc in DIRS:
        neighbours = neighbours + there(dr, dc).astype(jnp.int32)
    pl.semaphore_wait(barrier, neighbours)

    row_exchange, first_exchange = [], []
    for s in range(2):
        row_exchange.append((DIRS[s], ra_s.at[s], ra_r.at[1 - s], s, 1 - s))
        first_exchange.append((DIRS[s], rb_s.at[s], rb_r.at[1 - s], 2 + s, 3 - s))
    for s in range(4):
        first_exchange.append(
            (DIRS[4 + s], rb_s.at[s // 2, pl.ds(0, 24)], cr_r.at[3 - s], 6 + s, 9 - s)
        )
    for s in range(2):
        first_exchange.append((DIRS[2 + s], cm_s.at[s], cm_r.at[1 - s], 4 + s, 5 - s))
    second_exchange = []
    for s in range(2):
        second_exchange.append((DIRS[s], r2_s.at[s], r2_r.at[1 - s], s, 1 - s))
        second_exchange.append((DIRS[2 + s], c2_s, c2_r.at[1 - s], 2 + s, 3 - s))
    for s in range(4):
        second_exchange.append(
            (DIRS[4 + s], r2_s.at[s // 2, pl.ds(0, 8)], k2_r.at[3 - s], 4 + s, 7 - s)
        )

    def start(exchange, sends, recvs):
        for (dr, dc), src, dst, a, b in exchange:

            @pl.when(there(dr, dc))
            def _(dr=dr, dc=dc, src=src, dst=dst, a=a, b=b):
                remote(src, dst, sends.at[a], recvs.at[b], dr, dc).start()

    def wait_recv(exchange, sends, recvs):
        for (dr, dc), src, dst, a, b in exchange:

            @pl.when(there(-dr, -dc))
            def _(dr=dr, dc=dc, src=src, dst=dst, a=a, b=b):
                remote(src, dst, sends.at[a], recvs.at[b], -dr, -dc).wait_recv()

    def wait_send(exchange, sends, recvs):
        for (dr, dc), src, dst, a, b in exchange:

            @pl.when(there(dr, dc))
            def _(dr=dr, dc=dc, src=src, dst=dst, a=a, b=b):
                remote(src, dst, sends.at[a], recvs.at[b], dr, dc).wait_send()

    start(row_exchange, send_sem, recv_sem)
    arrived("inner")

    def prepare_more(n, carry):
        prepare(pl.multiple_of(n * 8, 8))
        return carry

    lax.fori_loop(1, ROWS // 8 - 1, prepare_more, 0, unroll=2)

    tile = pl.ds(M0, ROWS)
    for (ref, tiers), packed in zip(nodes, strips):
        packed[pl.ds(Q0, ROWS), :] = pack_edges(
            [(ref[t, 0, tile, :], ref[t, 3, tile, :]) for t in range(tiers)]
        )
    t_edges = pack_edges([(t_raw[t], t_raw[t]) for t in range(4)])
    for s, first in ((0, 0), (1, ROWS - 4)):
        for k, packed in enumerate(strips):
            rb_s[s, pl.ds(4 * k, 4), :] = packed[pl.ds(Q0 + first, 4), :]
        cell = 0 if s == 0 else 28
        rb_s[s, pl.ds(16, 4), :] = t_edges[cell : cell + 4]
        for t in range(4):
            rb_s[s, pl.ds(24 + 4 * t, 4), :] = t_raw[t, pl.ds(cell, 4), :]
    group = lane32((64, 128)) // 4
    for s, lane0 in ((0, 20), (1, 8)):
        mixed = jnp.zeros((64, 128), F32)
        for k, packed in enumerate(strips):
            for h in range(2):
                slot32 = h * 16 + k * 4
                part = packed[pl.ds(Q0 + 64 * h, 64), :]
                if slot32 != lane0:
                    part = pltpu.roll(part, (slot32 - lane0) % 128, 1)
                mixed = jnp.where(group == slot32 // 4, part, mixed)
        cm_s[s, pl.ds(0, 64), :] = mixed
        cm_s[s, pl.ds(64, 32), :] = t_edges
    start(first_exchange, send_sem, recv_sem)

    for ref, _ in nodes:
        ref[:, :, pl.ds(S0 + 4, 8), :] = ref[:, :, pl.ds(M0, 8), :]
        ref[:, :, pl.ds(S0 + 12, 8), :] = ref[:, :, pl.ds(M0 + ROWS - 8, 8), :]

    big = Domain(
        Tile, g, j, v, inv, gr, (lr, lg, lw), (x, x1, x2, x3), (wa, wb, wc), (p0, p1, p2)
    )
    side = Domain(
        Strip, qg, qj, qv, qi, qgr, (qlr, qlg, qlw),
        (qx, qx1, qx2, qx3), (qa, qb, qc), (q0, q1, q2),
    )
    solve(range(4), ROWS // 8, MAIN_UNROLL, (big, M0, 8))

    wait_recv(row_exchange, send_sem, recv_sem)
    wait_recv(first_exchange, send_sem, recv_sem)

    for s, first in ((0, 0), (1, 20)):
        for k, (ref, tiers) in enumerate(nodes):
            for h in range(2):
                ref[:, pl.ds(2 * h, 2), pl.ds(S0 + first, 4), :] = ra_r[
                    s, pl.ds(4 * k, tiers), :, pl.ds(4 * h, 4), :
                ]
    strip = pl.ds(S0, 24)
    wa[:, :, strip, :] = g[:, :, strip, :] * x[:, :, strip, :]

    l32 = lane32((64, 128))
    for k, packed in enumerate(strips):
        for s, first in ((0, Q0 - 4), (1, Q0 + ROWS)):
            part = pl.ds(4 * k, 4)
            packed[pl.ds(first, 4), :] = with_sides(
                rb_r[s, part, :], cr_r[2 * s, part, :], cr_r[2 * s + 1, part, :]
            )
        for h in range(2):
            rows = pl.ds(Q0 + 64 * h, 64)
            slot32 = h * 16 + k * 4
            mid = packed[rows, :]
            for s, lane0 in ((0, 16), (1, 12)):
                part = cm_r[s, pl.ds(0, 64), :]
                if slot32 != lane0:
                    part = pltpu.roll(part, (lane0 - slot32) % 128, 1)
                mid = jnp.where((l32 >= lane0) & (l32 < lane0 + 4), part, mid)
            packed[rows, :] = mid
    strip = pl.ds(8, 144)
    qa[strip, :] = qg[strip, :] * qx[strip, :]
    solve(range(4), 3, STRIP_UNROLL, (big, S0, 8), (side, 8, 48))

    for ref, before in ((p0, 0), (p1, 0), (p2, 1)):
        ref[:, :, pl.ds(M0 - before, 4 + before), :] = ref[
            :, :, pl.ds(S0 + 4 - before, 4 + before), :
        ]
        ref[:, :, pl.ds(M0 + ROWS - 4, 4), :] = ref[:, :, pl.ds(S0 + 16, 4), :]

    def cell_rows(parts, first):
        take = lambda ref, k: ref[
            (slice(None),) * (len(ref.shape) - 2) + (pl.ds(first + k, 32, 4), slice(None))
        ]
        total = 0.5 * (take(parts[2], -1) - take(parts[2], 3))
        right = take(parts[1], 0)
        for k in range(4):
            total = total + take(parts[0], k)
            if k:
                right = right + take(parts[1], k)
        return total, right

    sums, rights = cell_rows(big.power, M0)
    edge_sums, edge_rights = cell_rows(side.power, Q0)
    total = jnp.zeros((128, 128), F32)
    for h in range(2):
        for k, values in enumerate((sums, rights)):
            both = jnp.concatenate(
                [values[:, 2 * h].reshape(128, 128), values[:, 2 * h + 1].reshape(128, 128)],
                axis=1,
            )
            total = total + dot3(both, pick[h, k])
    ends = dot3(jnp.concatenate([edge_sums, edge_rights], axis=1), pick_ends[...])
    lane = iota((32, 128), 1)
    for t in range(4):
        mine = pltpu.roll(ends, (-32 * t) % 128, 1) if t else ends
        mine = jnp.where((lane == 0) | (lane == 127), mine, total[32 * t : 32 * (t + 1)])
        load[t] = GAIN * mine

    l_edges = pack_edges([(load[t], load[t]) for t in range(4)])
    c2_s[...] = l_edges
    for s, cell in ((0, 0), (1, 28)):
        r2_s[s, pl.ds(0, 4), :] = l_edges[cell : cell + 4]
        for t in range(4):
            r2_s[s, pl.ds(8 + 4 * t, 4), :] = load[t, pl.ds(cell, 4), :]
    start(second_exchange, send2_sem, recv2_sem)

    x3[:, :, pl.ds(M0, 4), :] = x3[:, :, pl.ds(S0 + 4, 4), :]
    x3[:, :, pl.ds(M0 + ROWS - 4, 4), :] = x3[:, :, pl.ds(S0 + 16, 4), :]
    lane = iota((ROWS, 128), 1)
    for t, ends in enumerate(unpack_edges(qx3[pl.ds(Q0, ROWS), :], 4)):
        x3[t, 0, tile, :] = jnp.where(lane < 4, ends, x3[t, 0, tile, :])
        x3[t, 3, tile, :] = jnp.where(lane >= 124, ends, x3[t, 3, tile, :])

    for t in range(4):
        tt[t, pl.ds(0, 4), :] = rb_r[0, pl.ds(24 + 4 * t, 4), :]
        tt[t, pl.ds(4, 32), :] = t_raw[t]
        tt[t, pl.ds(36, 4), :] = rb_r[1, pl.ds(24 + 4 * t, 4), :]
    cells = pl.ds(64, 32)
    edge = pl.ds(16, 4)
    ht[pl.ds(0, 4), :] = with_sides(rb_r[0, edge, :], cr_r[0, edge, :], cr_r[1, edge, :])
    ht[pl.ds(4, 32), :] = with_sides(t_edges, cm_r[0, cells, :], cm_r[1, cells, :])
    ht[pl.ds(36, 4), :] = with_sides(rb_r[1, edge, :], cr_r[2, edge, :], cr_r[3, edge, :])
    heat_of = Heat(n_row, n_col, ts, tu, hs, hu)
    theta, side = tt[...], ht[...]
    tt[...] = theta + DT * heat_of.tile(theta)
    ht[...] = side + DT * heat_of.strip(side)

    wait_recv(second_exchange, send2_sem, recv2_sem)
    for t in range(4):
        tl[t, pl.ds(0, 4), :] = r2_r[0, pl.ds(8 + 4 * t, 4), :]
        tl[t, pl.ds(4, 32), :] = load[t]
        tl[t, pl.ds(36, 4), :] = r2_r[1, pl.ds(8 + 4 * t, 4), :]
    edge = pl.ds(0, 4)
    hl[pl.ds(0, 4), :] = with_sides(r2_r[0, edge, :], k2_r[0, edge, :], k2_r[1, edge, :])
    hl[pl.ds(4, 32), :] = with_sides(l_edges, c2_r[0], c2_r[1])
    hl[pl.ds(36, 4), :] = with_sides(r2_r[1, edge, :], k2_r[2, edge, :], k2_r[3, edge, :])

    wait_send(row_exchange, send_sem, recv_sem)
    wait_send(first_exchange, send_sem, recv_sem)
    wait_send(second_exchange, send2_sem, recv2_sem)


class Heat:
    def __init__(self, n_row, n_col, ts, tu, hs, hu):
        row, col = lax.axis_index("row"), lax.axis_index("col")
        self.refs = (ts, tu, hs, hu)
        r, l32 = iota((40, 128), 0), lane32((40, 128))
        rows_in = ((r >= 4) | (row > 0)) & ((r < 36) | (row < n_row - 1))
        cols_in = ((l32 < 16) | (l32 >= 20) | (col > 0)) & (
            (l32 < 12) | (l32 >= 16) | (col < n_col - 1)
        )
        tier = ((iota((40, 128), 1) + 20) // 32) % 4
        real = lambda mask: jnp.where(mask, 1.0, 0.0).astype(F32)
        self.row_mask, self.all_mask = real(rows_in), real(rows_in & cols_in)
        self.not_first, self.not_last = real(tier > 0), real(tier < 3)

    @staticmethod
    def flux(theta, s, u, s_ref, u_ref, rows, axis):
        def near(ref, mid):
            around = ref[rows(7)] + ref[rows(9)]
            return around + pltpu.roll(mid, 1, axis) + pltpu.roll(mid, 127, axis)

        s_ref[rows(8)] = s
        u_ref[rows(8)] = u
        return s * (near(u_ref, u) - theta * near(s_ref, s))

    def tile(self, theta):
        s = jnp.exp(-0.15 * theta) * self.row_mask
        rows = lambda k: (slice(None), pl.ds(k, 40), slice(None))
        flux = self.flux(theta, s, s * theta, *self.refs[:2], rows, 2)
        vert = jnp.concatenate(
            [
                theta[1:2] - theta[0:1],
                theta[0:2] + theta[2:4] - 2.0 * theta[1:3],
                theta[2:3] - 2.0 * theta[3:4],
            ],
            axis=0,
        )
        return flux + vert

    def strip(self, theta):
        s = jnp.exp(-0.15 * theta) * self.all_mask
        rows = lambda k: (pl.ds(k, 40), slice(None))
        flux = self.flux(theta, s, s * theta, *self.refs[2:], rows, 1)
        vert = (
            self.not_last * pltpu.roll(theta, 96, 1)
            + self.not_first * pltpu.roll(theta, 32, 1)
            - (1.0 + self.not_first) * theta
        )
        return flux + vert


def finish(
    n_row, n_col, x3, tt, ht, tl, hl, xo_h, to_h, ts, tu, hs, hu, t_out, out_sem
):
    copies = []
    for b in range(4):
        copy = pltpu.make_async_copy(
            x3.at[:, b, pl.ds(M0, ROWS), :], xo_h.at[:, :, pl.ds(128 * b, 128)], out_sem.at[b]
        )
        copy.start()
        copies.append(copy)
    for ref in (ts, tu):
        for start in (0, 48):
            ref[:, pl.ds(start, 8), :] = jnp.zeros((4, 8, 128), F32)
    for ref in (hs, hu):
        for start in (0, 48):
            ref[pl.ds(start, 8), :] = jnp.zeros((8, 128), F32)
    heat_of = Heat(n_row, n_col, ts, tu, hs, hu)
    heat, side_heat = tl[...], hl[...]
    theta, side = tt[...] + DT * heat, ht[...] + DT * side_heat
    for _ in range(HEAT_SWEEPS - 1):
        gain, side_gain = heat_of.tile(theta), heat_of.strip(side)
        theta = theta + DT * (gain + heat)
        side = side + DT * (side_gain + side_heat)
    lane = iota((32, 128), 1)
    for t, ends in enumerate(unpack_edges(side[4:36], 4)):
        t_out[t] = jnp.where((lane < 4) | (lane >= 124), ends, theta[t, 4:36])
    copy = pltpu.make_async_copy(t_out, to_h, out_sem.at[4])
    copy.start()
    copies.append(copy)
    for copy in copies:
        copy.wait()


def vmem(*shape, dtype=F32):
    return pltpu.VMEM(shape, dtype)


def on_device(n_row, n_col, *args):
    node = (4, 4, R_ALL, 128)
    raw = (4, ROWS, 512)
    strip = (Q_ALL, 128)
    heat = [vmem(4, 56, 128), vmem(4, 56, 128), vmem(56, 128), vmem(56, 128)]
    scratch = [
        *[vmem(*node) for _ in range(5)], vmem(3, *node[1:]),
        *[vmem(*node) for _ in range(2)],
        *[vmem(MAIN_UNROLL, 4, 4, 8, 128) for _ in range(3)],
        *[vmem(*node) for _ in range(6)],
        vmem(4, 4, ROWS, 128), vmem(*raw), vmem(*raw), vmem(3, *raw[1:], dtype=jnp.int32),
        vmem(*raw, dtype=jnp.int32), vmem(*raw), vmem(4, 32, 128),
        *[vmem(*strip) for _ in range(9)],
        *[vmem(STRIP_UNROLL, 48, 128) for _ in range(3)],
        *[vmem(*strip) for _ in range(6)],
        vmem(2, 15, 2, 8, 128), vmem(2, 15, 2, 8, 128),
        vmem(2, 40, 128), vmem(2, 40, 128),
        vmem(2, 96, 128), vmem(2, 96, 128),
        vmem(4, 24, 128),
        vmem(4, 32, 128),
        vmem(2, 24, 128), vmem(2, 24, 128),
        vmem(32, 128), vmem(2, 32, 128),
        vmem(4, 8, 128),
        *heat,
        vmem(2, 2, 256, 128, dtype=BF16), vmem(256, 128, dtype=BF16),
        pltpu.SemaphoreType.DMA((16,)),
        pltpu.SemaphoreType.DMA((10,)),
        pltpu.SemaphoreType.DMA((10,)),
        pltpu.SemaphoreType.DMA((8,)),
        pltpu.SemaphoreType.DMA((8,)),
    ]
    hbm = pl.BlockSpec(memory_space=pltpu.HBM)
    local = pl.BlockSpec(memory_space=pltpu.VMEM)
    mids = pl.pallas_call(
        functools.partial(kernel, n_row, n_col),
        out_shape=tuple(
            pltpu.VMEM(shape, F32)
            for shape in (node, (4, 40, 128), (40, 128), (4, 40, 128), (40, 128))
        ),
        in_specs=[hbm] * 6,
        out_specs=(local,) * 5,
        scratch_shapes=scratch,
        compiler_params=pltpu.CompilerParams(
            collective_id=0,
            has_side_effects=True,
            vmem_limit_bytes=56 * 1024 * 1024,
        ),
    )(*[pltpu.with_memory_space_constraint(arg, pltpu.HBM) for arg in args])
    return pl.pallas_call(
        functools.partial(finish, n_row, n_col),
        out_shape=(
            jax.ShapeDtypeStruct((4, ROWS, 512), F32),
            jax.ShapeDtypeStruct((4, 32, 128), F32),
        ),
        in_specs=[local] * 5,
        out_specs=(hbm, hbm),
        scratch_shapes=[*heat, vmem(4, 32, 128), pltpu.SemaphoreType.DMA((5,))],
        compiler_params=pltpu.CompilerParams(vmem_limit_bytes=4 * 1024 * 1024),
    )(*mids)


def solution(mesh):
    spec = P(None, "row", "col")
    return jax.shard_map(
        functools.partial(on_device, mesh.shape["row"], mesh.shape["col"]),
        mesh=mesh,
        in_specs=(spec,) * 6,
        out_specs=(spec, spec),
        check_vma=False,
    )
```

```python
import functools

import jax
import jax.numpy as jnp
from jax import lax
from jax.experimental import pallas as pl
from jax.experimental.pallas import tpu as pltpu
from jax.sharding import PartitionSpec as P

F32 = jnp.float32
BF16 = jnp.bfloat16
MESH = pl.DeviceIdType.MESH

LEAK = 0.2
HALF = 0.95
SIGMA = 1.0 / HALF
RHO0 = 1.0 / SIGMA
RHO1 = 1.0 / (2.0 * SIGMA - RHO0)
RHO2 = 1.0 / (2.0 * SIGMA - RHO1)
STEP_1 = (RHO1 * RHO0, 2.0 * RHO1 / HALF)
STEP_2 = (RHO2 * RHO1, 2.0 * RHO2 / HALF)
HEAT_SWEEPS = 4
DT = 0.12
GAIN = 0.0625
MAIN_UNROLL = 4
STRIP_UNROLL = 3
GROUPS = 4
GROUP = 32

ROWS = 128
M0 = 8
S0 = 144
R_ALL = 176
Q0 = 16
Q_ALL = 160

DIRS = ((-1, 0), (1, 0), (0, -1), (0, 1), (-1, -1), (-1, 1), (1, -1), (1, 1))


def iota(shape, dim):
    return lax.broadcasted_iota(jnp.int32, shape, dim)


def split3(x):
    high = x.astype(BF16)
    rest = x - high.astype(F32)
    mid = rest.astype(BF16)
    low = (rest - mid.astype(F32)).astype(BF16)
    return jnp.concatenate([high, mid, low], axis=0)


def dot3(x, ones):
    rows = x.shape[0]
    y = jnp.dot(split3(x), ones, preferred_element_type=F32)
    return y[:rows] + y[rows : 2 * rows] + y[2 * rows :]


def one_zero(mask):
    return jnp.where(mask, 1.0, 0.0).astype(BF16)


class Tile:
    tiers = range(4)

    @staticmethod
    def part(ref, t, row, size):
        return ref[t, :, pl.ds(row, size), :]

    @staticmethod
    def put(ref, t, row, size, value):
        ref[t, :, pl.ds(row, size), :] = value

    @staticmethod
    def slot(ref, k, t):
        return ref[k, t]

    @staticmethod
    def put_slot(ref, k, t, value):
        ref[k, t] = value

    @staticmethod
    def left(x):
        lane = iota(x.shape, 2)
        y = pltpu.roll(x, 1, 2)
        return jnp.where(lane == 0, jnp.concatenate([y[3:], y[:3]], axis=0), y)

    @staticmethod
    def right(x):
        lane = iota(x.shape, 2)
        y = pltpu.roll(x, 127, 2)
        return jnp.where(lane == 127, jnp.concatenate([y[1:], y[:1]], axis=0), y)

    @staticmethod
    def vertical(read, v, x, t):
        if t == 0:
            return read(v, 0) * read(x, 1)
        if t == 3:
            return read(v, 2) * read(x, 2)
        return read(v, t) * read(x, t + 1) + read(v, t - 1) * read(x, t - 1)

    @staticmethod
    def via_sum(read, v, t):
        if t == 0:
            return read(v, 0)
        if t == 3:
            return read(v, 2)
        return read(v, t) + read(v, t - 1)

    @staticmethod
    def drops(read, v, x, t):
        total = None
        for low in (t - 1, t):
            if 0 <= low < 3:
                e = read(x, low) - read(x, low + 1)
                e = read(v, low) * (e * e)
                total = e if total is None else total + e
        return total


class Strip:
    tiers = (0,)

    @staticmethod
    def part(ref, t, row, size):
        return ref[pl.ds(row, size), :]

    @staticmethod
    def put(ref, t, row, size, value):
        ref[pl.ds(row, size), :] = value

    @staticmethod
    def slot(ref, k, t):
        return ref[k]

    @staticmethod
    def put_slot(ref, k, t, value):
        ref[k] = value

    @staticmethod
    def left(x):
        return pltpu.roll(x, 1, 1)

    @staticmethod
    def right(x):
        return pltpu.roll(x, 127, 1)

    @staticmethod
    def vertical(read, v, x, t):
        vm, xm = read(v, t), read(x, t)
        return vm * pltpu.roll(xm, 96, 1) + pltpu.roll(vm * xm, 32, 1)

    @staticmethod
    def via_sum(read, v, t):
        vm = read(v, t)
        return vm + pltpu.roll(vm, 32, 1)

    @staticmethod
    def drops(read, v, x, t):
        xm = read(x, t)
        e = xm - pltpu.roll(xm, 96, 1)
        e = read(v, t) * (e * e)
        return e + pltpu.roll(e, 32, 1)


class Domain:
    def __init__(self, kind, g, j, v, inv, gr, slots, x, w, power):
        self.kind, self.g, self.j, self.v, self.inv = kind, g, j, v, inv
        self.lr, self.lg, self.lw = slots
        self.gr, self.x, self.w, self.power = gr, x, w, power

    def lateral(self, p, row, size, slot):
        kind = self.kind
        for t in kind.tiers:
            if p == 3:
                x = kind.part(self.x[3], t, row, size)
                kind.put_slot(self.lw, slot, t, kind.right(x))
                continue
            w = kind.part(self.w[p], t, row, size)
            kind.put_slot(self.lw, slot, t, kind.left(w) + kind.right(w))
            if p == 0:
                g = kind.part(self.g, t, row, size)
                right = kind.right(g)
                kind.put_slot(self.lr, slot, t, right)
                kind.put_slot(self.lg, slot, t, kind.left(g) + right)

    def sweep(self, p, row, size, slot):
        kind, g, v = self.kind, self.g, self.v
        x, w = self.x[min(p, 3)], self.w
        for t in kind.tiers:
            read = lambda ref, t=t, k=0: kind.part(ref, t, row + k, size)
            put = lambda ref, value, t=t: kind.put(ref, t, row, size, value)
            gm, xm = read(g, t), read(x, t)
            if p == 3:
                right = xm - kind.slot(self.lw, slot, t)
                put(self.power[1], gm * (read(self.gr, t) * (right * right)))
                down = xm - read(x, t, 1)
                e = gm * (read(g, t, 1) * (down * down))
                put(self.power[2], e)
                node = (LEAK * xm) * xm + 0.5 * kind.drops(read, v, x, t)
                put(self.power[0], node + e)
                continue
            near = read(w[p], t, -1) + read(w[p], t, 1) + kind.slot(self.lw, slot, t)
            near = read(self.j, t) + gm * near + kind.vertical(read, v, x, t)
            if p == 0:
                near_g = read(g, t, -1) + read(g, t, 1) + kind.slot(self.lg, slot, t)
                inv = 1.0 / ((LEAK + gm * near_g) + kind.via_sum(read, v, t))
                new = inv * near
                put(self.inv, inv)
                put(self.gr, kind.slot(self.lr, slot, t))
            else:
                a, b = STEP_1 if p == 1 else STEP_2
                new = (1.0 + a - b) * xm - a * read(self.x[p - 1], t)
                new = new + b * (read(self.inv, t) * near)
            put(self.x[p + 1], new)
            if p < 2:
                put(w[p + 1], gm * new)


def solve(passes, steps, unroll, *parts):
    for p in passes:
        for domain, row, size in parts:
            domain.lateral(p, row, size, 0)

        def one(n, carry):
            for k in range(unroll):
                for domain, row, size in parts:
                    now = row + k * size
                    if steps > unroll:
                        now = now + pl.multiple_of(n * (unroll * size), unroll * size)
                    domain.sweep(p, now, size, k)
                    if steps > unroll or k + 1 < unroll:
                        domain.lateral(p, now + size, size, (k + 1) % unroll)
            return carry

        if steps > unroll:
            lax.fori_loop(0, steps // unroll, one, 0)
        else:
            one(0, 0)


def lane32(shape):
    return (iota(shape, 1) + 20) % 32


def pack_edges(tiers):
    shape = tiers[0][0].shape
    group = ((iota(shape, 1) + 12) // 32) % 4
    out = jnp.zeros(shape, F32)
    for t, (first, last) in enumerate(tiers):
        ends = first if first is last else jnp.where(iota(shape, 1) < 64, first, last)
        if t:
            ends = pltpu.roll(ends, 32 * t, 1)
        out = jnp.where(group == t, ends, out)
    return jnp.where(lane32(shape) >= 16, out, pltpu.roll(out, 120, 1))


def unpack_edges(packed, tiers):
    ends = jnp.where(lane32(packed.shape) >= 20, packed, pltpu.roll(packed, 8, 1))
    return [pltpu.roll(ends, (-32 * t) % 128, 1) if t else ends for t in range(tiers)]


def squeeze(edges, lane0):
    slot = lane32((8, 128)) // 4
    out = jnp.zeros((8, 128), F32)
    for q in range(4):
        part = edges[8 * q : 8 * q + 8]
        if 4 * q != lane0:
            part = pltpu.roll(part, (4 * q - lane0) % 128, 1)
        out = jnp.where(slot == q, part, out)
    return out


def with_squeezed_sides(mid, from_left, from_right):
    l32 = lane32((8, 128))
    rows = []
    for q in range(4):
        part = mid[8 * q : 8 * q + 8]
        for lane0, side in ((16, from_left), (12, from_right)):
            if 4 * q != lane0:
                side = pltpu.roll(side, (lane0 - 4 * q) % 128, 1)
            part = jnp.where((l32 >= lane0) & (l32 < lane0 + 4), side, part)
        rows.append(part)
    return jnp.concatenate(rows, axis=0)


def with_sides(mid, from_left, from_right):
    l32 = lane32(mid.shape)
    mid = jnp.where((l32 >= 16) & (l32 < 20), pltpu.roll(from_left, 8, 1), mid)
    return jnp.where((l32 >= 12) & (l32 < 16), pltpu.roll(from_right, 120, 1), mid)


def kernel(
    n_row, n_col,
    v_h, a_h, t_h, vi_h, fe_h, in_h,
    x3, tt, ht, tl, hl,
    x, x1, x2, g, j, v, inv, gr, lr, lg, lw, wa, wb, wc, p0, p1, p2,
    expand, x_raw, a_raw, vi_raw, fe_raw, in_raw, t_raw,
    qx, qx1, qx2, qx3, qg, qj, qv, qi, qgr, qlr, qlg, qlw, qa, qb, qc, q0, q1, q2,
    ra_s, ra_r, rb_s, rb_r, cm_s, cm_r, cr_r,
    load, r2_s, r2_r, c2_s, c2_r, k2_s, k2_r, ts, tu, hs, hu, pick, pick_ends,
    in_sem, send_sem, recv_sem, send2_sem, recv2_sem,
):
    row = lax.axis_index("row")
    col = lax.axis_index("col")

    def there(dr, dc):
        ok = None
        for cond in (
            (row > 0) if dr < 0 else (row < n_row - 1) if dr > 0 else None,
            (col > 0) if dc < 0 else (col < n_col - 1) if dc > 0 else None,
        ):
            if cond is not None:
                ok = cond if ok is None else jnp.logical_and(ok, cond)
        return ok

    def device(dr, dc):
        return {"row": row + dr, "col": col + dc}

    barrier = pltpu.get_barrier_semaphore()
    for dr, dc in DIRS:

        @pl.when(there(dr, dc))
        def _(dr=dr, dc=dc):
            pl.semaphore_signal(
                barrier, inc=1, device_id=device(dr, dc), device_id_type=MESH
            )

    copies = {}
    slot = 0

    def fetch(name, src, dst):
        nonlocal slot
        copy = pltpu.make_async_copy(src, dst, in_sem.at[slot])
        slot += 1
        copy.start()
        copies.setdefault(name, []).append(copy)

    fetch("t", t_h, t_raw)
    inputs = ((a_h, a_raw), (v_h, x_raw), (fe_h, fe_raw), (in_h, in_raw), (vi_h, vi_raw))
    for n in range(GROUPS):
        for src, dst in inputs:
            rows = pl.ds(n * GROUP, GROUP)
            fetch(n, src.at[:, rows, :], dst.at[:, rows, :])

    def arrived(*names):
        for name in names:
            for copy in copies[name]:
                copy.wait()

    for ref in (x3, g, wa, wb, wc):
        for start in (0, M0 + ROWS, S0 + 24):
            ref[:, :, pl.ds(start, 8), :] = jnp.zeros((4, 4, 8, 128), F32)
    for ref in (qx, qx3, qg, qj, qv, qa, qb, qc):
        for start in (0, Q0 + ROWS):
            ref[pl.ds(start, 16), :] = jnp.zeros((16, 128), F32)
    for ref in (ts, tu):
        for start in (0, 48):
            ref[:, pl.ds(start, 8), :] = jnp.zeros((4, 8, 128), F32)
    for ref in (hs, hu):
        for start in (0, 48):
            ref[pl.ds(start, 8), :] = jnp.zeros((8, 128), F32)
    for s in range(2):
        rb_s[s, pl.ds(16, 8), :] = jnp.zeros((8, 128), F32)
        k2_s[s] = jnp.zeros((8, 128), F32)

        @pl.when(jnp.logical_not(there(*DIRS[s])))
        def _(s=s):
            ra_r[s] = jnp.zeros((15, 2, 8, 128), F32)
            rb_r[s] = jnp.zeros((40, 128), F32)
            r2_r[s] = jnp.zeros((16, 128), F32)

        @pl.when(jnp.logical_not(there(*DIRS[2 + s])))
        def _(s=s):
            cm_r[s] = jnp.zeros((72, 128), F32)
            c2_r[s] = jnp.zeros((8, 128), F32)

    for s in range(4):

        @pl.when(jnp.logical_not(there(*DIRS[4 + s])))
        def _(s=s):
            cr_r[s] = jnp.zeros((24, 128), F32)
            k2_r[s] = jnp.zeros((8, 128), F32)

    node, cell = iota((256, 128), 0), iota((256, 128), 1)
    inner = (cell > 0) & (cell < 127)
    for h in range(2):
        own = inner & (node // 4 + 64 * h == cell)
        after = inner & (node // 4 + 64 * h + 1 == cell)
        last = node % 4 == 3
        pick[h, 0] = one_zero(own)
        pick[h, 1] = jnp.where(
            (own | after) & last, 0.5, jnp.where(own, 1.0, 0.0)
        ).astype(BF16)
    start_lane = jnp.where(cell % 32 == 0, cell, cell - 11)
    place = (node - start_lane + 1) % 128 - 1
    edge = (cell % 32 == 0) | (cell % 32 == 31)
    whole = edge & (place >= 0) & (place < 4)
    halved = edge & (node >= 128) & ((place == -1) | (place == 3))
    pick_ends[...] = jnp.where(halved, 0.5, jnp.where(whole, 1.0, 0.0)).astype(BF16)

    arrived("t")
    cells = jnp.exp(-0.25 * t_raw[...]).reshape(128, 128)
    wide = iota((128, 512), 1) // 4 == iota((128, 512), 0)
    fine = dot3(cells, one_zero(wide))
    for b in range(4):
        part = fine[:, 128 * b : 128 * (b + 1)].reshape(4, 32, 128)
        for k in range(4):
            expand[:, b, pl.ds(k, 32, 4), :] = part

    def prepare(off):
        raw, rows = pl.ds(off, 8), pl.ds(M0 + off, 8)
        for t in range(4):
            for b in range(4):
                lanes = slice(128 * b, 128 * (b + 1))
                adm, old = a_raw[t, raw, lanes], x_raw[t, raw, lanes]
                gm = adm * lax.rsqrt(adm) * expand[t, b, raw, :]
                g[t, b, rows, :] = gm
                x[t, b, rows, :] = old
                wa[t, b, rows, :] = gm * old
                j[t, b, rows, :] = fe_raw[t, raw, lanes].astype(F32) * in_raw[t, raw, lanes]
                if t < 3:
                    v[t, b, rows, :] = vi_raw[t, raw, lanes].astype(F32)

    def remote(src, dst, send, recv, dr, dc):
        return pltpu.make_async_remote_copy(
            src_ref=src,
            dst_ref=dst,
            send_sem=send,
            recv_sem=recv,
            device_id=device(dr, dc),
            device_id_type=MESH,
        )

    nodes = ((x, 4), (g, 4), (j, 4), (v, 3))
    strips = (qx, qg, qj, qv)

    for n in range(GROUPS):
        arrived(n)
        for off in range(n * GROUP, (n + 1) * GROUP, 8):
            prepare(off)
        tile = pl.ds(M0 + n * GROUP, GROUP)
        for (ref, tiers), packed in zip(nodes, strips):
            packed[pl.ds(Q0 + n * GROUP, GROUP), :] = pack_edges(
                [(ref[t, 0, tile, :], ref[t, 3, tile, :]) for t in range(tiers)]
            )
    tile = pl.ds(M0, ROWS)

    for s, first in ((0, 0), (1, ROWS - 4)):
        for k, (ref, tiers) in enumerate(nodes):
            for h in range(2):
                ra_s[s, pl.ds(4 * k, tiers), :, pl.ds(4 * h, 4), :] = ref[
                    :, pl.ds(2 * h, 2), pl.ds(M0 + first, 4), :
                ]
    t_edges = pack_edges([(t_raw[t], t_raw[t]) for t in range(4)])
    for s, first in ((0, 0), (1, ROWS - 4)):
        for k, packed in enumerate(strips):
            rb_s[s, pl.ds(4 * k, 4), :] = packed[pl.ds(Q0 + first, 4), :]
        cell = 0 if s == 0 else 28
        rb_s[s, pl.ds(16, 4), :] = t_edges[cell : cell + 4]
        for t in range(4):
            rb_s[s, pl.ds(24 + 4 * t, 4), :] = t_raw[t, pl.ds(cell, 4), :]
    group = lane32((64, 128)) // 4
    for s, lane0 in ((0, 20), (1, 8)):
        mixed = jnp.zeros((64, 128), F32)
        for k, packed in enumerate(strips):
            for h in range(2):
                slot32 = h * 16 + k * 4
                part = packed[pl.ds(Q0 + 64 * h, 64), :]
                if slot32 != lane0:
                    part = pltpu.roll(part, (slot32 - lane0) % 128, 1)
                mixed = jnp.where(group == slot32 // 4, part, mixed)
        cm_s[s, pl.ds(0, 64), :] = mixed
        cm_s[s, pl.ds(64, 8), :] = squeeze(t_edges, lane0)

    neighbours = 0
    for dr, dc in DIRS:
        neighbours = neighbours + there(dr, dc).astype(jnp.int32)
    pl.semaphore_wait(barrier, neighbours)

    row_exchange, first_exchange = [], []
    for s in range(2):
        row_exchange.append((DIRS[s], ra_s.at[s], ra_r.at[1 - s], s, 1 - s))
        first_exchange.append((DIRS[s], rb_s.at[s], rb_r.at[1 - s], 2 + s, 3 - s))
    for s in range(4):
        first_exchange.append(
            (DIRS[4 + s], rb_s.at[s // 2, pl.ds(0, 24)], cr_r.at[3 - s], 6 + s, 9 - s)
        )
    for s in range(2):
        first_exchange.append((DIRS[2 + s], cm_s.at[s], cm_r.at[1 - s], 4 + s, 5 - s))
    second_exchange = []
    for s in range(2):
        second_exchange.append((DIRS[s], r2_s.at[s], r2_r.at[1 - s], s, 1 - s))
        second_exchange.append((DIRS[2 + s], c2_s.at[s], c2_r.at[1 - s], 2 + s, 3 - s))
    for s in range(4):
        second_exchange.append(
            (DIRS[4 + s], k2_s.at[s // 2], k2_r.at[3 - s], 4 + s, 7 - s)
        )

    def start(exchange, sends, recvs):
        for (dr, dc), src, dst, a, b in exchange:

            @pl.when(there(dr, dc))
            def _(dr=dr, dc=dc, src=src, dst=dst, a=a, b=b):
                remote(src, dst, sends.at[a], recvs.at[b], dr, dc).start()

    def wait_recv(exchange, sends, recvs):
        for (dr, dc), src, dst, a, b in exchange:

            @pl.when(there(-dr, -dc))
            def _(dr=dr, dc=dc, src=src, dst=dst, a=a, b=b):
                remote(src, dst, sends.at[a], recvs.at[b], -dr, -dc).wait_recv()

    def wait_send(exchange, sends, recvs):
        for (dr, dc), src, dst, a, b in exchange:

            @pl.when(there(dr, dc))
            def _(dr=dr, dc=dc, src=src, dst=dst, a=a, b=b):
                remote(src, dst, sends.at[a], recvs.at[b], dr, dc).wait_send()

    start(first_exchange, send_sem, recv_sem)
    start(row_exchange, send_sem, recv_sem)

    for ref, _ in nodes:
        ref[:, :, pl.ds(S0 + 4, 8), :] = ref[:, :, pl.ds(M0, 8), :]
        ref[:, :, pl.ds(S0 + 12, 8), :] = ref[:, :, pl.ds(M0 + ROWS - 8, 8), :]

    big = Domain(
        Tile, g, j, v, inv, gr, (lr, lg, lw), (x, x1, x2, x3), (wa, wb, wc), (p0, p1, p2)
    )
    side = Domain(
        Strip, qg, qj, qv, qi, qgr, (qlr, qlg, qlw),
        (qx, qx1, qx2, qx3), (qa, qb, qc), (q0, q1, q2),
    )
    solve(range(4), ROWS // 8, MAIN_UNROLL, (big, M0, 8))

    wait_recv(row_exchange, send_sem, recv_sem)
    wait_recv(first_exchange, send_sem, recv_sem)

    for s, first in ((0, 0), (1, 20)):
        for k, (ref, tiers) in enumerate(nodes):
            for h in range(2):
                ref[:, pl.ds(2 * h, 2), pl.ds(S0 + first, 4), :] = ra_r[
                    s, pl.ds(4 * k, tiers), :, pl.ds(4 * h, 4), :
                ]
    strip = pl.ds(S0, 24)
    wa[:, :, strip, :] = g[:, :, strip, :] * x[:, :, strip, :]

    l32 = lane32((64, 128))
    for k, packed in enumerate(strips):
        for s, first in ((0, Q0 - 4), (1, Q0 + ROWS)):
            part = pl.ds(4 * k, 4)
            packed[pl.ds(first, 4), :] = with_sides(
                rb_r[s, part, :], cr_r[2 * s, part, :], cr_r[2 * s + 1, part, :]
            )
        for h in range(2):
            rows = pl.ds(Q0 + 64 * h, 64)
            slot32 = h * 16 + k * 4
            mid = packed[rows, :]
            for s, lane0 in ((0, 16), (1, 12)):
                part = cm_r[s, pl.ds(0, 64), :]
                if slot32 != lane0:
                    part = pltpu.roll(part, (lane0 - slot32) % 128, 1)
                mid = jnp.where((l32 >= lane0) & (l32 < lane0 + 4), part, mid)
            packed[rows, :] = mid
    strip = pl.ds(8, 144)
    qa[strip, :] = qg[strip, :] * qx[strip, :]
    solve(range(4), 3, STRIP_UNROLL, (big, S0, 8), (side, 8, 48))

    for ref, before in ((p0, 0), (p1, 0), (p2, 1)):
        ref[:, :, pl.ds(M0 - before, 4 + before), :] = ref[
            :, :, pl.ds(S0 + 4 - before, 4 + before), :
        ]
        ref[:, :, pl.ds(M0 + ROWS - 4, 4), :] = ref[:, :, pl.ds(S0 + 16, 4), :]

    def cell_rows(parts, first):
        take = lambda ref, k: ref[
            (slice(None),) * (len(ref.shape) - 2) + (pl.ds(first + k, 32, 4), slice(None))
        ]
        total = 0.5 * (take(parts[2], -1) - take(parts[2], 3))
        right = take(parts[1], 0)
        for k in range(4):
            total = total + take(parts[0], k)
            if k:
                right = right + take(parts[1], k)
        return total, right

    sums, rights = cell_rows(big.power, M0)
    edge_sums, edge_rights = cell_rows(side.power, Q0)
    total = jnp.zeros((128, 128), F32)
    for h in range(2):
        for k, values in enumerate((sums, rights)):
            both = jnp.concatenate(
                [values[:, 2 * h].reshape(128, 128), values[:, 2 * h + 1].reshape(128, 128)],
                axis=1,
            )
            total = total + dot3(both, pick[h, k])
    ends = dot3(jnp.concatenate([edge_sums, edge_rights], axis=1), pick_ends[...])
    lane = iota((32, 128), 1)
    for t in range(4):
        mine = pltpu.roll(ends, (-32 * t) % 128, 1) if t else ends
        mine = jnp.where((lane == 0) | (lane == 127), mine, total[32 * t : 32 * (t + 1)])
        load[t] = GAIN * mine

    l_edges = pack_edges([(load[t], load[t]) for t in range(4)])
    for s, (cell, lane0) in enumerate(((0, 20), (28, 8))):
        c2_s[s] = squeeze(l_edges, lane0)
        k2_s[s, pl.ds(0, 4), :] = l_edges[cell : cell + 4]
        for t in range(4):
            r2_s[s, pl.ds(4 * t, 4), :] = load[t, pl.ds(cell, 4), :]
        for t in range(3):
            own, free = (t, 3) if s == 0 else (29 + t, 0)
            r2_s[s, pl.ds(4 * t + free, 1), :] = l_edges[own : own + 1]
    start(second_exchange, send2_sem, recv2_sem)

    x3[:, :, pl.ds(M0, 4), :] = x3[:, :, pl.ds(S0 + 4, 4), :]
    x3[:, :, pl.ds(M0 + ROWS - 4, 4), :] = x3[:, :, pl.ds(S0 + 16, 4), :]
    lane = iota((ROWS, 128), 1)
    for t, ends in enumerate(unpack_edges(qx3[pl.ds(Q0, ROWS), :], 4)):
        x3[t, 0, tile, :] = jnp.where(lane < 4, ends, x3[t, 0, tile, :])
        x3[t, 3, tile, :] = jnp.where(lane >= 124, ends, x3[t, 3, tile, :])

    for t in range(4):
        tt[t, pl.ds(0, 4), :] = rb_r[0, pl.ds(24 + 4 * t, 4), :]
        tt[t, pl.ds(4, 32), :] = t_raw[t]
        tt[t, pl.ds(36, 4), :] = rb_r[1, pl.ds(24 + 4 * t, 4), :]
    cells = pl.ds(64, 8)
    edge = pl.ds(16, 4)
    ht[pl.ds(0, 4), :] = with_sides(rb_r[0, edge, :], cr_r[0, edge, :], cr_r[1, edge, :])
    ht[pl.ds(4, 32), :] = with_squeezed_sides(t_edges, cm_r[0, cells, :], cm_r[1, cells, :])
    ht[pl.ds(36, 4), :] = with_sides(rb_r[1, edge, :], cr_r[2, edge, :], cr_r[3, edge, :])
    heat_of = Heat(n_row, n_col, ts, tu, hs, hu)
    theta, side = tt[...], ht[...]
    tt[...] = theta + DT * heat_of.tile(theta)
    ht[...] = side + DT * heat_of.strip(side)

    wait_recv(second_exchange, send2_sem, recv2_sem)
    for t in range(4):
        tl[t, pl.ds(0, 4), :] = r2_r[0, pl.ds(4 * t, 4), :]
        tl[t, pl.ds(4, 32), :] = load[t]
        tl[t, pl.ds(36, 4), :] = r2_r[1, pl.ds(4 * t, 4), :]
    zero = jnp.zeros((1, 128), F32)
    above = [zero] + [r2_r[0, pl.ds(4 * t, 1), :] for t in range(3)]
    below = [r2_r[1, pl.ds(4 * t + 3, 1), :] for t in range(3)] + [zero]
    for first, corner, rows in ((0, 0, above), (36, 2, below)):
        hl[pl.ds(first, 4), :] = with_sides(
            jnp.concatenate(rows, axis=0),
            k2_r[corner, pl.ds(0, 4), :],
            k2_r[corner + 1, pl.ds(0, 4), :],
        )
    hl[pl.ds(4, 32), :] = with_squeezed_sides(l_edges, c2_r[0], c2_r[1])

    wait_send(row_exchange, send_sem, recv_sem)
    wait_send(first_exchange, send_sem, recv_sem)
    wait_send(second_exchange, send2_sem, recv2_sem)


class Heat:
    def __init__(self, n_row, n_col, ts, tu, hs, hu):
        row, col = lax.axis_index("row"), lax.axis_index("col")
        self.refs = (ts, tu, hs, hu)
        r, l32 = iota((40, 128), 0), lane32((40, 128))
        rows_in = ((r >= 4) | (row > 0)) & ((r < 36) | (row < n_row - 1))
        cols_in = ((l32 < 16) | (l32 >= 20) | (col > 0)) & (
            (l32 < 12) | (l32 >= 16) | (col < n_col - 1)
        )
        tier = ((iota((40, 128), 1) + 20) // 32) % 4
        real = lambda mask: jnp.where(mask, 1.0, 0.0).astype(F32)
        self.row_mask, self.all_mask = real(rows_in), real(rows_in & cols_in)
        self.not_first, self.not_last = real(tier > 0), real(tier < 3)

    @staticmethod
    def flux(theta, s, u, s_ref, u_ref, rows, axis):
        def near(ref, mid):
            around = ref[rows(7)] + ref[rows(9)]
            return around + pltpu.roll(mid, 1, axis) + pltpu.roll(mid, 127, axis)

        s_ref[rows(8)] = s
        u_ref[rows(8)] = u
        return s * (near(u_ref, u) - theta * near(s_ref, s))

    def tile(self, theta):
        s = jnp.exp(-0.15 * theta) * self.row_mask
        rows = lambda k: (slice(None), pl.ds(k, 40), slice(None))
        flux = self.flux(theta, s, s * theta, *self.refs[:2], rows, 2)
        vert = jnp.concatenate(
            [
                theta[1:2] - theta[0:1],
                theta[0:2] + theta[2:4] - 2.0 * theta[1:3],
                theta[2:3] - 2.0 * theta[3:4],
            ],
            axis=0,
        )
        return flux + vert

    def strip(self, theta):
        s = jnp.exp(-0.15 * theta) * self.all_mask
        rows = lambda k: (pl.ds(k, 40), slice(None))
        flux = self.flux(theta, s, s * theta, *self.refs[2:], rows, 1)
        vert = (
            self.not_last * pltpu.roll(theta, 96, 1)
            + self.not_first * pltpu.roll(theta, 32, 1)
            - (1.0 + self.not_first) * theta
        )
        return flux + vert


def finish(
    n_row, n_col, x3, tt, ht, tl, hl, xo_h, to_h, ts, tu, hs, hu, t_out, out_sem
):
    copies = []
    for b in range(4):
        copy = pltpu.make_async_copy(
            x3.at[:, b, pl.ds(M0, ROWS), :], xo_h.at[:, :, pl.ds(128 * b, 128)], out_sem.at[b]
        )
        copy.start()
        copies.append(copy)
    for ref in (ts, tu):
        for start in (0, 48):
            ref[:, pl.ds(start, 8), :] = jnp.zeros((4, 8, 128), F32)
    for ref in (hs, hu):
        for start in (0, 48):
            ref[pl.ds(start, 8), :] = jnp.zeros((8, 128), F32)
    heat_of = Heat(n_row, n_col, ts, tu, hs, hu)
    heat, side_heat = tl[...], hl[...]
    theta, side = tt[...] + DT * heat, ht[...] + DT * side_heat
    for _ in range(HEAT_SWEEPS - 1):
        gain, side_gain = heat_of.tile(theta), heat_of.strip(side)
        theta = theta + DT * (gain + heat)
        side = side + DT * (side_gain + side_heat)
    lane = iota((32, 128), 1)
    for t, ends in enumerate(unpack_edges(side[4:36], 4)):
        t_out[t] = jnp.where((lane < 4) | (lane >= 124), ends, theta[t, 4:36])
    copy = pltpu.make_async_copy(t_out, to_h, out_sem.at[4])
    copy.start()
    copies.append(copy)
    for copy in copies:
        copy.wait()


def vmem(*shape, dtype=F32):
    return pltpu.VMEM(shape, dtype)


def on_device(n_row, n_col, *args):
    node = (4, 4, R_ALL, 128)
    raw = (4, ROWS, 512)
    strip = (Q_ALL, 128)
    heat = [vmem(4, 56, 128), vmem(4, 56, 128), vmem(56, 128), vmem(56, 128)]
    scratch = [
        *[vmem(*node) for _ in range(5)], vmem(3, *node[1:]),
        *[vmem(*node) for _ in range(2)],
        *[vmem(MAIN_UNROLL, 4, 4, 8, 128) for _ in range(3)],
        *[vmem(*node) for _ in range(6)],
        vmem(4, 4, ROWS, 128), vmem(*raw), vmem(*raw), vmem(3, *raw[1:], dtype=jnp.int32),
        vmem(*raw, dtype=jnp.int32), vmem(*raw), vmem(4, 32, 128),
        *[vmem(*strip) for _ in range(9)],
        *[vmem(STRIP_UNROLL, 48, 128) for _ in range(3)],
        *[vmem(*strip) for _ in range(6)],
        vmem(2, 15, 2, 8, 128), vmem(2, 15, 2, 8, 128),
        vmem(2, 40, 128), vmem(2, 40, 128),
        vmem(2, 72, 128), vmem(2, 72, 128),
        vmem(4, 24, 128),
        vmem(4, 32, 128),
        vmem(2, 16, 128), vmem(2, 16, 128),
        vmem(2, 8, 128), vmem(2, 8, 128),
        vmem(2, 8, 128), vmem(4, 8, 128),
        *heat,
        vmem(2, 2, 256, 128, dtype=BF16), vmem(256, 128, dtype=BF16),
        pltpu.SemaphoreType.DMA((1 + 5 * GROUPS,)),
        pltpu.SemaphoreType.DMA((10,)),
        pltpu.SemaphoreType.DMA((10,)),
        pltpu.SemaphoreType.DMA((8,)),
        pltpu.SemaphoreType.DMA((8,)),
    ]
    hbm = pl.BlockSpec(memory_space=pltpu.HBM)
    local = pl.BlockSpec(memory_space=pltpu.VMEM)
    mids = pl.pallas_call(
        functools.partial(kernel, n_row, n_col),
        out_shape=tuple(
            pltpu.VMEM(shape, F32)
            for shape in (node, (4, 40, 128), (40, 128), (4, 40, 128), (40, 128))
        ),
        in_specs=[hbm] * 6,
        out_specs=(local,) * 5,
        scratch_shapes=scratch,
        compiler_params=pltpu.CompilerParams(
            collective_id=0,
            has_side_effects=True,
            vmem_limit_bytes=56 * 1024 * 1024,
        ),
    )(*[pltpu.with_memory_space_constraint(arg, pltpu.HBM) for arg in args])
    return pl.pallas_call(
        functools.partial(finish, n_row, n_col),
        out_shape=(
            jax.ShapeDtypeStruct((4, ROWS, 512), F32),
            jax.ShapeDtypeStruct((4, 32, 128), F32),
        ),
        in_specs=[local] * 5,
        out_specs=(hbm, hbm),
        scratch_shapes=[*heat, vmem(4, 32, 128), pltpu.SemaphoreType.DMA((5,))],
        compiler_params=pltpu.CompilerParams(vmem_limit_bytes=4 * 1024 * 1024),
    )(*mids)


def solution(mesh):
    spec = P(None, "row", "col")
    return jax.shard_map(
        functools.partial(on_device, mesh.shape["row"], mesh.shape["col"]),
        mesh=mesh,
        in_specs=(spec,) * 6,
        out_specs=(spec, spec),
        check_vma=False,
    )
```

```python
import functools

import jax
import jax.numpy as jnp
from jax import lax
from jax.experimental import pallas as pl
from jax.experimental.pallas import tpu as pltpu
from jax.sharding import PartitionSpec as P

F32 = jnp.float32
BF16 = jnp.bfloat16
MESH = pl.DeviceIdType.MESH

LEAK = 0.2
HALF = 0.95
SIGMA = 1.0 / HALF
RHO0 = 1.0 / SIGMA
RHO1 = 1.0 / (2.0 * SIGMA - RHO0)
RHO2 = 1.0 / (2.0 * SIGMA - RHO1)
STEP_1 = (RHO1 * RHO0, 2.0 * RHO1 / HALF)
STEP_2 = (RHO2 * RHO1, 2.0 * RHO2 / HALF)
HEAT_SWEEPS = 4
DT = 0.12
GAIN = 0.0625
MAIN_UNROLL = 4
STRIP_UNROLL = 3
GROUPS = 4
GROUP = 32
ORDER = (0, 3, 1, 2)

ROWS = 128
M0 = 8
S0 = 144
R_ALL = 176
Q0 = 16
Q_ALL = 160

DIRS = ((-1, 0), (1, 0), (0, -1), (0, 1), (-1, -1), (-1, 1), (1, -1), (1, 1))


def iota(shape, dim):
    return lax.broadcasted_iota(jnp.int32, shape, dim)


def split3(x):
    high = x.astype(BF16)
    rest = x - high.astype(F32)
    mid = rest.astype(BF16)
    low = (rest - mid.astype(F32)).astype(BF16)
    return jnp.concatenate([high, mid, low], axis=0)


def dot3(x, ones):
    rows = x.shape[0]
    y = jnp.dot(split3(x), ones, preferred_element_type=F32)
    return y[:rows] + y[rows : 2 * rows] + y[2 * rows :]


def one_zero(mask):
    return jnp.where(mask, 1.0, 0.0).astype(BF16)


class Tile:
    tiers = range(4)

    @staticmethod
    def part(ref, t, row, size):
        return ref[t, :, pl.ds(row, size), :]

    @staticmethod
    def put(ref, t, row, size, value):
        ref[t, :, pl.ds(row, size), :] = value

    @staticmethod
    def slot(ref, k, t):
        return ref[k, t]

    @staticmethod
    def put_slot(ref, k, t, value):
        ref[k, t] = value

    @staticmethod
    def left(x):
        lane = iota(x.shape, 2)
        y = pltpu.roll(x, 1, 2)
        return jnp.where(lane == 0, jnp.concatenate([y[3:], y[:3]], axis=0), y)

    @staticmethod
    def right(x):
        lane = iota(x.shape, 2)
        y = pltpu.roll(x, 127, 2)
        return jnp.where(lane == 127, jnp.concatenate([y[1:], y[:1]], axis=0), y)

    @staticmethod
    def vertical(read, v, x, t):
        if t == 0:
            return read(v, 0) * read(x, 1)
        if t == 3:
            return read(v, 2) * read(x, 2)
        return read(v, t) * read(x, t + 1) + read(v, t - 1) * read(x, t - 1)

    @staticmethod
    def via_sum(read, v, t):
        if t == 0:
            return read(v, 0)
        if t == 3:
            return read(v, 2)
        return read(v, t) + read(v, t - 1)

    @staticmethod
    def drops(read, v, x, t):
        total = None
        for low in (t - 1, t):
            if 0 <= low < 3:
                e = read(x, low) - read(x, low + 1)
                e = read(v, low) * (e * e)
                total = e if total is None else total + e
        return total


class Strip:
    tiers = (0,)

    @staticmethod
    def part(ref, t, row, size):
        return ref[pl.ds(row, size), :]

    @staticmethod
    def put(ref, t, row, size, value):
        ref[pl.ds(row, size), :] = value

    @staticmethod
    def slot(ref, k, t):
        return ref[k]

    @staticmethod
    def put_slot(ref, k, t, value):
        ref[k] = value

    @staticmethod
    def left(x):
        return pltpu.roll(x, 1, 1)

    @staticmethod
    def right(x):
        return pltpu.roll(x, 127, 1)

    @staticmethod
    def vertical(read, v, x, t):
        vm, xm = read(v, t), read(x, t)
        return vm * pltpu.roll(xm, 96, 1) + pltpu.roll(vm * xm, 32, 1)

    @staticmethod
    def via_sum(read, v, t):
        vm = read(v, t)
        return vm + pltpu.roll(vm, 32, 1)

    @staticmethod
    def drops(read, v, x, t):
        xm = read(x, t)
        e = xm - pltpu.roll(xm, 96, 1)
        e = read(v, t) * (e * e)
        return e + pltpu.roll(e, 32, 1)


class Domain:
    def __init__(self, kind, g, j, v, inv, gr, slots, x, w, power):
        self.kind, self.g, self.j, self.v, self.inv = kind, g, j, v, inv
        self.lr, self.lg, self.lw = slots
        self.gr, self.x, self.w, self.power = gr, x, w, power

    def lateral(self, p, row, size, slot):
        kind = self.kind
        for t in kind.tiers:
            if p == 3:
                x = kind.part(self.x[3], t, row, size)
                kind.put_slot(self.lw, slot, t, kind.right(x))
                continue
            w = kind.part(self.w[p], t, row, size)
            kind.put_slot(self.lw, slot, t, kind.left(w) + kind.right(w))
            if p == 0:
                g = kind.part(self.g, t, row, size)
                right = kind.right(g)
                kind.put_slot(self.lr, slot, t, right)
                kind.put_slot(self.lg, slot, t, kind.left(g) + right)

    def sweep(self, p, row, size, slot):
        kind, g, v = self.kind, self.g, self.v
        x, w = self.x[min(p, 3)], self.w
        for t in kind.tiers:
            read = lambda ref, t=t, k=0: kind.part(ref, t, row + k, size)
            put = lambda ref, value, t=t: kind.put(ref, t, row, size, value)
            gm, xm = read(g, t), read(x, t)
            if p == 3:
                right = xm - kind.slot(self.lw, slot, t)
                put(self.power[1], gm * (read(self.gr, t) * (right * right)))
                down = xm - read(x, t, 1)
                e = gm * (read(g, t, 1) * (down * down))
                put(self.power[2], e)
                node = (LEAK * xm) * xm + 0.5 * kind.drops(read, v, x, t)
                put(self.power[0], node + e)
                continue
            near = read(w[p], t, -1) + read(w[p], t, 1) + kind.slot(self.lw, slot, t)
            near = read(self.j, t) + gm * near + kind.vertical(read, v, x, t)
            if p == 0:
                near_g = read(g, t, -1) + read(g, t, 1) + kind.slot(self.lg, slot, t)
                inv = 1.0 / ((LEAK + gm * near_g) + kind.via_sum(read, v, t))
                new = inv * near
                put(self.inv, inv)
                put(self.gr, kind.slot(self.lr, slot, t))
            else:
                a, b = STEP_1 if p == 1 else STEP_2
                new = (1.0 + a - b) * xm - a * read(self.x[p - 1], t)
                new = new + b * (read(self.inv, t) * near)
            put(self.x[p + 1], new)
            if p < 2:
                put(w[p + 1], gm * new)


def solve(passes, steps, unroll, *parts):
    for p in passes:
        for domain, row, size in parts:
            domain.lateral(p, row, size, 0)

        def one(n, carry):
            for k in range(unroll):
                for domain, row, size in parts:
                    now = row + k * size
                    if steps > unroll:
                        now = now + pl.multiple_of(n * (unroll * size), unroll * size)
                    domain.sweep(p, now, size, k)
                    if steps > unroll or k + 1 < unroll:
                        domain.lateral(p, now + size, size, (k + 1) % unroll)
            return carry

        if steps > unroll:
            lax.fori_loop(0, steps // unroll, one, 0)
        else:
            one(0, 0)


def lane32(shape):
    return (iota(shape, 1) + 20) % 32


def pack_edges(tiers):
    shape = tiers[0][0].shape
    group = ((iota(shape, 1) + 12) // 32) % 4
    out = jnp.zeros(shape, F32)
    for t, (first, last) in enumerate(tiers):
        ends = first if first is last else jnp.where(iota(shape, 1) < 64, first, last)
        if t:
            ends = pltpu.roll(ends, 32 * t, 1)
        out = jnp.where(group == t, ends, out)
    return jnp.where(lane32(shape) >= 16, out, pltpu.roll(out, 120, 1))


def unpack_edges(packed, tiers):
    ends = jnp.where(lane32(packed.shape) >= 20, packed, pltpu.roll(packed, 8, 1))
    return [pltpu.roll(ends, (-32 * t) % 128, 1) if t else ends for t in range(tiers)]


def squeeze(edges, lane0):
    slot = lane32((8, 128)) // 4
    out = jnp.zeros((8, 128), F32)
    for q in range(4):
        part = edges[8 * q : 8 * q + 8]
        if 4 * q != lane0:
            part = pltpu.roll(part, (4 * q - lane0) % 128, 1)
        out = jnp.where(slot == q, part, out)
    return out


def with_squeezed_sides(mid, from_left, from_right):
    l32 = lane32((8, 128))
    rows = []
    for q in range(4):
        part = mid[8 * q : 8 * q + 8]
        for lane0, side in ((16, from_left), (12, from_right)):
            if 4 * q != lane0:
                side = pltpu.roll(side, (lane0 - 4 * q) % 128, 1)
            part = jnp.where((l32 >= lane0) & (l32 < lane0 + 4), side, part)
        rows.append(part)
    return jnp.concatenate(rows, axis=0)


def with_sides(mid, from_left, from_right):
    l32 = lane32(mid.shape)
    mid = jnp.where((l32 >= 16) & (l32 < 20), pltpu.roll(from_left, 8, 1), mid)
    return jnp.where((l32 >= 12) & (l32 < 16), pltpu.roll(from_right, 120, 1), mid)


def kernel(
    n_row, n_col,
    v_h, a_h, t_h, vi_h, fe_h, in_h,
    x3, tt, ht, tl, hl,
    x, x1, x2, g, j, v, inv, gr, lr, lg, lw, wa, wb, wc, p0, p1, p2,
    expand, x_raw, a_raw, vi_raw, fe_raw, in_raw, t_raw,
    qx, qx1, qx2, qx3, qg, qj, qv, qi, qgr, qlr, qlg, qlw, qa, qb, qc, q0, q1, q2,
    ra_s, ra_r, rc_s, rc_r, rb_s, rb_r, cm_s, cm_r, cr_r,
    load, r2_s, r2_r, c2_s, c2_r, k2_s, k2_r, ts, tu, hs, hu, pick, pick_ends,
    in_sem, send_sem, recv_sem, send2_sem, recv2_sem,
):
    row = lax.axis_index("row")
    col = lax.axis_index("col")

    def there(dr, dc):
        ok = None
        for cond in (
            (row > 0) if dr < 0 else (row < n_row - 1) if dr > 0 else None,
            (col > 0) if dc < 0 else (col < n_col - 1) if dc > 0 else None,
        ):
            if cond is not None:
                ok = cond if ok is None else jnp.logical_and(ok, cond)
        return ok

    def device(dr, dc):
        return {"row": row + dr, "col": col + dc}

    barrier = pltpu.get_barrier_semaphore()
    for dr, dc in DIRS:

        @pl.when(there(dr, dc))
        def _(dr=dr, dc=dc):
            pl.semaphore_signal(
                barrier, inc=1, device_id=device(dr, dc), device_id_type=MESH
            )

    copies = {}
    slot = 0

    def fetch(name, src, dst):
        nonlocal slot
        copy = pltpu.make_async_copy(src, dst, in_sem.at[slot])
        slot += 1
        copy.start()
        copies.setdefault(name, []).append(copy)

    fetch("t", t_h, t_raw)
    inputs = ((a_h, a_raw), (v_h, x_raw), (fe_h, fe_raw), (in_h, in_raw), (vi_h, vi_raw))
    for n in ORDER:
        for src, dst in inputs:
            rows = pl.ds(n * GROUP, GROUP)
            fetch(n, src.at[:, rows, :], dst.at[:, rows, :])

    def arrived(*names):
        for name in names:
            for copy in copies[name]:
                copy.wait()

    for ref in (x3, g, wa, wb, wc):
        for start in (0, M0 + ROWS, S0 + 24):
            ref[:, :, pl.ds(start, 8), :] = jnp.zeros((4, 4, 8, 128), F32)
    for ref, tiers in ((j, 4), (v, 3)):
        for start in (0, 16):
            ref[:, :, pl.ds(S0 + start, 8), :] = jnp.zeros((tiers, 4, 8, 128), F32)
    for ref in (qx, qx3, qg, qj, qv, qa, qb, qc):
        for start in (0, Q0 + ROWS):
            ref[pl.ds(start, 16), :] = jnp.zeros((16, 128), F32)
    for ref in (ts, tu):
        for start in (0, 48):
            ref[:, pl.ds(start, 8), :] = jnp.zeros((4, 8, 128), F32)
    for ref in (hs, hu):
        for start in (0, 48):
            ref[pl.ds(start, 8), :] = jnp.zeros((8, 128), F32)
    for s in range(2):
        rb_s[s, pl.ds(16, 8), :] = jnp.zeros((8, 128), F32)
        rc_s[s, pl.ds(80, 8), :] = jnp.zeros((8, 128), F32)
        k2_s[s] = jnp.zeros((8, 128), F32)

        @pl.when(jnp.logical_not(there(*DIRS[s])))
        def _(s=s):
            ra_r[s] = jnp.zeros((8, 2, 8, 128), F32)
            rc_r[s] = jnp.zeros((88, 128), F32)
            rb_r[s] = jnp.zeros((40, 128), F32)
            r2_r[s] = jnp.zeros((16, 128), F32)

        @pl.when(jnp.logical_not(there(*DIRS[2 + s])))
        def _(s=s):
            cm_r[s] = jnp.zeros((72, 128), F32)
            c2_r[s] = jnp.zeros((8, 128), F32)

    for s in range(4):

        @pl.when(jnp.logical_not(there(*DIRS[4 + s])))
        def _(s=s):
            cr_r[s] = jnp.zeros((24, 128), F32)
            k2_r[s] = jnp.zeros((8, 128), F32)

    node, cell = iota((256, 128), 0), iota((256, 128), 1)
    inner = (cell > 0) & (cell < 127)
    for h in range(2):
        own = inner & (node // 4 + 64 * h == cell)
        after = inner & (node // 4 + 64 * h + 1 == cell)
        last = node % 4 == 3
        pick[h, 0] = one_zero(own)
        pick[h, 1] = jnp.where(
            (own | after) & last, 0.5, jnp.where(own, 1.0, 0.0)
        ).astype(BF16)
    start_lane = jnp.where(cell % 32 == 0, cell, cell - 11)
    place = (node - start_lane + 1) % 128 - 1
    edge = (cell % 32 == 0) | (cell % 32 == 31)
    whole = edge & (place >= 0) & (place < 4)
    halved = edge & (node >= 128) & ((place == -1) | (place == 3))
    pick_ends[...] = jnp.where(halved, 0.5, jnp.where(whole, 1.0, 0.0)).astype(BF16)

    arrived("t")
    cells = jnp.exp(-0.25 * t_raw[...]).reshape(128, 128)
    wide = iota((128, 512), 1) // 4 == iota((128, 512), 0)
    fine = dot3(cells, one_zero(wide))
    for b in range(4):
        part = fine[:, 128 * b : 128 * (b + 1)].reshape(4, 32, 128)
        for k in range(4):
            expand[:, b, pl.ds(k, 32, 4), :] = part

    def prepare(off):
        raw, rows = pl.ds(off, 8), pl.ds(M0 + off, 8)
        for t in range(4):
            for b in range(4):
                lanes = slice(128 * b, 128 * (b + 1))
                adm, old = a_raw[t, raw, lanes], x_raw[t, raw, lanes]
                gm = adm * lax.rsqrt(adm) * expand[t, b, raw, :]
                g[t, b, rows, :] = gm
                x[t, b, rows, :] = old
                wa[t, b, rows, :] = gm * old
                j[t, b, rows, :] = fe_raw[t, raw, lanes].astype(F32) * in_raw[t, raw, lanes]
                if t < 3:
                    v[t, b, rows, :] = vi_raw[t, raw, lanes].astype(F32)

    def remote(src, dst, send, recv, dr, dc):
        return pltpu.make_async_remote_copy(
            src_ref=src,
            dst_ref=dst,
            send_sem=send,
            recv_sem=recv,
            device_id=device(dr, dc),
            device_id_type=MESH,
        )

    nodes = ((x, 4), (g, 4), (j, 4), (v, 3))
    strips = (qx, qg, qj, qv)
    three_deep = [
        (3 * (16 * k + 4 * t + b), ref, t, b)
        for k, (ref, tiers) in enumerate(((j, 4), (v, 3)))
        for t in range(tiers)
        for b in range(4)
    ]

    row_exchange, first_exchange = [], []
    for s in range(2):
        row_exchange.append((DIRS[s], ra_s.at[s], ra_r.at[1 - s], s, 1 - s))
        row_exchange.append((DIRS[s], rc_s.at[s], rc_r.at[1 - s], 10 + s, 11 - s))
        first_exchange.append((DIRS[s], rb_s.at[s], rb_r.at[1 - s], 2 + s, 3 - s))
    for s in range(4):
        first_exchange.append(
            (DIRS[4 + s], rb_s.at[s // 2, pl.ds(0, 24)], cr_r.at[3 - s], 6 + s, 9 - s)
        )
    for s in range(2):
        first_exchange.append((DIRS[2 + s], cm_s.at[s], cm_r.at[1 - s], 4 + s, 5 - s))
    second_exchange = []
    for s in range(2):
        second_exchange.append((DIRS[s], r2_s.at[s], r2_r.at[1 - s], s, 1 - s))
        second_exchange.append((DIRS[2 + s], c2_s.at[s], c2_r.at[1 - s], 2 + s, 3 - s))
    for s in range(4):
        second_exchange.append(
            (DIRS[4 + s], k2_s.at[s // 2], k2_r.at[3 - s], 4 + s, 7 - s)
        )

    def start(exchange, sends, recvs):
        for (dr, dc), src, dst, a, b in exchange:

            @pl.when(there(dr, dc))
            def _(dr=dr, dc=dc, src=src, dst=dst, a=a, b=b):
                remote(src, dst, sends.at[a], recvs.at[b], dr, dc).start()

    def wait_recv(exchange, sends, recvs):
        for (dr, dc), src, dst, a, b in exchange:

            @pl.when(there(-dr, -dc))
            def _(dr=dr, dc=dc, src=src, dst=dst, a=a, b=b):
                remote(src, dst, sends.at[a], recvs.at[b], -dr, -dc).wait_recv()

    def wait_send(exchange, sends, recvs):
        for (dr, dc), src, dst, a, b in exchange:

            @pl.when(there(dr, dc))
            def _(dr=dr, dc=dc, src=src, dst=dst, a=a, b=b):
                remote(src, dst, sends.at[a], recvs.at[b], dr, dc).wait_send()

    def ready(n):
        arrived(n)
        for off in range(n * GROUP, (n + 1) * GROUP, 8):
            prepare(off)

    def pack(n):
        tile = pl.ds(M0 + n * GROUP, GROUP)
        for (ref, tiers), packed in zip(nodes, strips):
            packed[pl.ds(Q0 + n * GROUP, GROUP), :] = pack_edges(
                [(ref[t, 0, tile, :], ref[t, 3, tile, :]) for t in range(tiers)]
            )

    for n in ORDER[:2]:
        ready(n)
    for s, first in ((0, 0), (1, ROWS - 4)):
        for k, ref in enumerate((x, g)):
            for h in range(2):
                ra_s[s, pl.ds(4 * k, 4), :, pl.ds(4 * h, 4), :] = ref[
                    :, pl.ds(2 * h, 2), pl.ds(M0 + first, 4), :
                ]
        first = (0, ROWS - 3)[s]
        for at, ref, t, b in three_deep:
            rc_s[s, pl.ds(at, 3), :] = ref[t, b, pl.ds(M0 + first, 3), :]

    neighbours = 0
    for dr, dc in DIRS:
        neighbours = neighbours + there(dr, dc).astype(jnp.int32)
    pl.semaphore_wait(barrier, neighbours)
    start(row_exchange, send_sem, recv_sem)

    for n in ORDER[:2]:
        pack(n)
    for n in ORDER[2:]:
        ready(n)
        pack(n)
    tile = pl.ds(M0, ROWS)

    t_edges = pack_edges([(t_raw[t], t_raw[t]) for t in range(4)])
    for s, first in ((0, 0), (1, ROWS - 4)):
        for k, packed in enumerate(strips):
            rb_s[s, pl.ds(4 * k, 4), :] = packed[pl.ds(Q0 + first, 4), :]
        cell = 0 if s == 0 else 28
        rb_s[s, pl.ds(16, 4), :] = t_edges[cell : cell + 4]
        for t in range(4):
            rb_s[s, pl.ds(24 + 4 * t, 4), :] = t_raw[t, pl.ds(cell, 4), :]
    group = lane32((64, 128)) // 4
    for s, lane0 in ((0, 20), (1, 8)):
        mixed = jnp.zeros((64, 128), F32)
        for k, packed in enumerate(strips):
            for h in range(2):
                slot32 = h * 16 + k * 4
                part = packed[pl.ds(Q0 + 64 * h, 64), :]
                if slot32 != lane0:
                    part = pltpu.roll(part, (slot32 - lane0) % 128, 1)
                mixed = jnp.where(group == slot32 // 4, part, mixed)
        cm_s[s, pl.ds(0, 64), :] = mixed
        cm_s[s, pl.ds(64, 8), :] = squeeze(t_edges, lane0)
    start(first_exchange, send_sem, recv_sem)

    for ref, _ in nodes:
        ref[:, :, pl.ds(S0 + 4, 8), :] = ref[:, :, pl.ds(M0, 8), :]
        ref[:, :, pl.ds(S0 + 12, 8), :] = ref[:, :, pl.ds(M0 + ROWS - 8, 8), :]

    big = Domain(
        Tile, g, j, v, inv, gr, (lr, lg, lw), (x, x1, x2, x3), (wa, wb, wc), (p0, p1, p2)
    )
    side = Domain(
        Strip, qg, qj, qv, qi, qgr, (qlr, qlg, qlw),
        (qx, qx1, qx2, qx3), (qa, qb, qc), (q0, q1, q2),
    )
    solve(range(4), ROWS // 8, MAIN_UNROLL, (big, M0, 8))

    wait_recv(row_exchange, send_sem, recv_sem)
    wait_recv(first_exchange, send_sem, recv_sem)

    for s, first in ((0, 0), (1, 20)):
        for k, ref in enumerate((x, g)):
            for h in range(2):
                ref[:, pl.ds(2 * h, 2), pl.ds(S0 + first, 4), :] = ra_r[
                    s, pl.ds(4 * k, 4), :, pl.ds(4 * h, 4), :
                ]
        first = (1, 20)[s]
        for at, ref, t, b in three_deep:
            ref[t, b, pl.ds(S0 + first, 3), :] = rc_r[s, pl.ds(at, 3), :]
    strip = pl.ds(S0, 24)
    wa[:, :, strip, :] = g[:, :, strip, :] * x[:, :, strip, :]

    l32 = lane32((64, 128))
    for k, packed in enumerate(strips):
        for s, first in ((0, Q0 - 4), (1, Q0 + ROWS)):
            part = pl.ds(4 * k, 4)
            packed[pl.ds(first, 4), :] = with_sides(
                rb_r[s, part, :], cr_r[2 * s, part, :], cr_r[2 * s + 1, part, :]
            )
        for h in range(2):
            rows = pl.ds(Q0 + 64 * h, 64)
            slot32 = h * 16 + k * 4
            mid = packed[rows, :]
            for s, lane0 in ((0, 16), (1, 12)):
                part = cm_r[s, pl.ds(0, 64), :]
                if slot32 != lane0:
                    part = pltpu.roll(part, (lane0 - slot32) % 128, 1)
                mid = jnp.where((l32 >= lane0) & (l32 < lane0 + 4), part, mid)
            packed[rows, :] = mid
    strip = pl.ds(8, 144)
    qa[strip, :] = qg[strip, :] * qx[strip, :]
    solve(range(4), 3, STRIP_UNROLL, (big, S0, 8), (side, 8, 48))

    for ref, before in ((p0, 0), (p1, 0), (p2, 1)):
        ref[:, :, pl.ds(M0 - before, 4 + before), :] = ref[
            :, :, pl.ds(S0 + 4 - before, 4 + before), :
        ]
        ref[:, :, pl.ds(M0 + ROWS - 4, 4), :] = ref[:, :, pl.ds(S0 + 16, 4), :]

    def cell_rows(parts, first):
        take = lambda ref, k: ref[
            (slice(None),) * (len(ref.shape) - 2) + (pl.ds(first + k, 32, 4), slice(None))
        ]
        total = 0.5 * (take(parts[2], -1) - take(parts[2], 3))
        right = take(parts[1], 0)
        for k in range(4):
            total = total + take(parts[0], k)
            if k:
                right = right + take(parts[1], k)
        return total, right

    sums, rights = cell_rows(big.power, M0)
    edge_sums, edge_rights = cell_rows(side.power, Q0)
    total = jnp.zeros((128, 128), F32)
    for h in range(2):
        for k, values in enumerate((sums, rights)):
            both = jnp.concatenate(
                [values[:, 2 * h].reshape(128, 128), values[:, 2 * h + 1].reshape(128, 128)],
                axis=1,
            )
            total = total + dot3(both, pick[h, k])
    ends = dot3(jnp.concatenate([edge_sums, edge_rights], axis=1), pick_ends[...])
    lane = iota((32, 128), 1)
    for t in range(4):
        mine = pltpu.roll(ends, (-32 * t) % 128, 1) if t else ends
        mine = jnp.where((lane == 0) | (lane == 127), mine, total[32 * t : 32 * (t + 1)])
        load[t] = GAIN * mine

    l_edges = pack_edges([(load[t], load[t]) for t in range(4)])
    for s, (cell, lane0) in enumerate(((0, 20), (28, 8))):
        c2_s[s] = squeeze(l_edges, lane0)
        k2_s[s, pl.ds(0, 4), :] = l_edges[cell : cell + 4]
        for t in range(4):
            r2_s[s, pl.ds(4 * t, 4), :] = load[t, pl.ds(cell, 4), :]
        for t in range(3):
            own, free = (t, 3) if s == 0 else (29 + t, 0)
            r2_s[s, pl.ds(4 * t + free, 1), :] = l_edges[own : own + 1]
    start(second_exchange, send2_sem, recv2_sem)

    x3[:, :, pl.ds(M0, 4), :] = x3[:, :, pl.ds(S0 + 4, 4), :]
    x3[:, :, pl.ds(M0 + ROWS - 4, 4), :] = x3[:, :, pl.ds(S0 + 16, 4), :]
    lane = iota((ROWS, 128), 1)
    for t, ends in enumerate(unpack_edges(qx3[pl.ds(Q0, ROWS), :], 4)):
        x3[t, 0, tile, :] = jnp.where(lane < 4, ends, x3[t, 0, tile, :])
        x3[t, 3, tile, :] = jnp.where(lane >= 124, ends, x3[t, 3, tile, :])

    for t in range(4):
        tt[t, pl.ds(0, 4), :] = rb_r[0, pl.ds(24 + 4 * t, 4), :]
        tt[t, pl.ds(4, 32), :] = t_raw[t]
        tt[t, pl.ds(36, 4), :] = rb_r[1, pl.ds(24 + 4 * t, 4), :]
    cells = pl.ds(64, 8)
    edge = pl.ds(16, 4)
    ht[pl.ds(0, 4), :] = with_sides(rb_r[0, edge, :], cr_r[0, edge, :], cr_r[1, edge, :])
    ht[pl.ds(4, 32), :] = with_squeezed_sides(t_edges, cm_r[0, cells, :], cm_r[1, cells, :])
    ht[pl.ds(36, 4), :] = with_sides(rb_r[1, edge, :], cr_r[2, edge, :], cr_r[3, edge, :])
    heat_of = Heat(n_row, n_col, ts, tu, hs, hu)
    theta, side = tt[...], ht[...]
    tt[...] = theta + DT * heat_of.tile(theta)
    ht[...] = side + DT * heat_of.strip(side)

    wait_recv(second_exchange, send2_sem, recv2_sem)
    for t in range(4):
        tl[t, pl.ds(0, 4), :] = r2_r[0, pl.ds(4 * t, 4), :]
        tl[t, pl.ds(4, 32), :] = load[t]
        tl[t, pl.ds(36, 4), :] = r2_r[1, pl.ds(4 * t, 4), :]
    zero = jnp.zeros((1, 128), F32)
    above = [zero] + [r2_r[0, pl.ds(4 * t, 1), :] for t in range(3)]
    below = [r2_r[1, pl.ds(4 * t + 3, 1), :] for t in range(3)] + [zero]
    for first, corner, rows in ((0, 0, above), (36, 2, below)):
        hl[pl.ds(first, 4), :] = with_sides(
            jnp.concatenate(rows, axis=0),
            k2_r[corner, pl.ds(0, 4), :],
            k2_r[corner + 1, pl.ds(0, 4), :],
        )
    hl[pl.ds(4, 32), :] = with_squeezed_sides(l_edges, c2_r[0], c2_r[1])

    wait_send(row_exchange, send_sem, recv_sem)
    wait_send(first_exchange, send_sem, recv_sem)
    wait_send(second_exchange, send2_sem, recv2_sem)


class Heat:
    def __init__(self, n_row, n_col, ts, tu, hs, hu):
        row, col = lax.axis_index("row"), lax.axis_index("col")
        self.refs = (ts, tu, hs, hu)
        r, l32 = iota((40, 128), 0), lane32((40, 128))
        rows_in = ((r >= 4) | (row > 0)) & ((r < 36) | (row < n_row - 1))
        cols_in = ((l32 < 16) | (l32 >= 20) | (col > 0)) & (
            (l32 < 12) | (l32 >= 16) | (col < n_col - 1)
        )
        tier = ((iota((40, 128), 1) + 20) // 32) % 4
        real = lambda mask: jnp.where(mask, 1.0, 0.0).astype(F32)
        self.row_mask, self.all_mask = real(rows_in), real(rows_in & cols_in)
        self.not_first, self.not_last = real(tier > 0), real(tier < 3)

    @staticmethod
    def flux(theta, s, u, s_ref, u_ref, rows, axis):
        def near(ref, mid):
            around = ref[rows(7)] + ref[rows(9)]
            return around + pltpu.roll(mid, 1, axis) + pltpu.roll(mid, 127, axis)

        s_ref[rows(8)] = s
        u_ref[rows(8)] = u
        return s * (near(u_ref, u) - theta * near(s_ref, s))

    def tile(self, theta):
        s = jnp.exp(-0.15 * theta) * self.row_mask
        rows = lambda k: (slice(None), pl.ds(k, 40), slice(None))
        flux = self.flux(theta, s, s * theta, *self.refs[:2], rows, 2)
        vert = jnp.concatenate(
            [
                theta[1:2] - theta[0:1],
                theta[0:2] + theta[2:4] - 2.0 * theta[1:3],
                theta[2:3] - 2.0 * theta[3:4],
            ],
            axis=0,
        )
        return flux + vert

    def strip(self, theta):
        s = jnp.exp(-0.15 * theta) * self.all_mask
        rows = lambda k: (pl.ds(k, 40), slice(None))
        flux = self.flux(theta, s, s * theta, *self.refs[2:], rows, 1)
        vert = (
            self.not_last * pltpu.roll(theta, 96, 1)
            + self.not_first * pltpu.roll(theta, 32, 1)
            - (1.0 + self.not_first) * theta
        )
        return flux + vert


def finish(
    n_row, n_col, x3, tt, ht, tl, hl, xo_h, to_h, ts, tu, hs, hu, t_out, out_sem
):
    copies = []
    for b in range(4):
        copy = pltpu.make_async_copy(
            x3.at[:, b, pl.ds(M0, ROWS), :], xo_h.at[:, :, pl.ds(128 * b, 128)], out_sem.at[b]
        )
        copy.start()
        copies.append(copy)
    for ref in (ts, tu):
        for start in (0, 48):
            ref[:, pl.ds(start, 8), :] = jnp.zeros((4, 8, 128), F32)
    for ref in (hs, hu):
        for start in (0, 48):
            ref[pl.ds(start, 8), :] = jnp.zeros((8, 128), F32)
    heat_of = Heat(n_row, n_col, ts, tu, hs, hu)
    heat, side_heat = tl[...], hl[...]
    theta, side = tt[...] + DT * heat, ht[...] + DT * side_heat
    for _ in range(HEAT_SWEEPS - 1):
        gain, side_gain = heat_of.tile(theta), heat_of.strip(side)
        theta = theta + DT * (gain + heat)
        side = side + DT * (side_gain + side_heat)
    lane = iota((32, 128), 1)
    for t, ends in enumerate(unpack_edges(side[4:36], 4)):
        t_out[t] = jnp.where((lane < 4) | (lane >= 124), ends, theta[t, 4:36])
    copy = pltpu.make_async_copy(t_out, to_h, out_sem.at[4])
    copy.start()
    copies.append(copy)
    for copy in copies:
        copy.wait()


def vmem(*shape, dtype=F32):
    return pltpu.VMEM(shape, dtype)


def on_device(n_row, n_col, *args):
    node = (4, 4, R_ALL, 128)
    raw = (4, ROWS, 512)
    strip = (Q_ALL, 128)
    heat = [vmem(4, 56, 128), vmem(4, 56, 128), vmem(56, 128), vmem(56, 128)]
    scratch = [
        *[vmem(*node) for _ in range(5)], vmem(3, *node[1:]),
        *[vmem(*node) for _ in range(2)],
        *[vmem(MAIN_UNROLL, 4, 4, 8, 128) for _ in range(3)],
        *[vmem(*node) for _ in range(6)],
        vmem(4, 4, ROWS, 128), vmem(*raw), vmem(*raw), vmem(3, *raw[1:], dtype=jnp.int32),
        vmem(*raw, dtype=jnp.int32), vmem(*raw), vmem(4, 32, 128),
        *[vmem(*strip) for _ in range(9)],
        *[vmem(STRIP_UNROLL, 48, 128) for _ in range(3)],
        *[vmem(*strip) for _ in range(6)],
        vmem(2, 8, 2, 8, 128), vmem(2, 8, 2, 8, 128),
        vmem(2, 88, 128), vmem(2, 88, 128),
        vmem(2, 40, 128), vmem(2, 40, 128),
        vmem(2, 72, 128), vmem(2, 72, 128),
        vmem(4, 24, 128),
        vmem(4, 32, 128),
        vmem(2, 16, 128), vmem(2, 16, 128),
        vmem(2, 8, 128), vmem(2, 8, 128),
        vmem(2, 8, 128), vmem(4, 8, 128),
        *heat,
        vmem(2, 2, 256, 128, dtype=BF16), vmem(256, 128, dtype=BF16),
        pltpu.SemaphoreType.DMA((1 + 5 * GROUPS,)),
        pltpu.SemaphoreType.DMA((12,)),
        pltpu.SemaphoreType.DMA((12,)),
        pltpu.SemaphoreType.DMA((8,)),
        pltpu.SemaphoreType.DMA((8,)),
    ]
    hbm = pl.BlockSpec(memory_space=pltpu.HBM)
    local = pl.BlockSpec(memory_space=pltpu.VMEM)
    mids = pl.pallas_call(
        functools.partial(kernel, n_row, n_col),
        out_shape=tuple(
            pltpu.VMEM(shape, F32)
            for shape in (node, (4, 40, 128), (40, 128), (4, 40, 128), (40, 128))
        ),
        in_specs=[hbm] * 6,
        out_specs=(local,) * 5,
        scratch_shapes=scratch,
        compiler_params=pltpu.CompilerParams(
            collective_id=0,
            has_side_effects=True,
            vmem_limit_bytes=56 * 1024 * 1024,
        ),
    )(*[pltpu.with_memory_space_constraint(arg, pltpu.HBM) for arg in args])
    return pl.pallas_call(
        functools.partial(finish, n_row, n_col),
        out_shape=(
            jax.ShapeDtypeStruct((4, ROWS, 512), F32),
            jax.ShapeDtypeStruct((4, 32, 128), F32),
        ),
        in_specs=[local] * 5,
        out_specs=(hbm, hbm),
        scratch_shapes=[*heat, vmem(4, 32, 128), pltpu.SemaphoreType.DMA((5,))],
        compiler_params=pltpu.CompilerParams(vmem_limit_bytes=4 * 1024 * 1024),
    )(*mids)


def solution(mesh):
    spec = P(None, "row", "col")
    return jax.shard_map(
        functools.partial(on_device, mesh.shape["row"], mesh.shape["col"]),
        mesh=mesh,
        in_specs=(spec,) * 6,
        out_specs=(spec, spec),
        check_vma=False,
    )
```

```python
import functools

import jax
import jax.numpy as jnp
from jax import lax
from jax.experimental import pallas as pl
from jax.experimental.pallas import tpu as pltpu
from jax.sharding import PartitionSpec as P

F32 = jnp.float32
BF16 = jnp.bfloat16
MESH = pl.DeviceIdType.MESH

LEAK = 0.2
HALF = 0.95
SIGMA = 1.0 / HALF
RHO0 = 1.0 / SIGMA
RHO1 = 1.0 / (2.0 * SIGMA - RHO0)
RHO2 = 1.0 / (2.0 * SIGMA - RHO1)
STEP_1 = (RHO1 * RHO0, 2.0 * RHO1 / HALF)
STEP_2 = (RHO2 * RHO1, 2.0 * RHO2 / HALF)
HEAT_SWEEPS = 4
DT = 0.12
GAIN = 0.0625
MAIN_UNROLL = 4
STRIP_UNROLL = 3
GROUPS = ((0, 8), (120, 8), (8, 56), (64, 56))

ROWS = 128
M0 = 8
S0 = 144
R_ALL = 176
Q0 = 16
Q_ALL = 160

DIRS = ((-1, 0), (1, 0), (0, -1), (0, 1), (-1, -1), (-1, 1), (1, -1), (1, 1))


def iota(shape, dim):
    return lax.broadcasted_iota(jnp.int32, shape, dim)


def split3(x):
    high = x.astype(BF16)
    rest = x - high.astype(F32)
    mid = rest.astype(BF16)
    low = (rest - mid.astype(F32)).astype(BF16)
    return jnp.concatenate([high, mid, low], axis=0)


def dot3(x, ones):
    rows = x.shape[0]
    y = jnp.dot(split3(x), ones, preferred_element_type=F32)
    return y[:rows] + y[rows : 2 * rows] + y[2 * rows :]


def one_zero(mask):
    return jnp.where(mask, 1.0, 0.0).astype(BF16)


class Tile:
    tiers = range(4)

    @staticmethod
    def part(ref, t, row, size):
        return ref[t, :, pl.ds(row, size), :]

    @staticmethod
    def put(ref, t, row, size, value):
        ref[t, :, pl.ds(row, size), :] = value

    @staticmethod
    def slot(ref, k, t):
        return ref[k, t]

    @staticmethod
    def put_slot(ref, k, t, value):
        ref[k, t] = value

    @staticmethod
    def left(x):
        lane = iota(x.shape, 2)
        y = pltpu.roll(x, 1, 2)
        return jnp.where(lane == 0, jnp.concatenate([y[3:], y[:3]], axis=0), y)

    @staticmethod
    def right(x):
        lane = iota(x.shape, 2)
        y = pltpu.roll(x, 127, 2)
        return jnp.where(lane == 127, jnp.concatenate([y[1:], y[:1]], axis=0), y)

    @staticmethod
    def vertical(read, v, x, t):
        if t == 0:
            return read(v, 0) * read(x, 1)
        if t == 3:
            return read(v, 2) * read(x, 2)
        return read(v, t) * read(x, t + 1) + read(v, t - 1) * read(x, t - 1)

    @staticmethod
    def via_sum(read, v, t):
        if t == 0:
            return read(v, 0)
        if t == 3:
            return read(v, 2)
        return read(v, t) + read(v, t - 1)

    @staticmethod
    def drops(read, v, x, t):
        total = None
        for low in (t - 1, t):
            if 0 <= low < 3:
                e = read(x, low) - read(x, low + 1)
                e = read(v, low) * (e * e)
                total = e if total is None else total + e
        return total


class Strip:
    tiers = (0,)

    @staticmethod
    def part(ref, t, row, size):
        return ref[pl.ds(row, size), :]

    @staticmethod
    def put(ref, t, row, size, value):
        ref[pl.ds(row, size), :] = value

    @staticmethod
    def slot(ref, k, t):
        return ref[k]

    @staticmethod
    def put_slot(ref, k, t, value):
        ref[k] = value

    @staticmethod
    def left(x):
        return pltpu.roll(x, 1, 1)

    @staticmethod
    def right(x):
        return pltpu.roll(x, 127, 1)

    @staticmethod
    def vertical(read, v, x, t):
        vm, xm = read(v, t), read(x, t)
        return vm * pltpu.roll(xm, 96, 1) + pltpu.roll(vm * xm, 32, 1)

    @staticmethod
    def via_sum(read, v, t):
        vm = read(v, t)
        return vm + pltpu.roll(vm, 32, 1)

    @staticmethod
    def drops(read, v, x, t):
        xm = read(x, t)
        e = xm - pltpu.roll(xm, 96, 1)
        e = read(v, t) * (e * e)
        return e + pltpu.roll(e, 32, 1)


class Domain:
    def __init__(self, kind, g, j, v, inv, gr, slots, x, w, power):
        self.kind, self.g, self.j, self.v, self.inv = kind, g, j, v, inv
        self.lr, self.lg, self.lw = slots
        self.gr, self.x, self.w, self.power = gr, x, w, power

    def lateral(self, p, row, size, slot):
        kind = self.kind
        for t in kind.tiers:
            if p == 3:
                x = kind.part(self.x[3], t, row, size)
                kind.put_slot(self.lw, slot, t, kind.right(x))
                continue
            w = kind.part(self.w[p], t, row, size)
            kind.put_slot(self.lw, slot, t, kind.left(w) + kind.right(w))
            if p == 0:
                g = kind.part(self.g, t, row, size)
                right = kind.right(g)
                kind.put_slot(self.lr, slot, t, right)
                kind.put_slot(self.lg, slot, t, kind.left(g) + right)

    def sweep(self, p, row, size, slot):
        kind, g, v = self.kind, self.g, self.v
        x, w = self.x[min(p, 3)], self.w
        for t in kind.tiers:
            read = lambda ref, t=t, k=0: kind.part(ref, t, row + k, size)
            put = lambda ref, value, t=t: kind.put(ref, t, row, size, value)
            gm, xm = read(g, t), read(x, t)
            if p == 3:
                right = xm - kind.slot(self.lw, slot, t)
                put(self.power[1], gm * (read(self.gr, t) * (right * right)))
                down = xm - read(x, t, 1)
                e = gm * (read(g, t, 1) * (down * down))
                put(self.power[2], e)
                node = (LEAK * xm) * xm + 0.5 * kind.drops(read, v, x, t)
                put(self.power[0], node + e)
                continue
            near = read(w[p], t, -1) + read(w[p], t, 1) + kind.slot(self.lw, slot, t)
            near = read(self.j, t) + gm * near + kind.vertical(read, v, x, t)
            if p == 0:
                near_g = read(g, t, -1) + read(g, t, 1) + kind.slot(self.lg, slot, t)
                inv = 1.0 / ((LEAK + gm * near_g) + kind.via_sum(read, v, t))
                new = inv * near
                put(self.inv, inv)
                put(self.gr, kind.slot(self.lr, slot, t))
            else:
                a, b = STEP_1 if p == 1 else STEP_2
                new = (1.0 + a - b) * xm - a * read(self.x[p - 1], t)
                new = new + b * (read(self.inv, t) * near)
            put(self.x[p + 1], new)
            if p < 2:
                put(w[p + 1], gm * new)


def solve(passes, steps, unroll, *parts):
    for p in passes:
        for domain, row, size in parts:
            domain.lateral(p, row, size, 0)

        def one(n, carry):
            for k in range(unroll):
                for domain, row, size in parts:
                    now = row + k * size
                    if steps > unroll:
                        now = now + pl.multiple_of(n * (unroll * size), unroll * size)
                    domain.sweep(p, now, size, k)
                    if steps > unroll or k + 1 < unroll:
                        domain.lateral(p, now + size, size, (k + 1) % unroll)
            return carry

        if steps > unroll:
            lax.fori_loop(0, steps // unroll, one, 0)
        else:
            one(0, 0)


def lane32(shape):
    return (iota(shape, 1) + 20) % 32


def pack_edges(tiers):
    shape = tiers[0][0].shape
    group = ((iota(shape, 1) + 12) // 32) % 4
    out = jnp.zeros(shape, F32)
    for t, (first, last) in enumerate(tiers):
        ends = first if first is last else jnp.where(iota(shape, 1) < 64, first, last)
        if t:
            ends = pltpu.roll(ends, 32 * t, 1)
        out = jnp.where(group == t, ends, out)
    return jnp.where(lane32(shape) >= 16, out, pltpu.roll(out, 120, 1))


def unpack_edges(packed, tiers):
    ends = jnp.where(lane32(packed.shape) >= 20, packed, pltpu.roll(packed, 8, 1))
    return [pltpu.roll(ends, (-32 * t) % 128, 1) if t else ends for t in range(tiers)]


def squeeze(edges, lane0):
    slot = lane32((8, 128)) // 4
    out = jnp.zeros((8, 128), F32)
    for q in range(4):
        part = edges[8 * q : 8 * q + 8]
        if 4 * q != lane0:
            part = pltpu.roll(part, (4 * q - lane0) % 128, 1)
        out = jnp.where(slot == q, part, out)
    return out


def with_squeezed_sides(mid, from_left, from_right):
    l32 = lane32((8, 128))
    rows = []
    for q in range(4):
        part = mid[8 * q : 8 * q + 8]
        for lane0, side in ((16, from_left), (12, from_right)):
            if 4 * q != lane0:
                side = pltpu.roll(side, (lane0 - 4 * q) % 128, 1)
            part = jnp.where((l32 >= lane0) & (l32 < lane0 + 4), side, part)
        rows.append(part)
    return jnp.concatenate(rows, axis=0)


def with_sides(mid, from_left, from_right):
    l32 = lane32(mid.shape)
    mid = jnp.where((l32 >= 16) & (l32 < 20), pltpu.roll(from_left, 8, 1), mid)
    return jnp.where((l32 >= 12) & (l32 < 16), pltpu.roll(from_right, 120, 1), mid)


def kernel(
    n_row, n_col,
    v_h, a_h, t_h, vi_h, fe_h, in_h,
    x3, tt, ht, tl, hl,
    x, x1, x2, g, j, v, inv, gr, lr, lg, lw, wa, wb, wc, p0, p1, p2,
    expand, x_raw, a_raw, vi_raw, fe_raw, in_raw, t_raw,
    qx, qx1, qx2, qx3, qg, qj, qv, qi, qgr, qlr, qlg, qlw, qa, qb, qc, q0, q1, q2,
    ra_s, ra_r, rc_s, rc_r, rb_s, rb_r, cm_s, cm_r, cr_r,
    load, r2_s, r2_r, c2_s, c2_r, k2_s, k2_r, ts, tu, hs, hu, pick, pick_ends,
    in_sem, send_sem, recv_sem, send2_sem, recv2_sem,
):
    row = lax.axis_index("row")
    col = lax.axis_index("col")

    def there(dr, dc):
        ok = None
        for cond in (
            (row > 0) if dr < 0 else (row < n_row - 1) if dr > 0 else None,
            (col > 0) if dc < 0 else (col < n_col - 1) if dc > 0 else None,
        ):
            if cond is not None:
                ok = cond if ok is None else jnp.logical_and(ok, cond)
        return ok

    def device(dr, dc):
        return {"row": row + dr, "col": col + dc}

    barrier = pltpu.get_barrier_semaphore()
    for dr, dc in DIRS:

        @pl.when(there(dr, dc))
        def _(dr=dr, dc=dc):
            pl.semaphore_signal(
                barrier, inc=1, device_id=device(dr, dc), device_id_type=MESH
            )

    copies = {}
    slot = 0

    def fetch(name, src, dst):
        nonlocal slot
        copy = pltpu.make_async_copy(src, dst, in_sem.at[slot])
        slot += 1
        copy.start()
        copies.setdefault(name, []).append(copy)

    fetch("t", t_h, t_raw)
    inputs = ((a_h, a_raw), (v_h, x_raw), (fe_h, fe_raw), (in_h, in_raw), (vi_h, vi_raw))
    for first, size in GROUPS:
        for src, dst in inputs:
            rows = pl.ds(first, size)
            fetch(first, src.at[:, rows, :], dst.at[:, rows, :])

    def arrived(*names):
        for name in names:
            for copy in copies[name]:
                copy.wait()

    for ref in (x3, g, wa, wb, wc):
        for start in (0, M0 + ROWS, S0 + 24):
            ref[:, :, pl.ds(start, 8), :] = jnp.zeros((4, 4, 8, 128), F32)
    for ref, tiers in ((j, 4), (v, 3)):
        for start in (0, 16):
            ref[:, :, pl.ds(S0 + start, 8), :] = jnp.zeros((tiers, 4, 8, 128), F32)
    for ref in (qx, qx3, qg, qj, qv, qa, qb, qc):
        for start in (0, Q0 + ROWS):
            ref[pl.ds(start, 16), :] = jnp.zeros((16, 128), F32)
    for ref in (ts, tu):
        for start in (0, 48):
            ref[:, pl.ds(start, 8), :] = jnp.zeros((4, 8, 128), F32)
    for ref in (hs, hu):
        for start in (0, 48):
            ref[pl.ds(start, 8), :] = jnp.zeros((8, 128), F32)
    for s in range(2):
        rb_s[s, pl.ds(16, 8), :] = jnp.zeros((8, 128), F32)
        rc_s[s, pl.ds(80, 8), :] = jnp.zeros((8, 128), F32)
        k2_s[s] = jnp.zeros((8, 128), F32)

        @pl.when(jnp.logical_not(there(*DIRS[s])))
        def _(s=s):
            ra_r[s] = jnp.zeros((8, 2, 8, 128), F32)
            rc_r[s] = jnp.zeros((88, 128), F32)
            rb_r[s] = jnp.zeros((40, 128), F32)
            r2_r[s] = jnp.zeros((16, 128), F32)

        @pl.when(jnp.logical_not(there(*DIRS[2 + s])))
        def _(s=s):
            cm_r[s] = jnp.zeros((72, 128), F32)
            c2_r[s] = jnp.zeros((8, 128), F32)

    for s in range(4):

        @pl.when(jnp.logical_not(there(*DIRS[4 + s])))
        def _(s=s):
            cr_r[s] = jnp.zeros((24, 128), F32)
            k2_r[s] = jnp.zeros((8, 128), F32)

    node, cell = iota((256, 128), 0), iota((256, 128), 1)
    inner = (cell > 0) & (cell < 127)
    for h in range(2):
        own = inner & (node // 4 + 64 * h == cell)
        after = inner & (node // 4 + 64 * h + 1 == cell)
        last = node % 4 == 3
        pick[h, 0] = one_zero(own)
        pick[h, 1] = jnp.where(
            (own | after) & last, 0.5, jnp.where(own, 1.0, 0.0)
        ).astype(BF16)
    start_lane = jnp.where(cell % 32 == 0, cell, cell - 11)
    place = (node - start_lane + 1) % 128 - 1
    edge = (cell % 32 == 0) | (cell % 32 == 31)
    whole = edge & (place >= 0) & (place < 4)
    halved = edge & (node >= 128) & ((place == -1) | (place == 3))
    pick_ends[...] = jnp.where(halved, 0.5, jnp.where(whole, 1.0, 0.0)).astype(BF16)

    arrived("t")
    cells = jnp.exp(-0.25 * t_raw[...]).reshape(128, 128)
    wide = iota((128, 512), 1) // 4 == iota((128, 512), 0)
    fine = dot3(cells, one_zero(wide))
    for b in range(4):
        part = fine[:, 128 * b : 128 * (b + 1)].reshape(4, 32, 128)
        for k in range(4):
            expand[:, b, pl.ds(k, 32, 4), :] = part

    def prepare(off):
        raw, rows = pl.ds(off, 8), pl.ds(M0 + off, 8)
        for t in range(4):
            for b in range(4):
                lanes = slice(128 * b, 128 * (b + 1))
                adm, old = a_raw[t, raw, lanes], x_raw[t, raw, lanes]
                gm = adm * lax.rsqrt(adm) * expand[t, b, raw, :]
                g[t, b, rows, :] = gm
                x[t, b, rows, :] = old
                wa[t, b, rows, :] = gm * old
                j[t, b, rows, :] = fe_raw[t, raw, lanes].astype(F32) * in_raw[t, raw, lanes]
                if t < 3:
                    v[t, b, rows, :] = vi_raw[t, raw, lanes].astype(F32)

    def remote(src, dst, send, recv, dr, dc):
        return pltpu.make_async_remote_copy(
            src_ref=src,
            dst_ref=dst,
            send_sem=send,
            recv_sem=recv,
            device_id=device(dr, dc),
            device_id_type=MESH,
        )

    nodes = ((x, 4), (g, 4), (j, 4), (v, 3))
    strips = (qx, qg, qj, qv)
    three_deep = [
        (3 * (16 * k + 4 * t + b), ref, t, b)
        for k, (ref, tiers) in enumerate(((j, 4), (v, 3)))
        for t in range(tiers)
        for b in range(4)
    ]

    row_exchange, first_exchange = [], []
    for s in range(2):
        row_exchange.append((DIRS[s], ra_s.at[s], ra_r.at[1 - s], s, 1 - s))
        row_exchange.append((DIRS[s], rc_s.at[s], rc_r.at[1 - s], 10 + s, 11 - s))
        first_exchange.append((DIRS[s], rb_s.at[s], rb_r.at[1 - s], 2 + s, 3 - s))
    for s in range(4):
        first_exchange.append(
            (DIRS[4 + s], rb_s.at[s // 2, pl.ds(0, 24)], cr_r.at[3 - s], 6 + s, 9 - s)
        )
    for s in range(2):
        first_exchange.append((DIRS[2 + s], cm_s.at[s], cm_r.at[1 - s], 4 + s, 5 - s))
    second_exchange = []
    for s in range(2):
        second_exchange.append((DIRS[s], r2_s.at[s], r2_r.at[1 - s], s, 1 - s))
        second_exchange.append((DIRS[2 + s], c2_s.at[s], c2_r.at[1 - s], 2 + s, 3 - s))
    for s in range(4):
        second_exchange.append(
            (DIRS[4 + s], k2_s.at[s // 2], k2_r.at[3 - s], 4 + s, 7 - s)
        )

    def start(exchange, sends, recvs):
        for (dr, dc), src, dst, a, b in exchange:

            @pl.when(there(dr, dc))
            def _(dr=dr, dc=dc, src=src, dst=dst, a=a, b=b):
                remote(src, dst, sends.at[a], recvs.at[b], dr, dc).start()

    def wait_recv(exchange, sends, recvs):
        for (dr, dc), src, dst, a, b in exchange:

            @pl.when(there(-dr, -dc))
            def _(dr=dr, dc=dc, src=src, dst=dst, a=a, b=b):
                remote(src, dst, sends.at[a], recvs.at[b], -dr, -dc).wait_recv()

    def wait_send(exchange, sends, recvs):
        for (dr, dc), src, dst, a, b in exchange:

            @pl.when(there(dr, dc))
            def _(dr=dr, dc=dc, src=src, dst=dst, a=a, b=b):
                remote(src, dst, sends.at[a], recvs.at[b], dr, dc).wait_send()

    def ready(first, size):
        arrived(first)
        for off in range(first, first + size, 8):
            prepare(off)

    def pack(first, size):
        tile = pl.ds(M0 + first, size)
        for (ref, tiers), packed in zip(nodes, strips):
            packed[pl.ds(Q0 + first, size), :] = pack_edges(
                [(ref[t, 0, tile, :], ref[t, 3, tile, :]) for t in range(tiers)]
            )

    for group in GROUPS[:2]:
        ready(*group)
    for s, first in ((0, 0), (1, ROWS - 4)):
        for k, ref in enumerate((x, g)):
            for h in range(2):
                ra_s[s, pl.ds(4 * k, 4), :, pl.ds(4 * h, 4), :] = ref[
                    :, pl.ds(2 * h, 2), pl.ds(M0 + first, 4), :
                ]
        first = (0, ROWS - 3)[s]
        for at, ref, t, b in three_deep:
            rc_s[s, pl.ds(at, 3), :] = ref[t, b, pl.ds(M0 + first, 3), :]

    neighbours = 0
    for dr, dc in DIRS:
        neighbours = neighbours + there(dr, dc).astype(jnp.int32)
    pl.semaphore_wait(barrier, neighbours)
    start(row_exchange, send_sem, recv_sem)

    for group in GROUPS[:2]:
        pack(*group)
    for group in GROUPS[2:]:
        ready(*group)
        pack(*group)
    tile = pl.ds(M0, ROWS)

    t_edges = pack_edges([(t_raw[t], t_raw[t]) for t in range(4)])
    for s, first in ((0, 0), (1, ROWS - 4)):
        for k, packed in enumerate(strips):
            rb_s[s, pl.ds(4 * k, 4), :] = packed[pl.ds(Q0 + first, 4), :]
        cell = 0 if s == 0 else 28
        rb_s[s, pl.ds(16, 4), :] = t_edges[cell : cell + 4]
        for t in range(4):
            rb_s[s, pl.ds(24 + 4 * t, 4), :] = t_raw[t, pl.ds(cell, 4), :]
    group = lane32((64, 128)) // 4
    for s, lane0 in ((0, 20), (1, 8)):
        mixed = jnp.zeros((64, 128), F32)
        for k, packed in enumerate(strips):
            for h in range(2):
                slot32 = h * 16 + k * 4
                part = packed[pl.ds(Q0 + 64 * h, 64), :]
                if slot32 != lane0:
                    part = pltpu.roll(part, (slot32 - lane0) % 128, 1)
                mixed = jnp.where(group == slot32 // 4, part, mixed)
        cm_s[s, pl.ds(0, 64), :] = mixed
        cm_s[s, pl.ds(64, 8), :] = squeeze(t_edges, lane0)
    start(first_exchange, send_sem, recv_sem)

    for ref, _ in nodes:
        ref[:, :, pl.ds(S0 + 4, 8), :] = ref[:, :, pl.ds(M0, 8), :]
        ref[:, :, pl.ds(S0 + 12, 8), :] = ref[:, :, pl.ds(M0 + ROWS - 8, 8), :]

    big = Domain(
        Tile, g, j, v, inv, gr, (lr, lg, lw), (x, x1, x2, x3), (wa, wb, wc), (p0, p1, p2)
    )
    side = Domain(
        Strip, qg, qj, qv, qi, qgr, (qlr, qlg, qlw),
        (qx, qx1, qx2, qx3), (qa, qb, qc), (q0, q1, q2),
    )
    solve(range(4), ROWS // 8, MAIN_UNROLL, (big, M0, 8))

    def cell_rows(parts, first, cells):
        take = lambda ref, k: ref[
            (slice(None),) * (len(ref.shape) - 2)
            + (pl.ds(first + k, cells, 4), slice(None))
        ]
        total = 0.5 * (take(parts[2], -1) - take(parts[2], 3))
        right = take(parts[1], 0)
        for k in range(4):
            total = total + take(parts[0], k)
            if k:
                right = right + take(parts[1], k)
        return total, right

    def tile_cells(first, cells):
        total = jnp.zeros((4 * cells, 128), F32)
        for k, values in enumerate(cell_rows(big.power, first, cells)):
            blocks = [values[:, b].reshape(4 * cells, 128) for b in range(4)]
            for h in range(2):
                both = jnp.concatenate(blocks[2 * h : 2 * h + 2], axis=1)
                total = total + dot3(both, pick[h, k])
        return GAIN * total

    inner_cells = tile_cells(M0, 32)
    for t in range(4):
        load[t] = inner_cells[32 * t : 32 * (t + 1)]

    wait_recv(row_exchange, send_sem, recv_sem)
    wait_recv(first_exchange, send_sem, recv_sem)

    for s, first in ((0, 0), (1, 20)):
        for k, ref in enumerate((x, g)):
            for h in range(2):
                ref[:, pl.ds(2 * h, 2), pl.ds(S0 + first, 4), :] = ra_r[
                    s, pl.ds(4 * k, 4), :, pl.ds(4 * h, 4), :
                ]
        first = (1, 20)[s]
        for at, ref, t, b in three_deep:
            ref[t, b, pl.ds(S0 + first, 3), :] = rc_r[s, pl.ds(at, 3), :]
    strip = pl.ds(S0, 24)
    wa[:, :, strip, :] = g[:, :, strip, :] * x[:, :, strip, :]

    l32 = lane32((64, 128))
    for k, packed in enumerate(strips):
        for s, first in ((0, Q0 - 4), (1, Q0 + ROWS)):
            part = pl.ds(4 * k, 4)
            packed[pl.ds(first, 4), :] = with_sides(
                rb_r[s, part, :], cr_r[2 * s, part, :], cr_r[2 * s + 1, part, :]
            )
        for h in range(2):
            rows = pl.ds(Q0 + 64 * h, 64)
            slot32 = h * 16 + k * 4
            mid = packed[rows, :]
            for s, lane0 in ((0, 16), (1, 12)):
                part = cm_r[s, pl.ds(0, 64), :]
                if slot32 != lane0:
                    part = pltpu.roll(part, (lane0 - slot32) % 128, 1)
                mid = jnp.where((l32 >= lane0) & (l32 < lane0 + 4), part, mid)
            packed[rows, :] = mid
    strip = pl.ds(8, 144)
    qa[strip, :] = qg[strip, :] * qx[strip, :]
    solve(range(4), 3, STRIP_UNROLL, (big, S0, 8), (side, 8, 48))

    for t, (first, last) in enumerate(
        (rows[8 * t : 8 * t + 1], rows[8 * t + 3 : 8 * t + 4])
        for rows in [tile_cells(S0 + 4, 8)]
        for t in range(4)
    ):
        load[t, pl.ds(0, 1), :] = first
        load[t, pl.ds(31, 1), :] = last
    values = cell_rows(side.power, Q0, 32)
    ends = GAIN * dot3(jnp.concatenate(values, axis=1), pick_ends[...])
    lane = iota((32, 128), 1)
    for t in range(4):
        mine = pltpu.roll(ends, (-32 * t) % 128, 1) if t else ends
        load[t] = jnp.where((lane == 0) | (lane == 127), mine, load[t])

    l_edges = pack_edges([(load[t], load[t]) for t in range(4)])
    for s, (cell, lane0) in enumerate(((0, 20), (28, 8))):
        c2_s[s] = squeeze(l_edges, lane0)
        k2_s[s, pl.ds(0, 4), :] = l_edges[cell : cell + 4]
        for t in range(4):
            r2_s[s, pl.ds(4 * t, 4), :] = load[t, pl.ds(cell, 4), :]
        for t in range(3):
            own, free = (t, 3) if s == 0 else (29 + t, 0)
            r2_s[s, pl.ds(4 * t + free, 1), :] = l_edges[own : own + 1]
    start(second_exchange, send2_sem, recv2_sem)

    x3[:, :, pl.ds(M0, 4), :] = x3[:, :, pl.ds(S0 + 4, 4), :]
    x3[:, :, pl.ds(M0 + ROWS - 4, 4), :] = x3[:, :, pl.ds(S0 + 16, 4), :]
    lane = iota((ROWS, 128), 1)
    for t, ends in enumerate(unpack_edges(qx3[pl.ds(Q0, ROWS), :], 4)):
        x3[t, 0, tile, :] = jnp.where(lane < 4, ends, x3[t, 0, tile, :])
        x3[t, 3, tile, :] = jnp.where(lane >= 124, ends, x3[t, 3, tile, :])

    for t in range(4):
        tt[t, pl.ds(0, 4), :] = rb_r[0, pl.ds(24 + 4 * t, 4), :]
        tt[t, pl.ds(4, 32), :] = t_raw[t]
        tt[t, pl.ds(36, 4), :] = rb_r[1, pl.ds(24 + 4 * t, 4), :]
    cells = pl.ds(64, 8)
    edge = pl.ds(16, 4)
    ht[pl.ds(0, 4), :] = with_sides(rb_r[0, edge, :], cr_r[0, edge, :], cr_r[1, edge, :])
    ht[pl.ds(4, 32), :] = with_squeezed_sides(t_edges, cm_r[0, cells, :], cm_r[1, cells, :])
    ht[pl.ds(36, 4), :] = with_sides(rb_r[1, edge, :], cr_r[2, edge, :], cr_r[3, edge, :])
    heat_of = Heat(n_row, n_col, ts, tu, hs, hu)
    theta, side = tt[...], ht[...]
    tt[...] = theta + DT * heat_of.tile(theta)
    ht[...] = side + DT * heat_of.strip(side)

    wait_recv(second_exchange, send2_sem, recv2_sem)
    for t in range(4):
        tl[t, pl.ds(0, 4), :] = r2_r[0, pl.ds(4 * t, 4), :]
        tl[t, pl.ds(4, 32), :] = load[t]
        tl[t, pl.ds(36, 4), :] = r2_r[1, pl.ds(4 * t, 4), :]
    zero = jnp.zeros((1, 128), F32)
    above = [zero] + [r2_r[0, pl.ds(4 * t, 1), :] for t in range(3)]
    below = [r2_r[1, pl.ds(4 * t + 3, 1), :] for t in range(3)] + [zero]
    for first, corner, rows in ((0, 0, above), (36, 2, below)):
        hl[pl.ds(first, 4), :] = with_sides(
            jnp.concatenate(rows, axis=0),
            k2_r[corner, pl.ds(0, 4), :],
            k2_r[corner + 1, pl.ds(0, 4), :],
        )
    hl[pl.ds(4, 32), :] = with_squeezed_sides(l_edges, c2_r[0], c2_r[1])

    wait_send(row_exchange, send_sem, recv_sem)
    wait_send(first_exchange, send_sem, recv_sem)
    wait_send(second_exchange, send2_sem, recv2_sem)


class Heat:
    def __init__(self, n_row, n_col, ts, tu, hs, hu):
        row, col = lax.axis_index("row"), lax.axis_index("col")
        self.refs = (ts, tu, hs, hu)
        r, l32 = iota((40, 128), 0), lane32((40, 128))
        rows_in = ((r >= 4) | (row > 0)) & ((r < 36) | (row < n_row - 1))
        cols_in = ((l32 < 16) | (l32 >= 20) | (col > 0)) & (
            (l32 < 12) | (l32 >= 16) | (col < n_col - 1)
        )
        tier = ((iota((40, 128), 1) + 20) // 32) % 4
        real = lambda mask: jnp.where(mask, 1.0, 0.0).astype(F32)
        self.row_mask, self.all_mask = real(rows_in), real(rows_in & cols_in)
        self.not_first, self.not_last = real(tier > 0), real(tier < 3)

    @staticmethod
    def flux(theta, s, u, s_ref, u_ref, rows, axis):
        s_ref[rows(8)] = s
        u_ref[rows(8)] = u
        near = lambda ref: ref[rows(7)] + ref[rows(9)]
        right = lambda x: pltpu.roll(x, 127, axis)
        e = s * right(s) * (right(theta) - theta)
        return s * (near(u_ref) - theta * near(s_ref)) + (e - pltpu.roll(e, 1, axis))

    def tile(self, theta):
        s = jnp.exp(-0.15 * theta) * self.row_mask
        rows = lambda k: (slice(None), pl.ds(k, 40), slice(None))
        flux = self.flux(theta, s, s * theta, *self.refs[:2], rows, 2)
        vert = jnp.concatenate(
            [
                theta[1:2] - theta[0:1],
                theta[0:2] + theta[2:4] - 2.0 * theta[1:3],
                theta[2:3] - 2.0 * theta[3:4],
            ],
            axis=0,
        )
        return flux + vert

    def strip(self, theta):
        s = jnp.exp(-0.15 * theta) * self.all_mask
        rows = lambda k: (pl.ds(k, 40), slice(None))
        flux = self.flux(theta, s, s * theta, *self.refs[2:], rows, 1)
        vert = (
            self.not_last * pltpu.roll(theta, 96, 1)
            + self.not_first * pltpu.roll(theta, 32, 1)
            - (1.0 + self.not_first) * theta
        )
        return flux + vert


def finish(
    n_row, n_col, x3, tt, ht, tl, hl, xo_h, to_h, ts, tu, hs, hu, t_out, out_sem
):
    copies = []
    for b in range(4):
        copy = pltpu.make_async_copy(
            x3.at[:, b, pl.ds(M0, ROWS), :], xo_h.at[:, :, pl.ds(128 * b, 128)], out_sem.at[b]
        )
        copy.start()
        copies.append(copy)
    for ref in (ts, tu):
        for start in (0, 48):
            ref[:, pl.ds(start, 8), :] = jnp.zeros((4, 8, 128), F32)
    for ref in (hs, hu):
        for start in (0, 48):
            ref[pl.ds(start, 8), :] = jnp.zeros((8, 128), F32)
    heat_of = Heat(n_row, n_col, ts, tu, hs, hu)
    heat, side_heat = tl[...], hl[...]
    theta, side = tt[...] + DT * heat, ht[...] + DT * side_heat
    for _ in range(HEAT_SWEEPS - 1):
        gain, side_gain = heat_of.tile(theta), heat_of.strip(side)
        theta = theta + DT * (gain + heat)
        side = side + DT * (side_gain + side_heat)
    lane = iota((32, 128), 1)
    for t, ends in enumerate(unpack_edges(side[4:36], 4)):
        t_out[t] = jnp.where((lane < 4) | (lane >= 124), ends, theta[t, 4:36])
    copy = pltpu.make_async_copy(t_out, to_h, out_sem.at[4])
    copy.start()
    copies.append(copy)
    for copy in copies:
        copy.wait()


def vmem(*shape, dtype=F32):
    return pltpu.VMEM(shape, dtype)


def on_device(n_row, n_col, *args):
    node = (4, 4, R_ALL, 128)
    raw = (4, ROWS, 512)
    strip = (Q_ALL, 128)
    heat = [vmem(4, 56, 128), vmem(4, 56, 128), vmem(56, 128), vmem(56, 128)]
    scratch = [
        *[vmem(*node) for _ in range(5)], vmem(3, *node[1:]),
        *[vmem(*node) for _ in range(2)],
        *[vmem(MAIN_UNROLL, 4, 4, 8, 128) for _ in range(3)],
        *[vmem(*node) for _ in range(3)],
        *[vmem(4, 4, R_ALL + 8, 128) for _ in range(3)],
        vmem(4, 4, ROWS, 128), vmem(*raw), vmem(*raw), vmem(3, *raw[1:], dtype=jnp.int32),
        vmem(*raw, dtype=jnp.int32), vmem(*raw), vmem(4, 32, 128),
        *[vmem(*strip) for _ in range(9)],
        *[vmem(STRIP_UNROLL, 48, 128) for _ in range(3)],
        *[vmem(*strip) for _ in range(6)],
        vmem(2, 8, 2, 8, 128), vmem(2, 8, 2, 8, 128),
        vmem(2, 88, 128), vmem(2, 88, 128),
        vmem(2, 40, 128), vmem(2, 40, 128),
        vmem(2, 72, 128), vmem(2, 72, 128),
        vmem(4, 24, 128),
        vmem(4, 32, 128),
        vmem(2, 16, 128), vmem(2, 16, 128),
        vmem(2, 8, 128), vmem(2, 8, 128),
        vmem(2, 8, 128), vmem(4, 8, 128),
        *heat,
        vmem(2, 2, 256, 128, dtype=BF16), vmem(256, 128, dtype=BF16),
        pltpu.SemaphoreType.DMA((1 + 5 * len(GROUPS),)),
        pltpu.SemaphoreType.DMA((12,)),
        pltpu.SemaphoreType.DMA((12,)),
        pltpu.SemaphoreType.DMA((8,)),
        pltpu.SemaphoreType.DMA((8,)),
    ]
    hbm = pl.BlockSpec(memory_space=pltpu.HBM)
    local = pl.BlockSpec(memory_space=pltpu.VMEM)
    mids = pl.pallas_call(
        functools.partial(kernel, n_row, n_col),
        out_shape=tuple(
            pltpu.VMEM(shape, F32)
            for shape in (node, (4, 40, 128), (40, 128), (4, 40, 128), (40, 128))
        ),
        in_specs=[hbm] * 6,
        out_specs=(local,) * 5,
        scratch_shapes=scratch,
        compiler_params=pltpu.CompilerParams(
            collective_id=0,
            has_side_effects=True,
            vmem_limit_bytes=56 * 1024 * 1024,
        ),
    )(*[pltpu.with_memory_space_constraint(arg, pltpu.HBM) for arg in args])
    return pl.pallas_call(
        functools.partial(finish, n_row, n_col),
        out_shape=(
            jax.ShapeDtypeStruct((4, ROWS, 512), F32),
            jax.ShapeDtypeStruct((4, 32, 128), F32),
        ),
        in_specs=[local] * 5,
        out_specs=(hbm, hbm),
        scratch_shapes=[*heat, vmem(4, 32, 128), pltpu.SemaphoreType.DMA((5,))],
        compiler_params=pltpu.CompilerParams(vmem_limit_bytes=4 * 1024 * 1024),
    )(*mids)


def solution(mesh):
    spec = P(None, "row", "col")
    return jax.shard_map(
        functools.partial(on_device, mesh.shape["row"], mesh.shape["col"]),
        mesh=mesh,
        in_specs=(spec,) * 6,
        out_specs=(spec, spec),
        check_vma=False,
    )
```

```python
import functools

import jax
import jax.numpy as jnp
from jax import lax
from jax.experimental import pallas as pl
from jax.experimental.pallas import tpu as pltpu
from jax.sharding import PartitionSpec as P

F32 = jnp.float32
BF16 = jnp.bfloat16
MESH = pl.DeviceIdType.MESH

LEAK = 0.2
HALF = 0.95
SIGMA = 1.0 / HALF
RHO0 = 1.0 / SIGMA
RHO1 = 1.0 / (2.0 * SIGMA - RHO0)
RHO2 = 1.0 / (2.0 * SIGMA - RHO1)
STEP_1 = (RHO1 * RHO0, 2.0 * RHO1 / HALF)
STEP_2 = (RHO2 * RHO1, 2.0 * RHO2 / HALF)
HEAT_SWEEPS = 4
DT = 0.12
GAIN = 0.0625
MAIN_UNROLL = 4
STRIP_UNROLL = 3
GROUPS = ((0, 8), (120, 8), (8, 56), (64, 56))

ROWS = 128
M0 = 8
S0 = 144
R_ALL = 176
Q0 = 16
Q_ALL = 160

DIRS = ((-1, 0), (1, 0), (0, -1), (0, 1), (-1, -1), (-1, 1), (1, -1), (1, 1))


def iota(shape, dim):
    return lax.broadcasted_iota(jnp.int32, shape, dim)


def split3(x):
    high = x.astype(BF16)
    rest = x - high.astype(F32)
    mid = rest.astype(BF16)
    low = (rest - mid.astype(F32)).astype(BF16)
    return jnp.concatenate([high, mid, low], axis=0)


def dot3(x, ones):
    rows = x.shape[0]
    y = jnp.dot(split3(x), ones, preferred_element_type=F32)
    return y[:rows] + y[rows : 2 * rows] + y[2 * rows :]


def one_zero(mask):
    return jnp.where(mask, 1.0, 0.0).astype(BF16)


class Tile:
    tiers = range(4)

    @staticmethod
    def part(ref, t, row, size):
        return ref[t, :, pl.ds(row, size), :]

    @staticmethod
    def put(ref, t, row, size, value):
        ref[t, :, pl.ds(row, size), :] = value

    @staticmethod
    def slot(ref, k, t):
        return ref[k, t]

    @staticmethod
    def put_slot(ref, k, t, value):
        ref[k, t] = value

    @staticmethod
    def left(x):
        lane = iota(x.shape, 2)
        y = pltpu.roll(x, 1, 2)
        return jnp.where(lane == 0, jnp.concatenate([y[3:], y[:3]], axis=0), y)

    @staticmethod
    def right(x):
        lane = iota(x.shape, 2)
        y = pltpu.roll(x, 127, 2)
        return jnp.where(lane == 127, jnp.concatenate([y[1:], y[:1]], axis=0), y)

    @staticmethod
    def vertical(read, v, x, t):
        if t == 0:
            return read(v, 0) * read(x, 1)
        if t == 3:
            return read(v, 2) * read(x, 2)
        return read(v, t) * read(x, t + 1) + read(v, t - 1) * read(x, t - 1)

    @staticmethod
    def via_sum(read, v, t):
        if t == 0:
            return read(v, 0)
        if t == 3:
            return read(v, 2)
        return read(v, t) + read(v, t - 1)

    @staticmethod
    def drops(read, v, x, t):
        total = None
        for low in (t - 1, t):
            if 0 <= low < 3:
                e = read(x, low) - read(x, low + 1)
                e = read(v, low) * (e * e)
                total = e if total is None else total + e
        return total


class Strip:
    tiers = (0,)

    @staticmethod
    def part(ref, t, row, size):
        return ref[pl.ds(row, size), :]

    @staticmethod
    def put(ref, t, row, size, value):
        ref[pl.ds(row, size), :] = value

    @staticmethod
    def slot(ref, k, t):
        return ref[k]

    @staticmethod
    def put_slot(ref, k, t, value):
        ref[k] = value

    @staticmethod
    def left(x):
        return pltpu.roll(x, 1, 1)

    @staticmethod
    def right(x):
        return pltpu.roll(x, 127, 1)

    @staticmethod
    def vertical(read, v, x, t):
        vm, xm = read(v, t), read(x, t)
        return vm * pltpu.roll(xm, 96, 1) + pltpu.roll(vm * xm, 32, 1)

    @staticmethod
    def via_sum(read, v, t):
        vm = read(v, t)
        return vm + pltpu.roll(vm, 32, 1)

    @staticmethod
    def drops(read, v, x, t):
        xm = read(x, t)
        e = xm - pltpu.roll(xm, 96, 1)
        e = read(v, t) * (e * e)
        return e + pltpu.roll(e, 32, 1)


class Domain:
    def __init__(self, kind, g, j, v, inv, gr, slots, x, w, power):
        self.kind, self.g, self.j, self.v, self.inv = kind, g, j, v, inv
        self.lr, self.lg, self.lw = slots
        self.gr, self.x, self.w, self.power = gr, x, w, power

    def lateral(self, p, row, size, slot):
        kind = self.kind
        for t in kind.tiers:
            if p == 3:
                x = kind.part(self.x[3], t, row, size)
                kind.put_slot(self.lw, slot, t, kind.right(x))
                continue
            w = kind.part(self.w[p], t, row, size)
            kind.put_slot(self.lw, slot, t, kind.left(w) + kind.right(w))
            if p == 0:
                g = kind.part(self.g, t, row, size)
                right = kind.right(g)
                kind.put_slot(self.lr, slot, t, right)
                kind.put_slot(self.lg, slot, t, kind.left(g) + right)

    def sweep(self, p, row, size, slot):
        kind, g, v = self.kind, self.g, self.v
        x, w = self.x[min(p, 3)], self.w
        for t in kind.tiers:
            read = lambda ref, t=t, k=0: kind.part(ref, t, row + k, size)
            put = lambda ref, value, t=t: kind.put(ref, t, row, size, value)
            gm, xm = read(g, t), read(x, t)
            if p == 3:
                right = xm - kind.slot(self.lw, slot, t)
                put(self.power[1], gm * (read(self.gr, t) * (right * right)))
                down = xm - read(x, t, 1)
                e = gm * (read(g, t, 1) * (down * down))
                put(self.power[2], e)
                node = (LEAK * xm) * xm + 0.5 * kind.drops(read, v, x, t)
                put(self.power[0], node + e)
                continue
            near = read(w[p], t, -1) + read(w[p], t, 1) + kind.slot(self.lw, slot, t)
            near = read(self.j, t) + gm * near + kind.vertical(read, v, x, t)
            if p == 0:
                near_g = read(g, t, -1) + read(g, t, 1) + kind.slot(self.lg, slot, t)
                inv = 1.0 / ((LEAK + gm * near_g) + kind.via_sum(read, v, t))
                new = inv * near
                put(self.inv, inv)
                put(self.gr, kind.slot(self.lr, slot, t))
            else:
                a, b = STEP_1 if p == 1 else STEP_2
                new = (1.0 + a - b) * xm - a * read(self.x[p - 1], t)
                new = new + b * (read(self.inv, t) * near)
            put(self.x[p + 1], new)
            if p < 2:
                put(w[p + 1], gm * new)


def solve(passes, steps, unroll, *parts):
    for p in passes:
        for domain, row, size in parts:
            domain.lateral(p, row, size, 0)

        def one(n, carry):
            for k in range(unroll):
                for domain, row, size in parts:
                    now = row + k * size
                    if steps > unroll:
                        now = now + pl.multiple_of(n * (unroll * size), unroll * size)
                    domain.sweep(p, now, size, k)
                    if steps > unroll or k + 1 < unroll:
                        domain.lateral(p, now + size, size, (k + 1) % unroll)
            return carry

        if steps > unroll:
            lax.fori_loop(0, steps // unroll, one, 0)
        else:
            one(0, 0)


def lane32(shape):
    return (iota(shape, 1) + 20) % 32


def pack_edges(tiers):
    shape = tiers[0][0].shape
    group = ((iota(shape, 1) + 12) // 32) % 4
    out = jnp.zeros(shape, F32)
    for t, (first, last) in enumerate(tiers):
        ends = first if first is last else jnp.where(iota(shape, 1) < 64, first, last)
        if t:
            ends = pltpu.roll(ends, 32 * t, 1)
        out = jnp.where(group == t, ends, out)
    return jnp.where(lane32(shape) >= 16, out, pltpu.roll(out, 120, 1))


def unpack_edges(packed, tiers):
    ends = jnp.where(lane32(packed.shape) >= 20, packed, pltpu.roll(packed, 8, 1))
    return [pltpu.roll(ends, (-32 * t) % 128, 1) if t else ends for t in range(tiers)]


def squeeze(edges, lane0):
    slot = lane32((8, 128)) // 4
    out = jnp.zeros((8, 128), F32)
    for q in range(4):
        part = edges[8 * q : 8 * q + 8]
        if 4 * q != lane0:
            part = pltpu.roll(part, (4 * q - lane0) % 128, 1)
        out = jnp.where(slot == q, part, out)
    return out


def with_squeezed_sides(mid, from_left, from_right):
    l32 = lane32((8, 128))
    rows = []
    for q in range(4):
        part = mid[8 * q : 8 * q + 8]
        for lane0, side in ((16, from_left), (12, from_right)):
            if 4 * q != lane0:
                side = pltpu.roll(side, (lane0 - 4 * q) % 128, 1)
            part = jnp.where((l32 >= lane0) & (l32 < lane0 + 4), side, part)
        rows.append(part)
    return jnp.concatenate(rows, axis=0)


def with_sides(mid, from_left, from_right):
    l32 = lane32(mid.shape)
    mid = jnp.where((l32 >= 16) & (l32 < 20), pltpu.roll(from_left, 8, 1), mid)
    return jnp.where((l32 >= 12) & (l32 < 16), pltpu.roll(from_right, 120, 1), mid)


def kernel(
    n_row, n_col,
    v_h, a_h, t_h, vi_h, fe_h, in_h,
    x3, tt, ht, tl, hl,
    x, x1, x2, g, j, v, inv, gr, lr, lg, lw, wa, wb, wc, p0, p1, p2,
    expand, x_raw, a_raw, vi_raw, fe_raw, in_raw, t_raw,
    qx, qx1, qx2, qx3, qg, qj, qv, qi, qgr, qlr, qlg, qlw, qa, qb, qc, q0, q1, q2,
    ra_s, ra_r, rc_s, rc_r, rb_s, rb_r, cm_s, cm_r, cr_r,
    load, r2_s, r2_r, c2_s, c2_r, k2_s, k2_r, ts, tu, hs, hu, pick, pick_ends,
    in_sem, send_sem, recv_sem, send2_sem, recv2_sem,
):
    row = lax.axis_index("row")
    col = lax.axis_index("col")

    def there(dr, dc):
        ok = None
        for cond in (
            (row > 0) if dr < 0 else (row < n_row - 1) if dr > 0 else None,
            (col > 0) if dc < 0 else (col < n_col - 1) if dc > 0 else None,
        ):
            if cond is not None:
                ok = cond if ok is None else jnp.logical_and(ok, cond)
        return ok

    def device(dr, dc):
        return {"row": row + dr, "col": col + dc}

    barrier = pltpu.get_barrier_semaphore()
    for dr, dc in DIRS:

        @pl.when(there(dr, dc))
        def _(dr=dr, dc=dc):
            pl.semaphore_signal(
                barrier, inc=1, device_id=device(dr, dc), device_id_type=MESH
            )

    copies = {}
    slot = 0

    def fetch(name, src, dst):
        nonlocal slot
        copy = pltpu.make_async_copy(src, dst, in_sem.at[slot])
        slot += 1
        copy.start()
        copies.setdefault(name, []).append(copy)

    fetch("t", t_h, t_raw)
    inputs = ((a_h, a_raw), (v_h, x_raw), (fe_h, fe_raw), (in_h, in_raw), (vi_h, vi_raw))
    for first, size in GROUPS:
        for src, dst in inputs:
            rows = pl.ds(first, size)
            fetch(first, src.at[:, rows, :], dst.at[:, rows, :])

    def arrived(*names):
        for name in names:
            for copy in copies[name]:
                copy.wait()

    for ref in (x3, g, wa, wb, wc):
        for start in (0, M0 + ROWS, S0 + 24):
            ref[:, :, pl.ds(start, 8), :] = jnp.zeros((4, 4, 8, 128), F32)
    for ref, tiers in ((j, 4), (v, 3)):
        for start in (0, 16):
            ref[:, :, pl.ds(S0 + start, 8), :] = jnp.zeros((tiers, 4, 8, 128), F32)
    for ref in (qx, qx3, qg, qj, qv, qa, qb, qc):
        for start in (0, Q0 + ROWS):
            ref[pl.ds(start, 16), :] = jnp.zeros((16, 128), F32)
    for ref in (ts, tu):
        for start in (0, 48):
            ref[:, pl.ds(start, 8), :] = jnp.zeros((4, 8, 128), F32)
    for ref in (hs, hu):
        for start in (0, 48):
            ref[pl.ds(start, 8), :] = jnp.zeros((8, 128), F32)
    for s in range(2):
        rb_s[s, pl.ds(16, 8), :] = jnp.zeros((8, 128), F32)
        rc_s[s, pl.ds(80, 8), :] = jnp.zeros((8, 128), F32)
        k2_s[s] = jnp.zeros((8, 128), F32)

        @pl.when(jnp.logical_not(there(*DIRS[s])))
        def _(s=s):
            ra_r[s] = jnp.zeros((8, 2, 8, 128), F32)
            rc_r[s] = jnp.zeros((88, 128), F32)
            rb_r[s] = jnp.zeros((40, 128), F32)
            r2_r[s] = jnp.zeros((16, 128), F32)

        @pl.when(jnp.logical_not(there(*DIRS[2 + s])))
        def _(s=s):
            cm_r[s] = jnp.zeros((72, 128), F32)
            c2_r[s] = jnp.zeros((8, 128), F32)

    for s in range(4):

        @pl.when(jnp.logical_not(there(*DIRS[4 + s])))
        def _(s=s):
            cr_r[s] = jnp.zeros((24, 128), F32)
            k2_r[s] = jnp.zeros((8, 128), F32)

    node, cell = iota((256, 128), 0), iota((256, 128), 1)
    inner = (cell > 0) & (cell < 127)
    for h in range(2):
        own = inner & (node // 4 + 64 * h == cell)
        after = inner & (node // 4 + 64 * h + 1 == cell)
        last = node % 4 == 3
        pick[h, 0] = one_zero(own)
        pick[h, 1] = jnp.where(
            (own | after) & last, 0.5, jnp.where(own, 1.0, 0.0)
        ).astype(BF16)
    start_lane = jnp.where(cell % 32 == 0, cell, cell - 11)
    place = (node - start_lane + 1) % 128 - 1
    edge = (cell % 32 == 0) | (cell % 32 == 31)
    whole = edge & (place >= 0) & (place < 4)
    halved = edge & (node >= 128) & ((place == -1) | (place == 3))
    pick_ends[...] = jnp.where(halved, 0.5, jnp.where(whole, 1.0, 0.0)).astype(BF16)

    arrived("t")
    cells = jnp.exp(-0.25 * t_raw[...]).reshape(128, 128)
    wide = iota((128, 512), 1) // 4 == iota((128, 512), 0)
    fine = dot3(cells, one_zero(wide))
    for b in range(4):
        part = fine[:, 128 * b : 128 * (b + 1)].reshape(4, 32, 128)
        for k in range(4):
            expand[:, b, pl.ds(k, 32, 4), :] = part

    def prepare(off):
        raw, rows = pl.ds(off, 8), pl.ds(M0 + off, 8)
        for t in range(4):
            for b in range(4):
                lanes = slice(128 * b, 128 * (b + 1))
                adm, old = a_raw[t, raw, lanes], x_raw[t, raw, lanes]
                gm = adm * lax.rsqrt(adm) * expand[t, b, raw, :]
                g[t, b, rows, :] = gm
                x[t, b, rows, :] = old
                wa[t, b, rows, :] = gm * old
                j[t, b, rows, :] = fe_raw[t, raw, lanes].astype(F32) * in_raw[t, raw, lanes]
                if t < 3:
                    v[t, b, rows, :] = vi_raw[t, raw, lanes].astype(F32)

    def remote(src, dst, send, recv, dr, dc):
        return pltpu.make_async_remote_copy(
            src_ref=src,
            dst_ref=dst,
            send_sem=send,
            recv_sem=recv,
            device_id=device(dr, dc),
            device_id_type=MESH,
        )

    nodes = ((x, 4), (g, 4), (j, 4), (v, 3))
    strips = (qx, qg, qj, qv)
    three_deep = [
        (3 * (16 * k + 4 * t + b), ref, t, b)
        for k, (ref, tiers) in enumerate(((j, 4), (v, 3)))
        for t in range(tiers)
        for b in range(4)
    ]

    row_exchange, col_exchange = [], []
    for s in range(2):
        row_exchange.append((DIRS[s], ra_s.at[s], ra_r.at[1 - s], s, 1 - s))
        row_exchange.append((DIRS[s], rc_s.at[s], rc_r.at[1 - s], 10 + s, 11 - s))
        row_exchange.append((DIRS[s], rb_s.at[s], rb_r.at[1 - s], 2 + s, 3 - s))
    for s in range(4):
        row_exchange.append(
            (DIRS[4 + s], rb_s.at[s // 2, pl.ds(0, 24)], cr_r.at[3 - s], 6 + s, 9 - s)
        )
    for s in range(2):
        col_exchange.append((DIRS[2 + s], cm_s.at[s], cm_r.at[1 - s], 4 + s, 5 - s))
    second_exchange = []
    for s in range(2):
        second_exchange.append((DIRS[s], r2_s.at[s], r2_r.at[1 - s], s, 1 - s))
        second_exchange.append((DIRS[2 + s], c2_s.at[s], c2_r.at[1 - s], 2 + s, 3 - s))
    for s in range(4):
        second_exchange.append(
            (DIRS[4 + s], k2_s.at[s // 2], k2_r.at[3 - s], 4 + s, 7 - s)
        )

    def start(exchange, sends, recvs):
        for (dr, dc), src, dst, a, b in exchange:

            @pl.when(there(dr, dc))
            def _(dr=dr, dc=dc, src=src, dst=dst, a=a, b=b):
                remote(src, dst, sends.at[a], recvs.at[b], dr, dc).start()

    def wait_recv(exchange, sends, recvs):
        for (dr, dc), src, dst, a, b in exchange:

            @pl.when(there(-dr, -dc))
            def _(dr=dr, dc=dc, src=src, dst=dst, a=a, b=b):
                remote(src, dst, sends.at[a], recvs.at[b], -dr, -dc).wait_recv()

    def wait_send(exchange, sends, recvs):
        for (dr, dc), src, dst, a, b in exchange:

            @pl.when(there(dr, dc))
            def _(dr=dr, dc=dc, src=src, dst=dst, a=a, b=b):
                remote(src, dst, sends.at[a], recvs.at[b], dr, dc).wait_send()

    def ready(first, size):
        arrived(first)
        for off in range(first, first + size, 8):
            prepare(off)

    def pack(first, size):
        tile = pl.ds(M0 + first, size)
        for (ref, tiers), packed in zip(nodes, strips):
            packed[pl.ds(Q0 + first, size), :] = pack_edges(
                [(ref[t, 0, tile, :], ref[t, 3, tile, :]) for t in range(tiers)]
            )

    for group in GROUPS[:2]:
        ready(*group)
    for s, first in ((0, 0), (1, ROWS - 4)):
        for k, ref in enumerate((x, g)):
            for h in range(2):
                ra_s[s, pl.ds(4 * k, 4), :, pl.ds(4 * h, 4), :] = ref[
                    :, pl.ds(2 * h, 2), pl.ds(M0 + first, 4), :
                ]
        first = (0, ROWS - 3)[s]
        for at, ref, t, b in three_deep:
            rc_s[s, pl.ds(at, 3), :] = ref[t, b, pl.ds(M0 + first, 3), :]

    for group in GROUPS[:2]:
        pack(*group)
    t_edges = pack_edges([(t_raw[t], t_raw[t]) for t in range(4)])
    for s, first in ((0, 0), (1, ROWS - 4)):
        for k, packed in enumerate(strips):
            rb_s[s, pl.ds(4 * k, 4), :] = packed[pl.ds(Q0 + first, 4), :]
        cell = 0 if s == 0 else 28
        rb_s[s, pl.ds(16, 4), :] = t_edges[cell : cell + 4]
        for t in range(4):
            rb_s[s, pl.ds(24 + 4 * t, 4), :] = t_raw[t, pl.ds(cell, 4), :]

    neighbours = 0
    for dr, dc in DIRS:
        neighbours = neighbours + there(dr, dc).astype(jnp.int32)
    pl.semaphore_wait(barrier, neighbours)
    start(row_exchange, send_sem, recv_sem)

    for group in GROUPS[2:]:
        ready(*group)
        pack(*group)
    tile = pl.ds(M0, ROWS)

    group = lane32((64, 128)) // 4
    for s, lane0 in ((0, 20), (1, 8)):
        mixed = jnp.zeros((64, 128), F32)
        for k, packed in enumerate(strips):
            for h in range(2):
                slot32 = h * 16 + k * 4
                part = packed[pl.ds(Q0 + 64 * h, 64), :]
                if slot32 != lane0:
                    part = pltpu.roll(part, (slot32 - lane0) % 128, 1)
                mixed = jnp.where(group == slot32 // 4, part, mixed)
        cm_s[s, pl.ds(0, 64), :] = mixed
        cm_s[s, pl.ds(64, 8), :] = squeeze(t_edges, lane0)
    start(col_exchange, send_sem, recv_sem)

    for ref, _ in nodes:
        ref[:, :, pl.ds(S0 + 4, 8), :] = ref[:, :, pl.ds(M0, 8), :]
        ref[:, :, pl.ds(S0 + 12, 8), :] = ref[:, :, pl.ds(M0 + ROWS - 8, 8), :]

    big = Domain(
        Tile, g, j, v, inv, gr, (lr, lg, lw), (x, x1, x2, x3), (wa, wb, wc), (p0, p1, p2)
    )
    side = Domain(
        Strip, qg, qj, qv, qi, qgr, (qlr, qlg, qlw),
        (qx, qx1, qx2, qx3), (qa, qb, qc), (q0, q1, q2),
    )
    solve(range(4), ROWS // 8, MAIN_UNROLL, (big, M0, 8))

    def cell_rows(parts, first, cells):
        take = lambda ref, k: ref[
            (slice(None),) * (len(ref.shape) - 2)
            + (pl.ds(first + k, cells, 4), slice(None))
        ]
        total = 0.5 * (take(parts[2], -1) - take(parts[2], 3))
        right = take(parts[1], 0)
        for k in range(4):
            total = total + take(parts[0], k)
            if k:
                right = right + take(parts[1], k)
        return total, right

    def tile_cells(first, cells):
        total = jnp.zeros((4 * cells, 128), F32)
        for k, values in enumerate(cell_rows(big.power, first, cells)):
            blocks = [values[:, b].reshape(4 * cells, 128) for b in range(4)]
            for h in range(2):
                both = jnp.concatenate(blocks[2 * h : 2 * h + 2], axis=1)
                total = total + dot3(both, pick[h, k])
        return GAIN * total

    inner_cells = tile_cells(M0, 32)
    for t in range(4):
        load[t] = inner_cells[32 * t : 32 * (t + 1)]

    wait_recv(row_exchange, send_sem, recv_sem)
    wait_recv(col_exchange, send_sem, recv_sem)

    for s, first in ((0, 0), (1, 20)):
        for k, ref in enumerate((x, g)):
            for h in range(2):
                ref[:, pl.ds(2 * h, 2), pl.ds(S0 + first, 4), :] = ra_r[
                    s, pl.ds(4 * k, 4), :, pl.ds(4 * h, 4), :
                ]
        first = (1, 20)[s]
        for at, ref, t, b in three_deep:
            ref[t, b, pl.ds(S0 + first, 3), :] = rc_r[s, pl.ds(at, 3), :]
    strip = pl.ds(S0, 24)
    wa[:, :, strip, :] = g[:, :, strip, :] * x[:, :, strip, :]

    l32 = lane32((64, 128))
    for k, packed in enumerate(strips):
        for s, first in ((0, Q0 - 4), (1, Q0 + ROWS)):
            part = pl.ds(4 * k, 4)
            packed[pl.ds(first, 4), :] = with_sides(
                rb_r[s, part, :], cr_r[2 * s, part, :], cr_r[2 * s + 1, part, :]
            )
        for h in range(2):
            rows = pl.ds(Q0 + 64 * h, 64)
            slot32 = h * 16 + k * 4
            mid = packed[rows, :]
            for s, lane0 in ((0, 16), (1, 12)):
                part = cm_r[s, pl.ds(0, 64), :]
                if slot32 != lane0:
                    part = pltpu.roll(part, (lane0 - slot32) % 128, 1)
                mid = jnp.where((l32 >= lane0) & (l32 < lane0 + 4), part, mid)
            packed[rows, :] = mid
    strip = pl.ds(8, 144)
    qa[strip, :] = qg[strip, :] * qx[strip, :]
    solve(range(4), 3, STRIP_UNROLL, (big, S0, 8), (side, 8, 48))

    for t, (first, last) in enumerate(
        (rows[8 * t : 8 * t + 1], rows[8 * t + 3 : 8 * t + 4])
        for rows in [tile_cells(S0 + 4, 8)]
        for t in range(4)
    ):
        load[t, pl.ds(0, 1), :] = first
        load[t, pl.ds(31, 1), :] = last
    values = cell_rows(side.power, Q0, 32)
    ends = GAIN * dot3(jnp.concatenate(values, axis=1), pick_ends[...])
    lane = iota((32, 128), 1)
    for t in range(4):
        mine = pltpu.roll(ends, (-32 * t) % 128, 1) if t else ends
        load[t] = jnp.where((lane == 0) | (lane == 127), mine, load[t])

    l_edges = pack_edges([(load[t], load[t]) for t in range(4)])
    for s, (cell, lane0) in enumerate(((0, 20), (28, 8))):
        c2_s[s] = squeeze(l_edges, lane0)
        k2_s[s, pl.ds(0, 4), :] = l_edges[cell : cell + 4]
        for t in range(4):
            r2_s[s, pl.ds(4 * t, 4), :] = load[t, pl.ds(cell, 4), :]
        for t in range(3):
            own, free = (t, 3) if s == 0 else (29 + t, 0)
            r2_s[s, pl.ds(4 * t + free, 1), :] = l_edges[own : own + 1]
    start(second_exchange, send2_sem, recv2_sem)

    x3[:, :, pl.ds(M0, 4), :] = x3[:, :, pl.ds(S0 + 4, 4), :]
    x3[:, :, pl.ds(M0 + ROWS - 4, 4), :] = x3[:, :, pl.ds(S0 + 16, 4), :]
    lane = iota((ROWS, 128), 1)
    for t, ends in enumerate(unpack_edges(qx3[pl.ds(Q0, ROWS), :], 4)):
        x3[t, 0, tile, :] = jnp.where(lane < 4, ends, x3[t, 0, tile, :])
        x3[t, 3, tile, :] = jnp.where(lane >= 124, ends, x3[t, 3, tile, :])

    for t in range(4):
        tt[t, pl.ds(0, 4), :] = rb_r[0, pl.ds(24 + 4 * t, 4), :]
        tt[t, pl.ds(4, 32), :] = t_raw[t]
        tt[t, pl.ds(36, 4), :] = rb_r[1, pl.ds(24 + 4 * t, 4), :]
    cells = pl.ds(64, 8)
    edge = pl.ds(16, 4)
    ht[pl.ds(0, 4), :] = with_sides(rb_r[0, edge, :], cr_r[0, edge, :], cr_r[1, edge, :])
    ht[pl.ds(4, 32), :] = with_squeezed_sides(t_edges, cm_r[0, cells, :], cm_r[1, cells, :])
    ht[pl.ds(36, 4), :] = with_sides(rb_r[1, edge, :], cr_r[2, edge, :], cr_r[3, edge, :])
    heat_of = Heat(n_row, n_col, ts, tu, hs, hu)
    theta, side = tt[...], ht[...]
    tt[...] = theta + DT * heat_of.tile(theta)
    ht[...] = side + DT * heat_of.strip(side)

    wait_recv(second_exchange, send2_sem, recv2_sem)
    for t in range(4):
        tl[t, pl.ds(0, 4), :] = r2_r[0, pl.ds(4 * t, 4), :]
        tl[t, pl.ds(4, 32), :] = load[t]
        tl[t, pl.ds(36, 4), :] = r2_r[1, pl.ds(4 * t, 4), :]
    zero = jnp.zeros((1, 128), F32)
    above = [zero] + [r2_r[0, pl.ds(4 * t, 1), :] for t in range(3)]
    below = [r2_r[1, pl.ds(4 * t + 3, 1), :] for t in range(3)] + [zero]
    for first, corner, rows in ((0, 0, above), (36, 2, below)):
        hl[pl.ds(first, 4), :] = with_sides(
            jnp.concatenate(rows, axis=0),
            k2_r[corner, pl.ds(0, 4), :],
            k2_r[corner + 1, pl.ds(0, 4), :],
        )
    hl[pl.ds(4, 32), :] = with_squeezed_sides(l_edges, c2_r[0], c2_r[1])

    wait_send(row_exchange, send_sem, recv_sem)
    wait_send(col_exchange, send_sem, recv_sem)
    wait_send(second_exchange, send2_sem, recv2_sem)


class Heat:
    def __init__(self, n_row, n_col, ts, tu, hs, hu):
        row, col = lax.axis_index("row"), lax.axis_index("col")
        self.refs = (ts, tu, hs, hu)
        r, l32 = iota((40, 128), 0), lane32((40, 128))
        rows_in = ((r >= 4) | (row > 0)) & ((r < 36) | (row < n_row - 1))
        cols_in = ((l32 < 16) | (l32 >= 20) | (col > 0)) & (
            (l32 < 12) | (l32 >= 16) | (col < n_col - 1)
        )
        tier = ((iota((40, 128), 1) + 20) // 32) % 4
        real = lambda mask: jnp.where(mask, 1.0, 0.0).astype(F32)
        self.row_mask, self.all_mask = real(rows_in), real(rows_in & cols_in)
        self.not_first, self.not_last = real(tier > 0), real(tier < 3)

    @staticmethod
    def flux(theta, s, u, s_ref, u_ref, rows, axis):
        s_ref[rows(8)] = s
        u_ref[rows(8)] = u
        near = lambda ref: ref[rows(7)] + ref[rows(9)]
        right = lambda x: pltpu.roll(x, 127, axis)
        e = s * right(s) * (right(theta) - theta)
        return s * (near(u_ref) - theta * near(s_ref)) + (e - pltpu.roll(e, 1, axis))

    def tile(self, theta):
        s = jnp.exp(-0.15 * theta) * self.row_mask
        rows = lambda k: (slice(None), pl.ds(k, 40), slice(None))
        flux = self.flux(theta, s, s * theta, *self.refs[:2], rows, 2)
        vert = jnp.concatenate(
            [
                theta[1:2] - theta[0:1],
                theta[0:2] + theta[2:4] - 2.0 * theta[1:3],
                theta[2:3] - 2.0 * theta[3:4],
            ],
            axis=0,
        )
        return flux + vert

    def strip(self, theta):
        s = jnp.exp(-0.15 * theta) * self.all_mask
        rows = lambda k: (pl.ds(k, 40), slice(None))
        flux = self.flux(theta, s, s * theta, *self.refs[2:], rows, 1)
        vert = (
            self.not_last * pltpu.roll(theta, 96, 1)
            + self.not_first * pltpu.roll(theta, 32, 1)
            - (1.0 + self.not_first) * theta
        )
        return flux + vert


def finish(
    n_row, n_col, x3, tt, ht, tl, hl, xo_h, to_h, ts, tu, hs, hu, t_out, out_sem
):
    copies = []
    for b in range(4):
        copy = pltpu.make_async_copy(
            x3.at[:, b, pl.ds(M0, ROWS), :], xo_h.at[:, :, pl.ds(128 * b, 128)], out_sem.at[b]
        )
        copy.start()
        copies.append(copy)
    for ref in (ts, tu):
        for start in (0, 48):
            ref[:, pl.ds(start, 8), :] = jnp.zeros((4, 8, 128), F32)
    for ref in (hs, hu):
        for start in (0, 48):
            ref[pl.ds(start, 8), :] = jnp.zeros((8, 128), F32)
    heat_of = Heat(n_row, n_col, ts, tu, hs, hu)
    heat, side_heat = tl[...], hl[...]
    theta, side = tt[...] + DT * heat, ht[...] + DT * side_heat
    for _ in range(HEAT_SWEEPS - 1):
        gain, side_gain = heat_of.tile(theta), heat_of.strip(side)
        theta = theta + DT * (gain + heat)
        side = side + DT * (side_gain + side_heat)
    lane = iota((32, 128), 1)
    for t, ends in enumerate(unpack_edges(side[4:36], 4)):
        t_out[t] = jnp.where((lane < 4) | (lane >= 124), ends, theta[t, 4:36])
    copy = pltpu.make_async_copy(t_out, to_h, out_sem.at[4])
    copy.start()
    copies.append(copy)
    for copy in copies:
        copy.wait()


def vmem(*shape, dtype=F32):
    return pltpu.VMEM(shape, dtype)


def on_device(n_row, n_col, *args):
    node = (4, 4, R_ALL, 128)
    raw = (4, ROWS, 512)
    strip = (Q_ALL, 128)
    heat = [vmem(4, 56, 128), vmem(4, 56, 128), vmem(56, 128), vmem(56, 128)]
    scratch = [
        *[vmem(*node) for _ in range(5)], vmem(3, *node[1:]),
        *[vmem(*node) for _ in range(2)],
        *[vmem(MAIN_UNROLL, 4, 4, 8, 128) for _ in range(3)],
        *[vmem(*node) for _ in range(3)],
        *[vmem(4, 4, R_ALL + 8, 128) for _ in range(3)],
        vmem(4, 4, ROWS, 128), vmem(*raw), vmem(*raw), vmem(3, *raw[1:], dtype=jnp.int32),
        vmem(*raw, dtype=jnp.int32), vmem(*raw), vmem(4, 32, 128),
        *[vmem(*strip) for _ in range(9)],
        *[vmem(STRIP_UNROLL, 48, 128) for _ in range(3)],
        *[vmem(*strip) for _ in range(6)],
        vmem(2, 8, 2, 8, 128), vmem(2, 8, 2, 8, 128),
        vmem(2, 88, 128), vmem(2, 88, 128),
        vmem(2, 40, 128), vmem(2, 40, 128),
        vmem(2, 72, 128), vmem(2, 72, 128),
        vmem(4, 24, 128),
        vmem(4, 32, 128),
        vmem(2, 16, 128), vmem(2, 16, 128),
        vmem(2, 8, 128), vmem(2, 8, 128),
        vmem(2, 8, 128), vmem(4, 8, 128),
        *heat,
        vmem(2, 2, 256, 128, dtype=BF16), vmem(256, 128, dtype=BF16),
        pltpu.SemaphoreType.DMA((1 + 5 * len(GROUPS),)),
        pltpu.SemaphoreType.DMA((12,)),
        pltpu.SemaphoreType.DMA((12,)),
        pltpu.SemaphoreType.DMA((8,)),
        pltpu.SemaphoreType.DMA((8,)),
    ]
    hbm = pl.BlockSpec(memory_space=pltpu.HBM)
    local = pl.BlockSpec(memory_space=pltpu.VMEM)
    mids = pl.pallas_call(
        functools.partial(kernel, n_row, n_col),
        out_shape=tuple(
            pltpu.VMEM(shape, F32)
            for shape in (node, (4, 40, 128), (40, 128), (4, 40, 128), (40, 128))
        ),
        in_specs=[hbm] * 6,
        out_specs=(local,) * 5,
        scratch_shapes=scratch,
        compiler_params=pltpu.CompilerParams(
            collective_id=0,
            has_side_effects=True,
            vmem_limit_bytes=56 * 1024 * 1024,
        ),
    )(*[pltpu.with_memory_space_constraint(arg, pltpu.HBM) for arg in args])
    return pl.pallas_call(
        functools.partial(finish, n_row, n_col),
        out_shape=(
            jax.ShapeDtypeStruct((4, ROWS, 512), F32),
            jax.ShapeDtypeStruct((4, 32, 128), F32),
        ),
        in_specs=[local] * 5,
        out_specs=(hbm, hbm),
        scratch_shapes=[*heat, vmem(4, 32, 128), pltpu.SemaphoreType.DMA((5,))],
        compiler_params=pltpu.CompilerParams(vmem_limit_bytes=4 * 1024 * 1024),
    )(*mids)


def solution(mesh):
    spec = P(None, "row", "col")
    return jax.shard_map(
        functools.partial(on_device, mesh.shape["row"], mesh.shape["col"]),
        mesh=mesh,
        in_specs=(spec,) * 6,
        out_specs=(spec, spec),
        check_vma=False,
    )
```
